32 devices in a mesh: seq: 8 (over z, x), fsdp: 4 (over y, core).
Axes of the slice: x: 2, y: 2, z: 4, core: 2. Of those that a mesh axis runs over, the one named last changes fastest.
Arguments:
- layer_input: bfloat16 [4, 1024, 1024], P('fsdp', 'seq'), may hold values from -6 to 6
- doc_lengths: int32 [4, 5], replicated, may hold values from 1 to 512, 1024 in all within a row
- attn_gain: bfloat16 [1024], P(('seq', 'fsdp')), may hold values from 0.5 to 1.5
- qkv_weight: bfloat16 [1024, 3, 1024], P('seq', None, 'fsdp'), may hold values from -2 to 2
- out_weight: bfloat16 [1024, 1024], P('fsdp', 'seq'), may hold values from -0.5 to 0.5
- mlp_gain: bfloat16 [1024], P(('seq', 'fsdp')), may hold values from 0.5 to 1.5
- in_weight: bfloat16 [1024, 2, 2624], P('seq', None, 'fsdp'), may hold values from -0.1875 to 0.1875
- down_weight: bfloat16 [1024, 2624], P('seq', 'fsdp'), may hold values from -0.125 to 0.125
- out_grad: bfloat16 [4, 1024, 1024], P('fsdp', 'seq'), may hold values from -6 to 6
Outputs:
- layer_output: bfloat16 [4, 1024, 1024], P('fsdp', 'seq')
- input_grad: float32 [4, 1024, 1024], P('fsdp', 'seq')
- attn_gain_grad: float32 [1024], P(('seq', 'fsdp'))
- qkv_weight_grad: float32 [1024, 3, 1024], P('seq', None, 'fsdp')
- out_weight_grad: float32 [1024, 1024], P('fsdp', 'seq')
- mlp_gain_grad: float32 [1024], P(('seq', 'fsdp'))
- in_weight_grad: float32 [1024, 2, 2624], P('seq', None, 'fsdp')
- down_weight_grad: float32 [1024, 2624], P('seq', 'fsdp')
The draws below stay inside these ranges and needn't reach their ends.
Inputs may be any that keep to these rules, and one draw needn't show every extreme that they name: Each row of doc_lengths lists the lengths of the documents of one stream in order; they sum to 1024 and the longest is exactly 512.
All inputs are finite; a program needn't handle non-finite values.
Results may differ from the reference program's by a relative error of at most 0.02.
Values may be sent and summed in bfloat16 or wider, within the bound.
A program may use at most 128 MiB of HBM per device.

```python
import math
import jax
import jax.numpy as jnp
import numpy as np
from jax import lax

D = 1024
HEADS = 16
HEAD = 64
FF = 2624
WIN = 64
DOCS = 5
STREAM = 1024
N_FSDP = 4


def draw_qkv_weight(key, part):
    first = jax.random.fold_in(key, 11)
    second = jax.random.fold_in(key, 12)
    base = jax.random.normal(first, (D, 3 * D), jnp.float32) * D ** (-0.5)
    strength = jnp.exp(jax.random.uniform(second, (HEADS,), jnp.float32, math.log(0.5), math.log(2.0)))
    columns = jnp.repeat(strength, HEAD)[None, :]
    whole = jnp.concatenate([base[:, :2 * D] * jnp.concatenate([columns, columns], axis=1), base[:, 2 * D:]], axis=1)
    return jnp.clip(whole, -2.0, 2.0).reshape(D, 3, D).astype(jnp.bfloat16)


def with_spikes(drawn, rng, source, target, shards_of, factor):
    def block_of(axis_at):
        return (jnp.arange(drawn.shape[axis_at]) // (drawn.shape[axis_at] // shards_of)).reshape((-1,) + (1,) * (drawn.ndim - 1 - axis_at))

    near = jax.random.permutation(rng, shards_of)[block_of(target)]
    other_side = (block_of(target) + shards_of // 2) % shards_of
    return jnp.where((block_of(source) == near) | (block_of(source) == other_side), factor * drawn, drawn)


def level_of(key, extent, shards, smallest, high):
    level = 1.0
    for axis_at, parts in shards:
        heights = jax.random.uniform(jax.random.fold_in(jax.random.fold_in(key, 6), axis_at), (parts,), jnp.float32, smallest / len(shards), high / len(shards))
        level = level * jnp.repeat(jnp.exp(heights), extent[axis_at] // parts).reshape((-1,) + (1,) * (len(extent) - 1 - axis_at))
    return level


def length_profile(amount, total, most, skew):
    portions = [(1 << 20) // math.isqrt(grade ** skew) + 1 for grade in range(2, amount + 1)]
    spare, given = total - most - (amount - 1), [1] * (amount - 1)
    while spare > 0:
        movable = [i for i in range(amount - 1) if given[i] < most]
        pool, remaining = sum([portions[i] for i in movable]), spare
        for i in movable:
            extra = min(most - given[i], max(1, remaining * portions[i] // pool), spare)
            given[i] = given[i] + extra
            spare = spare - extra
    return np.array([most] + given)


def ragged_sizes(key, amount, total, bound, lean):
    if amount == 2:
        one = jax.random.randint(key, (), max(1, total - bound), min(bound, total - 1) + 1)
        return jnp.stack([one, total - one])
    tallies = jnp.asarray(length_profile(amount, total, bound, lean), jnp.int32)
    twos = (amount - 1) // 2
    source_of, sink = tallies[1:1 + 2 * twos:2], tallies[2:2 + 2 * twos:2]
    margin = jnp.minimum(source_of - 1, bound - sink)
    moved = jax.random.randint(jax.random.fold_in(key, 1), (twos,), 0, 1 << 20) % (margin + 1)
    tallies = tallies.at[1:1 + 2 * twos:2].set(source_of - moved).at[2:2 + 2 * twos:2].set(sink + moved)
    return tallies[jax.random.permutation(jax.random.fold_in(key, 2), amount)]


def normal_values(rng, extent, scale, most, cuts=(), kind=jnp.bfloat16):
    array = jax.random.normal(rng, extent, jnp.float32) * scale
    if len(cuts) > 0:
        array = level_of(rng, extent, cuts, -0.22, 0.18) * array
    return jnp.clip(array, min=-most, max=most).astype(kind)


def bell_draw_with(stream_key, shape, deviation, limit, cuts, heavy, kind=jnp.bfloat16):
    drawn = deviation * jax.random.normal(stream_key, shape, jnp.float32)
    if cuts:
        drawn = drawn * level_of(stream_key, shape, cuts, -0.22, 0.18)
    return jnp.clip(with_spikes(drawn, jax.random.fold_in(stream_key, 3), *heavy), -limit, limit).astype(kind)


def setup_inputs(seed: int = 0) -> dict:
    streams_of = jax.random.split(jax.random.key(seed), 10)
    return {
        "layer_input": normal_values(streams_of[0], (N_FSDP, STREAM, D), 1.0, 6.0, ((0, 4), (1, 8))),
        "doc_lengths": jax.vmap(lambda own: ragged_sizes(own, DOCS, STREAM, STREAM // 2, 2))(jax.random.split(streams_of[1], N_FSDP)).reshape((N_FSDP, DOCS)).astype(jnp.int32),
        "attn_gain": jnp.clip(1.0 + 0.1 * jax.random.normal(streams_of[2], (D,), jnp.float32), 0.5, 1.5).astype(jnp.bfloat16),
        "qkv_weight": draw_qkv_weight(jax.random.fold_in(streams_of[9], 71), 0),
        "out_weight": normal_values(streams_of[4], (D, D), (D // 8) ** -0.5, 0.5, ((0, 4), (1, 8))),
        "mlp_gain": jnp.clip(1.0 + 0.1 * jax.random.normal(streams_of[5], (D,), jnp.float32), 0.5, 1.5).astype(jnp.bfloat16),
        "in_weight": normal_values(streams_of[6], (D, 2, FF), D ** -0.5, 0.1875, ((0, 8), (2, 4))),
        "down_weight": normal_values(streams_of[7], (D, FF), FF ** -0.5, 0.125, ((0, 8), (1, 4))),
        "out_grad": bell_draw_with(streams_of[8], (N_FSDP, STREAM, D), 1.0, 6.0, ((0, 4), (1, 8)), (1, 2, 8, 2.0)),
    }


EPSILON = 1e-05

def norm_forward(values, gain):
    mean = lax.optimization_barrier(jnp.mean(values, axis=-1, keepdims=True))
    centred = values - mean
    inverse = lax.rsqrt(lax.optimization_barrier(jnp.mean(centred * centred, axis=-1, keepdims=True)) + EPSILON)
    scaled = centred * inverse
    return (scaled, inverse, (scaled * gain.astype(jnp.float32)).astype(jnp.bfloat16))

def norm_backward(grad, scaled, inverse, gain):
    weighted = grad * gain.astype(jnp.float32)
    back = inverse * (weighted - lax.optimization_barrier(jnp.mean(weighted, axis=-1, keepdims=True)) - scaled * lax.optimization_barrier(jnp.mean(weighted * scaled, axis=-1, keepdims=True)))
    return (back, lax.optimization_barrier(jnp.sum(grad * scaled, axis=0)))

def gelu_parts(inner):
    cdf = 0.5 * (1.0 + jax.scipy.special.erf(inner * 0.7071067811865476))
    density = jnp.exp(-0.5 * inner * inner) * 0.3989422804014327
    return (inner * cdf, cdf + inner * density)

def rope_tables(positions, head_size):
    half = head_size // 2
    inv_freq = 10000.0 ** (-(2.0 / head_size) * jnp.arange(half, dtype=jnp.float32))
    angle = positions.astype(jnp.float32)[:, None] * inv_freq[None, :]
    return (jnp.cos(angle)[:, None, :], jnp.sin(angle)[:, None, :])

def rotate(field, cosine, sine):
    half = field.shape[-1] // 2
    first, second = (field[..., :half], field[..., half:])
    return jnp.concatenate([first * cosine - second * sine, second * cosine + first * sine], axis=-1)

def unrotate(grad, cosine, sine):
    half = grad.shape[-1] // 2
    first, second = (grad[..., :half], grad[..., half:])
    return jnp.concatenate([first * cosine + second * sine, second * cosine - first * sine], axis=-1)

def doc_ids(lengths_row, positions):
    starts = jnp.cumsum(lengths_row, dtype=jnp.int32) - lengths_row
    total = jnp.sum(lengths_row, dtype=jnp.int32)
    found = lax.optimization_barrier(jnp.sum((positions[:, None] >= starts[None, :]).astype(jnp.int32), axis=1, dtype=jnp.int32)) - 1
    valid = (positions >= 0) & (positions < total)
    return jnp.where(valid, found, -1).astype(jnp.int32)

def window_mask(ids_query, ids_key, reach):
    block = ids_query.shape[0]
    offset = jnp.arange(block, dtype=jnp.int32)[:, None] + reach - jnp.arange(block + 2 * reach, dtype=jnp.int32)[None, :]
    return (jnp.abs(offset) <= reach) & (ids_query[:, None] == ids_key[None, :])

def attend_forward(query, keys, values, allowed):
    scale = query.shape[-1] ** (-0.5)
    scores = jnp.einsum('nhe,mhe->hnm', query.astype(jnp.float32), keys.astype(jnp.float32)) * scale
    masked = jnp.where(allowed[None], scores, -1e+30)
    top = lax.optimization_barrier(jnp.max(masked, axis=-1, keepdims=True))
    expd = jnp.exp(masked - top)
    total = lax.optimization_barrier(jnp.sum(expd, axis=-1, keepdims=True))
    log_total = (top + jnp.log(total))[..., 0]
    probs = (expd / total).astype(jnp.bfloat16)
    out = jnp.einsum('hnm,mhe->nhe', probs.astype(jnp.float32), values.astype(jnp.float32))
    return (out.astype(jnp.bfloat16), log_total)

def attend_backward(query, keys, values, allowed, log_total, attended, grad_out):
    scale = query.shape[-1] ** (-0.5)
    scores = jnp.einsum('nhe,mhe->hnm', query.astype(jnp.float32), keys.astype(jnp.float32)) * scale
    masked = jnp.where(allowed[None], scores, -1e+30)
    again = jnp.exp(masked - log_total[..., None])
    again_b = again.astype(jnp.bfloat16)
    grad_f = grad_out.astype(jnp.float32)
    grad_values = jnp.einsum('hnm,nhe->mhe', again_b.astype(jnp.float32), grad_f)
    grad_probs = jnp.einsum('nhe,mhe->hnm', grad_f, values.astype(jnp.float32))
    delta = lax.optimization_barrier(jnp.sum(grad_f * attended.astype(jnp.float32), axis=-1)).T
    grad_scores = (again * (grad_probs - delta[..., None]) * scale).astype(jnp.bfloat16).astype(jnp.float32)
    grad_query = jnp.einsum('hnm,mhe->nhe', grad_scores, keys.astype(jnp.float32))
    grad_keys = jnp.einsum('hnm,nhe->mhe', grad_scores, query.astype(jnp.float32))
    return (grad_query, grad_keys, grad_values)

def attention_forward(query, ext_keys, ext_values, ids_query, ids_key, block, reach):
    rows, heads = (query.shape[0], query.shape[1])
    count = rows // block

    def step(carry, index):
        start = index * block
        q_block = lax.dynamic_slice_in_dim(query, start, block, 0)
        k_block = lax.dynamic_slice_in_dim(ext_keys, start, block + 2 * reach, 0)
        v_block = lax.dynamic_slice_in_dim(ext_values, start, block + 2 * reach, 0)
        allowed = window_mask(lax.dynamic_slice_in_dim(ids_query, start, block, 0), lax.dynamic_slice_in_dim(ids_key, start, block + 2 * reach, 0), reach)
        return (carry, attend_forward(q_block, k_block, v_block, allowed))
    _, (outs, totals) = lax.scan(step, jnp.zeros((), jnp.float32), jnp.arange(count, dtype=jnp.int32))
    return (outs.reshape(rows, heads, -1), totals.transpose(1, 0, 2).reshape(heads, rows))

def attention_backward(query, ext_keys, ext_values, ids_query, ids_key, log_total, attended, grad_out, block, reach):
    rows = query.shape[0]
    count = rows // block
    zero = jnp.zeros(ext_keys.shape, jnp.float32)

    def step(carry, index):
        keys_acc, values_acc = carry
        start = index * block
        span = block + 2 * reach
        q_block = lax.dynamic_slice_in_dim(query, start, block, 0)
        k_block = lax.dynamic_slice_in_dim(ext_keys, start, span, 0)
        v_block = lax.dynamic_slice_in_dim(ext_values, start, span, 0)
        allowed = window_mask(lax.dynamic_slice_in_dim(ids_query, start, block, 0), lax.dynamic_slice_in_dim(ids_key, start, span, 0), reach)
        lse_block = lax.dynamic_slice_in_dim(log_total, start, block, 1)
        a_block = lax.dynamic_slice_in_dim(attended, start, block, 0)
        g_block = lax.dynamic_slice_in_dim(grad_out, start, block, 0)
        grad_query, grad_keys, grad_values = attend_backward(q_block, k_block, v_block, allowed, lse_block, a_block, g_block)
        keys_acc = lax.dynamic_update_slice_in_dim(keys_acc, lax.dynamic_slice_in_dim(keys_acc, start, span, 0) + grad_keys, start, 0)
        values_acc = lax.dynamic_update_slice_in_dim(values_acc, lax.dynamic_slice_in_dim(values_acc, start, span, 0) + grad_values, start, 0)
        return ((keys_acc, values_acc), grad_query)
    (keys_acc, values_acc), grads = lax.scan(step, (zero, zero), jnp.arange(count, dtype=jnp.int32))
    return (grads.reshape(query.shape), keys_acc, values_acc)

def stream_layer(tokens, lengths_row, attn_gain, qkv_weight, out_weight, mlp_gain, in_weight, down_weight, grad_rows):
    rows = tokens.shape[0]
    width = tokens.shape[1]
    heads = attn_gain.shape[0] // HEAD
    hidden_units = down_weight.shape[1]
    reach = WIN
    block = min(rows, 512)
    positions = jnp.arange(rows, dtype=jnp.int32)
    outer = jnp.arange(rows + 2 * reach, dtype=jnp.int32) - reach
    ids_query = doc_ids(lengths_row, positions)
    ids_key = doc_ids(lengths_row, outer)
    cosine, sine = rope_tables(positions, HEAD)
    resid_in = tokens.astype(jnp.float32)
    scaled_one, inverse_one, normed_one = norm_forward(resid_in, attn_gain)
    projected = jnp.dot(normed_one, qkv_weight, preferred_element_type=jnp.float32)
    split = projected.reshape(rows, 3, heads, HEAD)
    query = rotate(split[:, 0], cosine, sine).astype(jnp.bfloat16)
    keys = rotate(split[:, 1], cosine, sine).astype(jnp.bfloat16)
    values = split[:, 2].astype(jnp.bfloat16)
    padding = ((reach, reach), (0, 0), (0, 0))
    ext_keys = jnp.pad(keys, padding)
    ext_values = jnp.pad(values, padding)
    attended, log_total = attention_forward(query, ext_keys, ext_values, ids_query, ids_key, block, reach)
    attended_flat = attended.reshape(rows, width)
    middle = resid_in + jnp.dot(attended_flat, out_weight, preferred_element_type=jnp.float32)
    scaled_two, inverse_two, normed_two = norm_forward(middle, mlp_gain)
    hidden = jnp.dot(normed_two, in_weight, preferred_element_type=jnp.float32)
    inner, gate = (hidden[:, :hidden_units], hidden[:, hidden_units:])
    activated, slope = gelu_parts(inner)
    mixed = (activated * gate).astype(jnp.bfloat16)
    projected_down = lax.dot_general(mixed, down_weight, (((1,), (1,)), ((), ())), preferred_element_type=jnp.float32)
    output = (middle + projected_down).astype(jnp.bfloat16)
    grad_down = lax.dot_general(grad_rows, mixed, (((0,), (0,)), ((), ())), preferred_element_type=jnp.float32)
    grad_mixed = jnp.dot(grad_rows, down_weight, preferred_element_type=jnp.float32)
    grad_hidden = jnp.concatenate([grad_mixed * gate * slope, grad_mixed * activated], axis=1).astype(jnp.bfloat16)
    grad_in = lax.dot_general(normed_two, grad_hidden, (((0,), (0,)), ((), ())), preferred_element_type=jnp.float32)
    grad_normed_two = lax.dot_general(grad_hidden, in_weight, (((1,), (1,)), ((), ())), preferred_element_type=jnp.float32)
    back_two, grad_gain_two = norm_backward(grad_normed_two, scaled_two, inverse_two, mlp_gain)
    grad_middle = grad_rows.astype(jnp.float32) + back_two
    grad_middle_b = grad_middle.astype(jnp.bfloat16)
    grad_out_weight = lax.dot_general(attended_flat, grad_middle_b, (((0,), (0,)), ((), ())), preferred_element_type=jnp.float32)
    grad_attended = lax.dot_general(grad_middle_b, out_weight, (((1,), (1,)), ((), ())), preferred_element_type=jnp.float32).astype(jnp.bfloat16)
    grad_query, keys_acc, values_acc = attention_backward(query, ext_keys, ext_values, ids_query, ids_key, log_total, attended, grad_attended.reshape(rows, heads, HEAD), block, reach)
    grad_keys = unrotate(keys_acc[reach:reach + rows], cosine, sine)
    grad_values = values_acc[reach:reach + rows]
    grad_query = unrotate(grad_query, cosine, sine)
    grad_projected = jnp.concatenate([grad_query.reshape(rows, width), grad_keys.reshape(rows, width), grad_values.reshape(rows, width)], axis=1).astype(jnp.bfloat16)
    grad_qkv = lax.dot_general(normed_one, grad_projected, (((0,), (0,)), ((), ())), preferred_element_type=jnp.float32)
    grad_normed_one = lax.dot_general(grad_projected, qkv_weight, (((1,), (1,)), ((), ())), preferred_element_type=jnp.float32)
    back_one, grad_gain_one = norm_backward(grad_normed_one, scaled_one, inverse_one, attn_gain)
    input_grad = grad_middle + back_one
    return (output, input_grad, (grad_gain_one, grad_qkv, grad_out_weight, grad_gain_two, grad_in, grad_down))

def reference(layer_input, doc_lengths, attn_gain, qkv_weight, out_weight, mlp_gain, in_weight, down_weight, out_grad):
    qkv_flat = qkv_weight.reshape(D, 3 * D)
    in_flat = in_weight.reshape(D, 2 * FF)
    outputs = []
    inputs_grads = []
    sums = None
    for stream in range(N_FSDP):
        output, input_grad, grads = stream_layer(layer_input[stream], doc_lengths[stream], attn_gain, qkv_flat, out_weight, mlp_gain, in_flat, down_weight, out_grad[stream])
        outputs.append(output)
        inputs_grads.append(input_grad)
        if sums is None:
            sums = grads
        else:
            sums = tuple((left + right for left, right in zip(sums, grads)))
    return (jnp.stack(outputs), jnp.stack(inputs_grads), sums[0], sums[1].reshape(D, 3, D), sums[2], sums[3], sums[4].reshape(D, 2, FF), sums[5])
```

```python
import functools

import jax
import jax.numpy as jnp
from jax import lax
from jax.experimental import pallas as pl
from jax.experimental.pallas import tpu as pltpu
from jax.sharding import PartitionSpec as P

HEAD = 64
WIN = 64


EPSILON = 1e-05


class Place:
    def __init__(self, axis):
        self.axis = axis
        self.n = lax.axis_size(axis)
        self.length = self.n // 2
        me = lax.axis_index(axis)
        self.me = me
        self.at = me // 2
        self.side = me % 2

    def partner(self):
        return {self.axis: self.at * 2 + (1 - self.side)}

    def right(self):
        return {self.axis: self.me + 2}

    def left(self):
        return {self.axis: self.me - 2}

    def has_right(self):
        return self.at < self.length - 1

    def has_left(self):
        return self.at > 0

    def greet(self, barrier):
        mesh = pl.DeviceIdType.MESH
        pl.semaphore_signal(barrier, inc=1, device_id=self.partner(), device_id_type=mesh)

        @pl.when(self.has_left())
        def _():
            pl.semaphore_signal(barrier, inc=1, device_id=self.left(), device_id_type=mesh)

        @pl.when(self.has_right())
        def _():
            pl.semaphore_signal(barrier, inc=1, device_id=self.right(), device_id_type=mesh)

    def diagonal(self):
        there = jnp.where(self.side == 1, self.has_right(), self.has_left())
        return there, {self.axis: self.me + 2 * self.side - 1}

    def peers(self):
        one, none = jnp.int32(1), jnp.int32(0)
        return 1 + jnp.where(self.has_left(), one, none) + jnp.where(self.has_right(), one, none)


def remote(src, dst, send, recv, device):
    return pltpu.make_async_remote_copy(
        src_ref=src,
        dst_ref=dst,
        send_sem=send,
        recv_sem=recv,
        device_id=device,
        device_id_type=pl.DeviceIdType.MESH,
    )


class Gather:
    scratch = staticmethod(
        lambda n: [
            pltpu.SemaphoreType.DMA((3, n)),
            pltpu.SemaphoreType.DMA((n,)),
            pltpu.SemaphoreType.DMA,
        ]
    )

    def __init__(self, place, src, dst, sems):
        self.place, self.src, self.dst = place, src, dst
        self.send, self.recv, self.local = sems

    def copy(self, way, block, device, own=False):
        src = self.src if own else self.dst.at[block]
        return remote(src, self.dst.at[block], self.send.at[way, block], self.recv.at[block], device)

    def onward(self, block, own, act):
        place = self.place
        act(self.copy(0, block, place.partner(), own))

    def start(self):
        place = self.place
        pltpu.make_async_copy(self.src, self.dst.at[place.me], self.local).start()
        self.ahead(place.me, True, lambda c: c.start())
        self.behind(place.me, True, lambda c: c.start())
        self.onward(place.me, True, lambda c: c.start())

    def ahead(self, block, own, act):
        place = self.place

        @pl.when(place.has_right())
        def _():
            act(self.copy(1, block, place.right(), own))

    def behind(self, block, own, act):
        place = self.place

        @pl.when(place.has_left())
        def _():
            act(self.copy(2, block, place.left(), own))

    def step(self, d):
        place = self.place

        @pl.when(place.at - d >= 0)
        def _():
            block = place.me - 2 * d
            self.copy(1, block, place.partner()).wait_recv()
            self.ahead(block, False, lambda c: c.start())
            self.onward(block, False, lambda c: c.start())

        @pl.when(place.at + d < place.length)
        def _():
            block = place.me + 2 * d
            self.copy(2, block, place.partner()).wait_recv()
            self.behind(block, False, lambda c: c.start())
            self.onward(block, False, lambda c: c.start())

    def finish(self):
        place = self.place
        pltpu.make_async_copy(self.src, self.dst.at[place.me], self.local).wait()

        def arrived(i, carry):
            self.copy(0, 2 * i + 1 - place.side, place.partner()).wait_recv()
            self.onward(2 * i + place.side, False, lambda c: c.wait_send())

            @pl.when(i <= place.at)
            def _():
                self.ahead(2 * i + place.side, False, lambda c: c.wait_send())

            @pl.when(i >= place.at)
            def _():
                self.behind(2 * i + place.side, False, lambda c: c.wait_send())

            return carry

        lax.fori_loop(0, place.length, arrived, 0)


class Reduce:
    @staticmethod
    def scratch(n, block, dtype):
        length = n // 2
        return [
            pltpu.VMEM((length,) + block, dtype),
            pltpu.VMEM((length + 1,) + block, dtype),
            pltpu.SemaphoreType.DMA((2, length)),
            pltpu.SemaphoreType.DMA((length,)),
            pltpu.SemaphoreType.DMA((length + 1,)),
        ]

    def __init__(self, place, src, dst, scratch):
        self.place, self.src, self.dst = place, src, dst
        self.paired, self.lined, self.send, self.pair_recv, self.line_recv = scratch

    def mine(self, i):
        return self.src.at[2 * i + self.place.side]

    def across(self, i):
        place = self.place
        return remote(
            self.src.at[2 * i + 1 - place.side],
            self.paired.at[i],
            self.send.at[0, i],
            self.pair_recv.at[i],
            place.partner(),
        )

    def along(self, i, slot, device):
        return remote(
            self.mine(i), self.lined.at[slot], self.send.at[1, i], self.line_recv.at[slot], device
        )

    def exchange(self, d):
        place = self.place

        @pl.when(place.at + d < place.length)
        def _():
            self.across(place.at + d).start()

        @pl.when(jnp.logical_and(d > 0, place.at - d >= 0))
        def _():
            self.across(place.at - d).start()

    def add(self, out, refs):
        rows = out.shape[0]
        tile = 16 if rows % 16 == 0 else 8

        def each(i, carry):
            at = pl.ds(pl.multiple_of(i * tile, tile), tile)
            total = refs[0][at, :].astype(jnp.float32)
            for ref in refs[1:]:
                total = total + ref[at, :].astype(jnp.float32)
            out[at, :] = total.astype(out.dtype)
            return carry

        lax.fori_loop(0, rows // tile, each, 0)

    def own(self, i):
        self.across(i).wait_recv()
        return [self.mine(i), self.paired.at[i]]

    def step(self, d):
        place = self.place

        @pl.when(place.at + d < place.length)
        def _():
            i = place.at + d
            refs = self.own(i)

            @pl.when(place.has_left())
            def _():
                self.along(i, i, place.partner()).wait_recv()
                self.add(self.mine(i), refs + [self.lined.at[i]])

            @pl.when(jnp.logical_not(place.has_left()))
            def _():
                self.add(self.mine(i), refs)

            self.along(i, i, place.right()).start()

        @pl.when(place.at - d >= 0)
        def _():
            i = place.at - d
            refs = self.own(i)

            @pl.when(place.has_right())
            def _():
                self.along(i, i, place.partner()).wait_recv()
                self.add(self.mine(i), refs + [self.lined.at[i]])

            @pl.when(jnp.logical_not(place.has_right()))
            def _():
                self.add(self.mine(i), refs)

            slot = jnp.where(d == 1, place.length, i)
            self.along(i, slot, place.left()).start()

    def last(self):
        place = self.place
        i, extra = place.at, place.length
        refs = self.own(i)

        @pl.when(place.has_left())
        def _():
            self.along(i, i, place.partner()).wait_recv()

        @pl.when(place.has_right())
        def _():
            self.along(i, extra, place.partner()).wait_recv()

        both = jnp.logical_and(place.has_left(), place.has_right())

        @pl.when(both)
        def _():
            self.add(self.dst, refs + [self.lined.at[i], self.lined.at[extra]])

        @pl.when(jnp.logical_and(place.has_left(), jnp.logical_not(both)))
        def _():
            self.add(self.dst, refs + [self.lined.at[i]])

        @pl.when(jnp.logical_and(place.has_right(), jnp.logical_not(both)))
        def _():
            self.add(self.dst, refs + [self.lined.at[extra]])

    def finish(self):
        place = self.place

        def each(i, carry):
            self.across(i).wait_send()

            @pl.when(i != place.at)
            def _():
                self.along(i, i, place.partner()).wait_send()

            return carry

        lax.fori_loop(0, place.length, each, 0)


class Halo:
    scratch = staticmethod(lambda: [pltpu.SemaphoreType.DMA((2,)), pltpu.SemaphoreType.DMA((2,))])

    def __init__(self, place, src, mid, sems):
        self.place, self.src, self.mid = place, src, mid
        self.send, self.recv = sems
        self.after = place.me < place.n - 1
        self.before = place.me > 0

    def copy(self, way):
        rows, width = self.src.shape[0], self.mid.shape[1]
        at = rows - width if way == 0 else 0
        other = {self.place.axis: self.place.me + 1 - 2 * way}
        return remote(
            self.src.at[pl.ds(at, width)],
            self.mid.at[way],
            self.send.at[way],
            self.recv.at[way],
            other,
        )

    def start(self):
        @pl.when(self.after)
        def _():
            self.copy(0).start()

        @pl.when(self.before)
        def _():
            self.copy(1).start()

        @pl.when(jnp.logical_not(self.before))
        def _():
            self.mid[0] = jnp.zeros(self.mid.shape[1:], self.mid.dtype)

        @pl.when(jnp.logical_not(self.after))
        def _():
            self.mid[1] = jnp.zeros(self.mid.shape[1:], self.mid.dtype)

    def arrive(self):
        @pl.when(self.before)
        def _():
            self.copy(0).wait_recv()

        @pl.when(self.after)
        def _():
            self.copy(1).wait_recv()

    def finish(self):
        @pl.when(self.after)
        def _():
            self.copy(0).wait_send()

        @pl.when(self.before)
        def _():
            self.copy(1).wait_send()


def greet_all(places, slanted):
    barrier = pltpu.get_barrier_semaphore()
    extra = jnp.int32(0)
    if slanted:
        there, device = places[0].diagonal()
        extra = jnp.where(there, jnp.int32(1), jnp.int32(0))

        @pl.when(there)
        def _():
            pl.semaphore_signal(
                barrier, inc=1, device_id=device, device_id_type=pl.DeviceIdType.MESH
            )

    for place in places:
        place.greet(barrier)
    pl.semaphore_wait(barrier, extra + sum(place.peers() for place in places))


def steps(jobs, down, skip=0, stop=None):
    length = jobs[0].place.length
    stop = length - 1 if stop is None else min(stop, length - 1)

    def each(k, carry):
        d = length - 1 - k if down else k + 1
        for job in jobs:
            job.step(d)
        return carry

    if skip < stop:
        lax.fori_loop(skip, stop, each, 0)


def exchanges(jobs):
    length = jobs[0].place.length

    def each(k, carry):
        for job in jobs:
            job.exchange(length - 1 - k)
        return carry

    lax.fori_loop(0, length, each, 0)


B16, F32 = jnp.bfloat16, jnp.float32
LANES = 128
TILE = 256
CHUNK = 32


class Edge(Halo):
    def copy(self, way):
        other = {self.place.axis: self.place.me + 1 - 2 * way}
        return remote(
            self.src.at[way], self.mid.at[way], self.send.at[way], self.recv.at[way], other
        )


class Plan:
    def __init__(self):
        self.names, self.shapes = [], []

    def add(self, name, *items):
        self.names += [name] * len(items)
        self.shapes += items

    def vmem(self, name, shape, dtype):
        self.add(name, pltpu.VMEM(shape, dtype))


class Refs:
    def __init__(self, names, refs):
        self.groups = {}
        for name, ref in zip(names, refs):
            self.groups.setdefault(name, []).append(ref)

    def __getattr__(self, name):
        return self.groups[name][0]

    def all(self, name):
        return self.groups[name]


def nn(left, right):
    return jnp.dot(left, right, preferred_element_type=F32)


def nt(left, right):
    return lax.dot_general(left, right, (((1,), (1,)), ((), ())), preferred_element_type=F32)


def loop(count, body):
    def each(i, carry):
        body(i)
        return carry

    lax.fori_loop(0, count, each, 0)


def span(i, width):
    return pl.ds(pl.multiple_of(i * width, width), width)


def norm_forward(values, gain):
    mean = jnp.mean(values, axis=-1, keepdims=True)
    centred = values - mean
    inverse = lax.rsqrt(jnp.mean(centred * centred, axis=-1, keepdims=True) + EPSILON)
    scaled = centred * inverse
    return (scaled, inverse, (scaled * gain).astype(B16))


def norm_backward(grad, scaled, inverse, gain):
    weighted = grad * gain
    return inverse * (
        weighted
        - jnp.mean(weighted, axis=-1, keepdims=True)
        - scaled * jnp.mean(weighted * scaled, axis=-1, keepdims=True)
    )


def gelu_parts(inner):
    cdf = 0.5 * (1.0 + lax.erf(inner * 0.7071067811865476))
    density = jnp.exp(-0.5 * inner * inner) * 0.3989422804014327
    return (inner * cdf, cdf + inner * density)


def swap(field):
    lane = lax.broadcasted_iota(jnp.int32, field.shape, 1)
    half = HEAD // 2
    return jnp.where(
        lane % HEAD < half, pltpu.roll(field, LANES - half, 1), pltpu.roll(field, half, 1)
    )


def rotate(field, cosine, sine):
    return field * cosine + swap(field) * sine


def unrotate(field, cosine, sine):
    return field * cosine - swap(field) * sine


def halves(field):
    lane = lax.broadcasted_iota(jnp.int32, field.shape, 1)
    low = lane < HEAD
    zero = jnp.zeros_like(field)
    return jnp.concatenate([jnp.where(low, field, zero), jnp.where(low, zero, field)], axis=0)


def layer_kernel(names, count, *refs):
    r = Refs(names, refs)
    seq, fsdp = Place("seq"), Place("fsdp")
    rows, width = r.tok.shape
    streams = r.tok_all.shape[0]
    group = streams * rows
    quarter = r.att.shape[1]
    pairs = quarter // LANES
    part = r.wa.shape[0]
    reach, outer = WIN, rows + 2 * WIN
    main = r.wb2.shape[1] // LANES
    tail = count - main * LANES
    flat = main * LANES
    rim_at = 2 * flat
    blocks = TILE // part
    tiles = width // TILE
    per = rows // CHUNK
    scale = HEAD**-0.5
    three = 3 * quarter
    half_streams = TILE // rows

    tokens = Gather(fsdp, r.tok, r.tok_all, r.all("tok_g"))
    cots = Gather(fsdp, r.grd, r.grd_all, r.all("grd_g"))
    halo = Halo(seq, r.tok, r.rim_mid, r.all("halo_s"))
    rim = Gather(fsdp, r.rim_mid, r.rim_all, r.all("rim_g"))
    gains = Gather(seq, r.gains, r.gains_mid, r.all("gains_g"))
    gains2 = Gather(fsdp, r.gains_mid, r.gains_all, r.all("gains2_g"))
    get_a = Gather(seq, r.wa, r.a_all, r.all("a_g"))
    get_b1 = Gather(seq, r.wb1, r.b1_all, r.all("b1_g"))
    get_b2 = Gather(seq, r.wb2, r.b2_all, r.all("b2_g"))
    attn = Reduce(fsdp, r.src_a, r.attn_mid, r.all("attn_r"))
    attn2 = Gather(fsdp, r.attn_mid, r.attn_all, r.all("attn_g"))
    back = Reduce(fsdp, r.src_a, r.back_mid, r.all("back_r"))
    back2 = Gather(fsdp, r.back_mid, r.back_all, r.all("back_g"))
    down = Reduce(fsdp, r.src_b, r.down_sum, r.all("down_r"))
    one = Reduce(fsdp, r.src_b, r.one_sum, r.all("one_r"))
    put_b1 = Reduce(seq, r.gb1, r.db1, r.all("b1_r"))
    put_b2 = Reduce(seq, r.gb2, r.db2, r.all("b2_r"))
    put_a = Reduce(seq, r.ga, r.da, r.all("a_r"))
    put_g = Reduce(seq, r.gain_parts, r.gain_mid, r.all("gain_r"))
    put_g2 = Gather(fsdp, r.gain_mid, r.dgain, r.all("gain_g"))
    edge = Edge(seq, r.edge_src, r.edge_mid, r.all("edge_s"))

    greet_all((seq, fsdp), True)
    halo.start()
    for job in (gains, tokens, get_a, cots):
        job.start()
    halo.arrive()
    rim.start()
    steps([tokens, cots, rim], False)
    steps([gains, get_a], False)
    get_b1.start()
    get_b2.start()
    gains.finish()
    gains2.start()
    steps([gains2], False)
    gains2.finish()

    for k in range(width // LANES):
        total = jnp.zeros((r.gains.shape[0], LANES), F32)
        for s in range(k * LANES // part, (k + 1) * LANES // part):
            for f in range(streams):
                total = total + r.gains_all[f, s].astype(F32)
        r.gain[:, k * LANES : (k + 1) * LANES] = total
    tokens.finish()
    rim.finish()
    halo.finish()

    def norm_own(i):
        s, h = i // per, i % per
        x = r.tok_all[s, span(h, CHUNK), :].astype(F32)
        at = pl.ds(pl.multiple_of(reach + h * CHUNK, CHUNK), CHUNK)
        r.nx[s, at, :] = norm_forward(x, r.gain[0:1, :])[2]

    loop(streams * per, norm_own)

    rims = reach // CHUNK

    def norm_rim(i):
        s, w, h = i // (2 * rims), i // rims % 2, i % rims
        x = r.rim_all[s, w, span(h, CHUNK), :].astype(F32)
        at = pl.ds(pl.multiple_of(w * (rows + reach) + h * CHUNK, CHUNK), CHUNK)
        r.nx[s, at, :] = norm_forward(x, r.gain[0:1, :])[2]

    loop(streams * 2 * rims, norm_rim)

    def turn_one(i):
        x = r.nx[:, reach : reach + rows, span(i, LANES)].reshape(group, LANES)
        r.n1t[span(i, LANES), :] = x.T

    loop(width // LANES, turn_one)
    cots.finish()

    def turn_grad(i):
        x = r.grd_all[:, :, span(i, LANES)].reshape(group, LANES)
        r.gt[span(i, LANES), :] = x.T

    loop(width // LANES, turn_grad)
    get_a.finish()

    band = jnp.abs(
        lax.broadcasted_iota(jnp.int32, (rows, outer), 0)
        + reach
        - lax.broadcasted_iota(jnp.int32, (rows, outer), 1)
    )

    def lanes(p):
        return slice(p * LANES, (p + 1) * LANES)

    def project(s):
        x = r.nx[s]
        out = nn(x, r.a_all[:, :, quarter:three].reshape(width, 2 * quarter))
        for p in range(pairs):
            keys = rotate(out[:, lanes(p)], r.cosine[...], r.sine[...])
            r.k2[s, p] = halves(keys).astype(B16)
            r.v2[s, p] = halves(out[:, lanes(pairs + p)]).astype(B16)
        out = nn(x[reach : reach + rows], r.a_all[:, :, :quarter].reshape(width, quarter))
        for p in range(pairs):
            query = rotate(
                out[:, lanes(p)], r.cosine[reach : reach + rows], r.sine[reach : reach + rows]
            )
            r.qs[s, p] = query.astype(B16)
            r.q2[s, p] = halves(query).astype(B16)

    loop(streams, project)

    def visible(s):
        return (band <= reach) & (r.idq[s] == r.idk[s])

    def attend(s):
        allowed = visible(s)
        for p in range(pairs):
            scores = nt(r.qs[s, p], r.k2[s, p]) * scale
            probs = []
            for h in range(2):
                masked = jnp.where(allowed, scores[:, h * outer : (h + 1) * outer], -1e30)
                top = jnp.max(masked, axis=-1, keepdims=True)
                expd = jnp.exp(masked - top)
                total = jnp.sum(expd, axis=-1, keepdims=True)
                r.lse[s, 2 * p + h] = jnp.broadcast_to(top + jnp.log(total), (rows, LANES))
                probs.append((expd / total).astype(B16))
            out = nn(jnp.concatenate(probs, axis=1), r.v2[s, p])
            r.att[span(s, rows), lanes(p)] = out.astype(B16)

    loop(streams, attend)

    def out_project(j):
        w = r.a_all[span(j, blocks), :, three:].reshape(TILE, quarter)
        out = nt(r.att[...], w).astype(B16)
        r.src_a[:, :, span(j, TILE)] = out.reshape(streams, rows, TILE)

    loop(tiles, out_project)
    exchanges([attn])
    steps([get_b1, get_b2], False, stop=1)
    steps([attn], True)
    attn.last()
    attn2.start()
    steps([get_b1, get_b2], False, skip=1, stop=2)
    steps([attn2], False)
    attn2.finish()
    attn.finish()

    def norm_two(i):
        s, h = i // per, i % per
        at = span(h, CHUNK)
        x = r.tok_all[s, at, :].astype(F32) + r.attn_all[s, at, :].astype(F32)
        scaled, inverse, normed = norm_forward(x, r.gain[1:2, :])
        r.scaled[span(i, CHUNK), :] = scaled
        r.inverse[span(i, CHUNK), :] = jnp.broadcast_to(inverse, (CHUNK, LANES))
        r.nx[s, pl.ds(pl.multiple_of(rows + h * CHUNK, CHUNK), CHUNK), :] = normed

    loop(streams * per, norm_two)
    steps([get_b1, get_b2], False, skip=2)

    def normed_two(m):
        return r.nx[span(m, half_streams), rows : 2 * rows, :].reshape(TILE, width)

    def turn_two(i):
        x = r.nx[:, rows : 2 * rows, span(i, LANES)].reshape(group, LANES)
        r.tt[span(i, LANES), :] = x.T

    loop(width // LANES, turn_two)
    get_b1.finish()

    sides = group // TILE
    rest = flat + LANES

    def hidden(i):
        m, j = i // main, i % main
        w = r.b1_all[:, :, span(j, TILE)].reshape(width, TILE)
        out = nn(normed_two(m), w)
        inner, gate = out[:, :LANES], out[:, LANES:]
        activated, slope = gelu_parts(inner)
        at = span(m, TILE)
        r.big[at, span(j, LANES)] = activated
        r.big[at, pl.ds(pl.multiple_of(rest + j * LANES, LANES), LANES)] = gate * slope
        r.mix[at, span(j, LANES)] = (activated * gate).astype(B16)

    loop(sides * main, hidden)
    lane = lax.broadcasted_iota(jnp.int32, (TILE, LANES), 1)

    def hidden_rim(m):
        w = r.b1_all[:, :, rim_at:].reshape(width, LANES)
        inner = nn(normed_two(m), w)
        gate = pltpu.roll(inner, LANES - tail, 1)
        activated, slope = gelu_parts(inner)
        at = span(m, TILE)
        zero = jnp.zeros((TILE, LANES), F32)
        mixed = jnp.where(lane < tail, activated * gate, zero)
        r.big[at, flat:rest] = jnp.where(lane < tail, activated, zero)
        r.big[at, rest + flat :] = jnp.where(lane < tail, gate * slope, zero)
        r.mix[at, flat:] = mixed.astype(B16)
        r.mix_rim[at, :] = pltpu.roll(mixed, 2 * tail, 1).astype(B16)

    loop(sides, hidden_rim)

    def grad_down(m):
        out = nn(r.gt[span(m, TILE), :], r.mix[:, :flat]).astype(B16)
        r.gb2[span(m, blocks), :, :] = out.reshape(blocks, part, flat)

    loop(tiles, grad_down)
    get_b2.finish()
    exchanges([put_b2])

    def unpack(j):
        at = span(j, TILE)
        r.dfull[at, :flat] = r.b2_all[span(j, blocks), :, :].reshape(TILE, flat)
        x = r.b1_all[span(j, blocks), :, rim_at:].reshape(TILE, LANES).astype(F32)
        x = jnp.where(lane < tail, pltpu.roll(x, LANES - 2 * tail, 1), jnp.zeros_like(x))
        r.dfull[at, flat:] = x.astype(B16)

    loop(tiles, unpack)

    def grad_hidden(m, t, grad):
        at = span(m, TILE)
        inner = grad * r.big[at, pl.ds(pl.multiple_of(rest + t * LANES, LANES), LANES)]
        gate = grad * r.big[at, span(t, LANES)]
        return at, inner, gate

    def grad_mixed(i):
        m, t = i // main, i % main
        g = r.grd_all[span(m, half_streams)].reshape(TILE, width)
        grad = nn(g, r.dfull[:, span(t, LANES)])
        at, inner, gate = grad_hidden(m, t, grad)
        r.gh[at, span(2 * t, LANES)] = inner.astype(B16)
        r.gh[at, span(2 * t + 1, LANES)] = gate.astype(B16)

    loop(sides * main, grad_mixed)

    def grad_mixed_rim(m):
        g = r.grd_all[span(m, half_streams)].reshape(TILE, width)
        grad = nn(g, r.dfull[:, flat:])
        at, inner, gate = grad_hidden(m, main, grad)
        r.gh[at, rim_at:] = (inner + pltpu.roll(gate, tail, 1)).astype(B16)

    loop(sides, grad_mixed_rim)

    def grad_in(i):
        m, j = i // main, i % main
        out = nn(r.tt[span(m, TILE), :], r.gh[:, span(j, TILE)]).astype(B16)
        r.gb1[span(m, blocks), :, span(j, TILE)] = out.reshape(blocks, part, TILE)

    loop(tiles * main, grad_in)

    def grad_in_rim(m):
        at = span(m, TILE)
        out = nn(r.tt[at, :], r.gh[:, rim_at:]) + nn(r.gt[at, :], r.mix_rim[...])
        r.gb1[span(m, blocks), :, rim_at:] = out.astype(B16).reshape(blocks, part, LANES)

    loop(tiles, grad_in_rim)
    exchanges([put_b1])
    r.gain_row[...] = jnp.zeros(r.gain_row.shape, F32)

    def back_project(j):
        w = r.b1_all[span(j, blocks)].reshape(TILE, rim_at + LANES)
        out = nt(r.gh[...], w)
        at = span(j, TILE)
        r.gain_row[1:2, at] = jnp.sum(out * r.scaled[:, at], axis=0, keepdims=True)
        r.src_a[:, :, at] = out.astype(B16).reshape(streams, rows, TILE)

    loop(tiles, back_project)
    exchanges([back])

    def down_project(j):
        out = nt(r.mix[...], r.dfull[span(j, TILE), :]).astype(B16)
        r.src_b[:, :, span(j, TILE)] = out.reshape(streams, rows, TILE)

    loop(tiles, down_project)
    exchanges([down])
    steps([back], True)
    back.last()
    back2.start()
    steps([put_b2, put_b1], True, stop=1)
    steps([down], True)
    steps([back2], False)
    back2.finish()
    back.finish()

    def middle_grad(i):
        s, h = i // per, i % per
        at = span(h, CHUNK)
        here = span(i, CHUNK)
        got = norm_backward(
            r.back_all[s, at, :].astype(F32),
            r.scaled[here, :],
            r.inverse[here, 0:1],
            r.gain[1:2, :],
        )
        grad = r.grd_all[s, at, :].astype(F32) + got
        r.nx[s, at, :] = grad.astype(B16)

        @pl.when(s == fsdp.me)
        def _():
            r.own_grad[at, :] = grad

    loop(streams * per, middle_grad)

    def turn_middle(i):
        x = r.nx[:, :rows, span(i, LANES)].reshape(group, LANES)
        r.tt[span(i, LANES), :] = x.T

    loop(width // LANES, turn_middle)

    def grad_attended(s):
        w = r.a_all[:, :, three:].reshape(width, quarter)
        r.gatt[span(s, TILE), :] = nn(
            r.nx[span(s, half_streams), :rows, :].reshape(TILE, width), w
        ).astype(B16)

    loop(sides, grad_attended)
    down.last()
    steps([put_b2, put_b1], True, skip=1, stop=2)

    def attend_back(s):
        allowed = visible(s)
        at = span(s, rows)
        low = lax.broadcasted_iota(jnp.int32, (rows, LANES), 1) < HEAD
        for p in range(pairs):
            scores = nt(r.qs[s, p], r.k2[s, p]) * scale
            grad = r.gatt[at, lanes(p)]
            grad_probs = nt(grad, r.v2[s, p])
            grad_f = grad.astype(F32)
            product = grad_f * r.att[at, lanes(p)].astype(F32)
            zero = jnp.zeros_like(product)
            agains, grads = [], []
            for h in range(2):
                cut = slice(h * outer, (h + 1) * outer)
                masked = jnp.where(allowed, scores[:, cut], -1e30)
                again = jnp.exp(masked - r.lse[s, 2 * p + h][:, 0:1])
                side = jnp.where(low, product, zero) if h == 0 else jnp.where(low, zero, product)
                delta = jnp.sum(side, axis=-1, keepdims=True)
                agains.append(again.astype(B16))
                grads.append((again * (grad_probs[:, cut] - delta) * scale).astype(B16))
            grad_query = nn(jnp.concatenate(grads, axis=1), r.k2[s, p])
            grad_keys = nn(jnp.concatenate(grads, axis=0).T, r.q2[s, p])
            grad_values = nn(jnp.concatenate(agains, axis=0).T, halves(grad_f).astype(B16))
            r.gp[at, lanes(p)] = unrotate(
                grad_query, r.cosine[reach : reach + rows], r.sine[reach : reach + rows]
            ).astype(B16)
            for k, value in ((p, grad_keys), (pairs + p, grad_values)):
                r.own_kv[s, :, lanes(k)] = value[reach : reach + rows]
                r.edge_src[0, span(s, reach), lanes(k)] = value[reach + rows :].astype(B16)
                r.edge_src[1, span(s, reach), lanes(k)] = value[:reach].astype(B16)

    loop(streams, attend_back)
    edge.start()

    def grad_out(m):
        out = nn(r.tt[span(m, TILE), :], r.att[...]).astype(B16)
        r.ga[span(m, blocks), :, three:] = out.reshape(blocks, part, quarter)

    loop(tiles, grad_out)
    steps([put_b2, put_b1], True, skip=2)

    def norm_again(i):
        s, h = i // per, i % per
        x = r.tok_all[s, span(h, CHUNK), :].astype(F32)
        scaled, inverse, _ = norm_forward(x, r.gain[0:1, :])
        r.scaled[span(i, CHUNK), :] = scaled
        r.inverse[span(i, CHUNK), :] = jnp.broadcast_to(inverse, (CHUNK, LANES))

    loop(streams * per, norm_again)
    down.finish()
    edge.arrive()

    def join(s):
        for k in range(2 * pairs):
            value = r.own_kv[s, :, lanes(k)]
            first = value[:reach] + r.edge_mid[0, span(s, reach), lanes(k)].astype(F32)
            final = value[rows - reach :] + r.edge_mid[1, span(s, reach), lanes(k)].astype(F32)
            middle = [value[reach : rows - reach]] if rows > 2 * reach else []
            value = jnp.concatenate([first] + middle + [final], axis=0)
            if k < pairs:
                value = unrotate(
                    value, r.cosine[reach : reach + rows], r.sine[reach : reach + rows]
                )
            r.gp[span(s, rows), lanes(pairs + k)] = value.astype(B16)

    loop(streams, join)

    def grad_qkv(i):
        m, j = i // 3, i % 3
        out = nn(r.n1t[span(m, TILE), :], r.gp[:, span(j, quarter)]).astype(B16)
        r.ga[span(m, blocks), :, span(j, quarter)] = out.reshape(blocks, part, quarter)

    loop(tiles * 3, grad_qkv)
    exchanges([put_a])

    def one_project(j):
        w = r.a_all[span(j, blocks), :, :three].reshape(TILE, three)
        out = nt(r.gp[...], w)
        at = span(j, TILE)
        r.gain_row[0:1, at] = jnp.sum(out * r.scaled[:, at], axis=0, keepdims=True)
        r.src_b[:, :, at] = out.astype(B16).reshape(streams, rows, TILE)

    loop(tiles, one_project)
    exchanges([one])
    for s in range(seq.n):
        k = s * part // LANES
        r.gain_parts[s] = r.gain_row[:, k * LANES : (k + 1) * LANES]
    exchanges([put_g])
    put_b2.last()
    put_b1.last()
    steps([one], True)
    one.last()
    steps([put_g, put_a], True)
    put_g.last()
    put_g2.start()
    put_a.last()
    steps([put_g2], False)

    def final(h):
        at = span(h, CHUNK)
        here = pl.ds(pl.multiple_of(fsdp.me * rows + h * CHUNK, CHUNK), CHUNK)
        got = norm_backward(
            r.one_sum[at, :], r.scaled[here, :], r.inverse[here, 0:1], r.gain[0:1, :]
        )
        r.dinput[at, :] = r.own_grad[at, :] + got
        middle = r.tok[at, :].astype(F32) + r.attn_all[fsdp.me, at, :].astype(F32)
        r.out[at, :] = (middle + r.down_sum[at, :]).astype(B16)

    loop(per, final)
    for job in (edge, one, put_b1, put_b2, put_a, put_g, put_g2):
        job.finish()


def run_layer(tok, grd, gains, wa, wb1, wb2, idq, idk, cosine, sine, count):
    n, nf = lax.axis_size("seq"), lax.axis_size("fsdp")
    rows, width = tok.shape
    part, wide_a = wa.shape
    wide_1, wide_2 = wb1.shape[1], wb2.shape[1]
    quarter = wide_a // 4
    pairs = quarter // LANES
    streams = nf
    group = streams * rows
    outer = rows + 2 * WIN
    vmem = pl.BlockSpec(memory_space=pltpu.VMEM)
    anywhere = pl.BlockSpec(memory_space=pl.ANY)
    ins = [
        ("tok", tok, vmem),
        ("grd", grd, vmem),
        ("gains", gains, vmem),
        ("wa", wa, anywhere),
        ("wb1", wb1, anywhere),
        ("wb2", wb2, anywhere),
        ("idq", idq, vmem),
        ("idk", idk, vmem),
        ("cosine", cosine, vmem),
        ("sine", sine, vmem),
    ]
    outs = [
        ("out", (rows, width), B16),
        ("dinput", (rows, width), F32),
        ("dgain", (nf, 8, LANES), F32),
        ("da", (part, wide_a), F32),
        ("db1", (part, wide_1), F32),
        ("db2", (part, wide_2), F32),
    ]
    plan = Plan()
    token_block = (rows, width)
    for name, count_, shape, dtype in (
        ("tok", nf, token_block, B16),
        ("grd", nf, token_block, B16),
        ("rim", nf, (2, WIN, width), B16),
        ("a", n, wa.shape, B16),
        ("b1", n, wb1.shape, B16),
        ("b2", n, wb2.shape, B16),
        ("attn", nf, token_block, B16),
        ("back", nf, token_block, B16),
    ):
        plan.vmem(name + "_all", (count_,) + shape, dtype)
        plan.add(name + "_g", *Gather.scratch(count_))
    for name, count_, shape, dtype in (
        ("attn", nf, token_block, B16),
        ("back", nf, token_block, B16),
        ("down", nf, token_block, B16),
        ("one", nf, token_block, B16),
        ("b1", n, wb1.shape, B16),
        ("b2", n, wb2.shape, B16),
        ("a", n, wa.shape, B16),
        ("gain", n, (8, LANES), F32),
    ):
        plan.add(name + "_r", *Reduce.scratch(count_, shape, dtype))
    plan.vmem("rim_mid", (2, WIN, width), B16)
    plan.add("halo_s", *Halo.scratch())
    plan.vmem("gains_mid", (n,) + gains.shape, B16)
    plan.add("gains_g", *Gather.scratch(n))
    plan.vmem("gains_all", (nf, n) + gains.shape, B16)
    plan.add("gains2_g", *Gather.scratch(nf))
    plan.vmem("gain_mid", (8, LANES), F32)
    plan.add("gain_g", *Gather.scratch(nf))
    plan.add("edge_s", *Halo.scratch())
    for name, shape, dtype in (
        ("edge_src", (2, streams * WIN, 2 * quarter), B16),
        ("edge_mid", (2, streams * WIN, 2 * quarter), B16),
        ("gain", (gains.shape[0], width), F32),
        ("gain_row", (8, width), F32),
        ("gain_parts", (n, 8, LANES), F32),
        ("nx", (streams, outer, width), B16),
        ("n1t", (width, group), B16),
        ("gt", (width, group), B16),
        ("tt", (width, group), B16),
        ("qs", (streams, pairs, rows, LANES), B16),
        ("q2", (streams, pairs, 2 * rows, LANES), B16),
        ("k2", (streams, pairs, 2 * outer, LANES), B16),
        ("v2", (streams, pairs, 2 * outer, LANES), B16),
        ("lse", (streams, 2 * pairs, rows, LANES), F32),
        ("att", (group, quarter), B16),
        ("src_a", (streams,) + token_block, B16),
        ("src_b", (streams,) + token_block, B16),
        ("attn_mid", token_block, B16),
        ("back_mid", token_block, B16),
        ("down_sum", token_block, F32),
        ("one_sum", token_block, F32),
        ("scaled", (group, width), F32),
        ("inverse", (group, LANES), F32),
        ("big", (group, 2 * (wide_2 + LANES)), F32),
        ("mix", (group, wide_2 + LANES), B16),
        ("mix_rim", (group, LANES), B16),
        ("dfull", (width, wide_2 + LANES), B16),
        ("gh", (group, wide_1), B16),
        ("gb1", (n,) + wb1.shape, B16),
        ("gb2", (n,) + wb2.shape, B16),
        ("ga", (n,) + wa.shape, B16),
        ("own_grad", token_block, F32),
        ("own_kv", (streams, rows, 2 * quarter), F32),
        ("gatt", (group, quarter), B16),
        ("gp", (group, 3 * quarter), B16),
    ):
        plan.vmem(name, shape, dtype)
    names = [i[0] for i in ins] + [o[0] for o in outs] + plan.names
    return pl.pallas_call(
        functools.partial(layer_kernel, tuple(names), count),
        out_shape=[jax.ShapeDtypeStruct(s, d) for _, s, d in outs],
        in_specs=[i[2] for i in ins],
        out_specs=[vmem] * len(outs),
        scratch_shapes=plan.shapes,
        compiler_params=pltpu.CompilerParams(
            collective_id=1, has_side_effects=True, vmem_limit_bytes=63 * 1024 * 1024
        ),
    )(*[i[1] for i in ins])


def doc_ids(lengths, positions):
    docs = lengths.shape[1]
    earlier = jnp.arange(docs)[:, None] > jnp.arange(docs)[None, :]
    starts = jnp.sum(jnp.where(earlier[None], lengths[:, None, :], 0), axis=2)
    total = jnp.sum(lengths, axis=1)
    found = jnp.sum((positions[None, :, None] >= starts[:, None, :]).astype(jnp.int32), axis=2) - 1
    valid = (positions[None] >= 0) & (positions[None] < total[:, None])
    return jnp.where(valid, found, -1).astype(jnp.int32)


def per_device(
    layer_input,
    doc_lengths,
    attn_gain,
    qkv_weight,
    out_weight,
    mlp_gain,
    in_weight,
    down_weight,
    out_grad,
):
    tokens = layer_input[0]
    rows, width = tokens.shape
    quarter = qkv_weight.shape[2]
    share = down_weight.shape[1]
    n_fsdp = lax.axis_size("fsdp")
    part, piece = qkv_weight.shape[0], attn_gain.shape[0]
    device, stream = lax.axis_index("seq"), lax.axis_index("fsdp")
    first = device * rows
    outer = first - WIN + jnp.arange(rows + 2 * WIN, dtype=jnp.int32)
    ids = doc_ids(doc_lengths, outer)
    idq, idk = ids[:, WIN : WIN + rows, None], ids[:, None, :]
    half = HEAD // 2
    lane = jnp.arange(LANES)
    inv_freq = 10000.0 ** (-(2.0 / HEAD) * (lane % half).astype(F32))
    angle = outer.astype(F32)[:, None] * inv_freq[None, :]
    cosine = jnp.cos(angle)
    sine = jnp.where(lane[None, :] % HEAD < half, -1.0, 1.0) * jnp.sin(angle)
    gains = jnp.zeros((16, LANES), B16)
    place = (device * n_fsdp + stream) * piece % LANES
    gains = lax.dynamic_update_slice(gains, jnp.stack([attn_gain, mlp_gain]), (0, place))
    main = share // LANES
    flat, tail = main * LANES, share % LANES
    wa = jnp.concatenate([qkv_weight.reshape(part, 3 * quarter), out_weight.T], axis=1)
    paired = in_weight[:, :, :flat].reshape(part, 2, main, LANES).transpose(0, 2, 1, 3)
    spare = jnp.zeros((part, LANES - 3 * tail), B16)
    wb1 = jnp.concatenate(
        [
            paired.reshape(part, 2 * flat),
            in_weight[:, 0, flat:],
            in_weight[:, 1, flat:],
            down_weight[:, flat:],
            spare,
        ],
        axis=1,
    )
    wb2 = down_weight[:, :flat]
    output, input_grad, dgain, da, db1, db2 = run_layer(
        tokens, out_grad[0], gains, wa, wb1, wb2, idq, idk, cosine, sine, share
    )
    gain = lax.dynamic_slice_in_dim(jnp.sum(dgain, axis=0), place, piece, axis=1)
    grad_in = db1[:, : 2 * flat].reshape(part, main, 2, LANES).transpose(0, 2, 1, 3)
    rim = db1[:, 2 * flat :]
    grad_in = jnp.concatenate(
        [grad_in.reshape(part, 2, flat), rim[:, : 2 * tail].reshape(part, 2, tail)], axis=2
    )
    grad_down = jnp.concatenate([db2, rim[:, 2 * tail : 3 * tail]], axis=1)
    return (
        output[None],
        input_grad[None],
        gain[0],
        da[:, : 3 * quarter].reshape(part, 3, quarter),
        da[:, 3 * quarter :].T,
        gain[1],
        grad_in,
        grad_down,
    )


def solution(mesh):
    in_specs = (
        P("fsdp", "seq", None),
        P(),
        P(("seq", "fsdp")),
        P("seq", None, "fsdp"),
        P("fsdp", "seq"),
        P(("seq", "fsdp")),
        P("seq", None, "fsdp"),
        P("seq", "fsdp"),
        P("fsdp", "seq", None),
    )
    out_specs = (
        P("fsdp", "seq", None),
        P("fsdp", "seq", None),
        P(("seq", "fsdp")),
        P("seq", None, "fsdp"),
        P("fsdp", "seq"),
        P(("seq", "fsdp")),
        P("seq", None, "fsdp"),
        P("seq", "fsdp"),
    )
    return jax.shard_map(
        per_device, mesh=mesh, in_specs=in_specs, out_specs=out_specs, check_vma=False
    )
```

```python
import functools

import jax
import jax.numpy as jnp
import numpy as np
from jax import lax
from jax.experimental import pallas as pl
from jax.experimental.pallas import tpu as pltpu
from jax.sharding import PartitionSpec as P

HEAD = 64
WIN = 64


EPSILON = 1e-05


class Place:
    def __init__(self, axis):
        self.axis = axis
        self.n = lax.axis_size(axis)
        self.length = self.n // 2
        me = lax.axis_index(axis)
        self.me = me
        self.at = me // 2
        self.side = me % 2

    def partner(self):
        return {self.axis: self.at * 2 + (1 - self.side)}

    def right(self):
        return {self.axis: self.me + 2}

    def left(self):
        return {self.axis: self.me - 2}

    def has_right(self):
        return self.at < self.length - 1

    def has_left(self):
        return self.at > 0

    def greet(self, barrier):
        mesh = pl.DeviceIdType.MESH
        pl.semaphore_signal(barrier, inc=1, device_id=self.partner(), device_id_type=mesh)

        @pl.when(self.has_left())
        def _():
            pl.semaphore_signal(barrier, inc=1, device_id=self.left(), device_id_type=mesh)

        @pl.when(self.has_right())
        def _():
            pl.semaphore_signal(barrier, inc=1, device_id=self.right(), device_id_type=mesh)

    def diagonal(self):
        there = jnp.where(self.side == 1, self.has_right(), self.has_left())
        return there, {self.axis: self.me + 2 * self.side - 1}

    def peers(self):
        one, none = jnp.int32(1), jnp.int32(0)
        return 1 + jnp.where(self.has_left(), one, none) + jnp.where(self.has_right(), one, none)


def remote(src, dst, send, recv, device):
    return pltpu.make_async_remote_copy(
        src_ref=src,
        dst_ref=dst,
        send_sem=send,
        recv_sem=recv,
        device_id=device,
        device_id_type=pl.DeviceIdType.MESH,
    )


class Gather:
    scratch = staticmethod(
        lambda n: [
            pltpu.SemaphoreType.DMA((3, n)),
            pltpu.SemaphoreType.DMA((n,)),
            pltpu.SemaphoreType.DMA,
        ]
    )

    def __init__(self, place, src, dst, sems):
        self.place, self.src, self.dst = place, src, dst
        self.send, self.recv, self.local = sems

    def copy(self, way, block, device, own=False):
        src = self.src if own else self.dst.at[block]
        return remote(src, self.dst.at[block], self.send.at[way, block], self.recv.at[block], device)

    def onward(self, block, own, act):
        place = self.place
        act(self.copy(0, block, place.partner(), own))

    def start(self):
        place = self.place
        if self.src is not None:
            pltpu.make_async_copy(self.src, self.dst.at[place.me], self.local).start()
        self.start_lines()
        self.start_across()

    def start_lines(self):
        place = self.place
        self.ahead(place.me, self.src is not None, lambda c: c.start())
        self.behind(place.me, self.src is not None, lambda c: c.start())

    def start_across(self):
        self.onward(self.place.me, self.src is not None, lambda c: c.start())

    def ahead(self, block, own, act):
        place = self.place

        @pl.when(place.has_right())
        def _():
            act(self.copy(1, block, place.right(), own))

    def behind(self, block, own, act):
        place = self.place

        @pl.when(place.has_left())
        def _():
            act(self.copy(2, block, place.left(), own))

    def step(self, d):
        place = self.place

        @pl.when(place.at - d >= 0)
        def _():
            block = place.me - 2 * d
            self.copy(1, block, place.partner()).wait_recv()
            self.ahead(block, False, lambda c: c.start())
            self.onward(block, False, lambda c: c.start())

        @pl.when(place.at + d < place.length)
        def _():
            block = place.me + 2 * d
            self.copy(2, block, place.partner()).wait_recv()
            self.behind(block, False, lambda c: c.start())
            self.onward(block, False, lambda c: c.start())

    def finish(self):
        place = self.place
        if self.src is not None:
            pltpu.make_async_copy(self.src, self.dst.at[place.me], self.local).wait()

        def arrived(i, carry):
            self.copy(0, 2 * i + 1 - place.side, place.partner()).wait_recv()
            self.onward(2 * i + place.side, False, lambda c: c.wait_send())

            @pl.when(i <= place.at)
            def _():
                self.ahead(2 * i + place.side, False, lambda c: c.wait_send())

            @pl.when(i >= place.at)
            def _():
                self.behind(2 * i + place.side, False, lambda c: c.wait_send())

            return carry

        lax.fori_loop(0, place.length, arrived, 0)


class Reduce:
    @staticmethod
    def scratch(n, block, dtype):
        length = n // 2
        return [
            pltpu.VMEM((length,) + block, dtype),
            pltpu.VMEM((length + 1,) + block, dtype),
            pltpu.SemaphoreType.DMA((2, length)),
            pltpu.SemaphoreType.DMA((length,)),
            pltpu.SemaphoreType.DMA((length + 1,)),
        ]

    def __init__(self, place, src, dst, scratch):
        self.place, self.src, self.dst = place, src, dst
        self.paired, self.lined, self.send, self.pair_recv, self.line_recv = scratch

    def mine(self, i):
        return self.src.at[2 * i + self.place.side]

    def across(self, i):
        place = self.place
        return remote(
            self.src.at[2 * i + 1 - place.side],
            self.paired.at[i],
            self.send.at[0, i],
            self.pair_recv.at[i],
            place.partner(),
        )

    def along(self, i, slot, device):
        return remote(
            self.mine(i), self.lined.at[slot], self.send.at[1, i], self.line_recv.at[slot], device
        )

    def exchange(self, d):
        place = self.place

        @pl.when(place.at + d < place.length)
        def _():
            self.across(place.at + d).start()

        @pl.when(jnp.logical_and(d > 0, place.at - d >= 0))
        def _():
            self.across(place.at - d).start()

    def add(self, out, refs):
        rows = out.shape[0]
        tile = 16 if rows % 16 == 0 else 8

        def each(i, carry):
            at = pl.ds(pl.multiple_of(i * tile, tile), tile)
            total = refs[0][at, :].astype(jnp.float32)
            for ref in refs[1:]:
                total = total + ref[at, :].astype(jnp.float32)
            out[at, :] = total.astype(out.dtype)
            return carry

        lax.fori_loop(0, rows // tile, each, 0)

    def own(self, i):
        self.across(i).wait_recv()
        return [self.mine(i), self.paired.at[i]]

    def step(self, d):
        place = self.place

        @pl.when(place.at + d < place.length)
        def _():
            i = place.at + d
            refs = self.own(i)

            @pl.when(place.has_left())
            def _():
                self.along(i, i, place.partner()).wait_recv()
                self.add(self.mine(i), refs + [self.lined.at[i]])

            @pl.when(jnp.logical_not(place.has_left()))
            def _():
                self.add(self.mine(i), refs)

            self.along(i, i, place.right()).start()

        @pl.when(place.at - d >= 0)
        def _():
            i = place.at - d
            refs = self.own(i)

            @pl.when(place.has_right())
            def _():
                self.along(i, i, place.partner()).wait_recv()
                self.add(self.mine(i), refs + [self.lined.at[i]])

            @pl.when(jnp.logical_not(place.has_right()))
            def _():
                self.add(self.mine(i), refs)

            slot = jnp.where(d == 1, place.length, i)
            self.along(i, slot, place.left()).start()

    def last(self):
        place = self.place
        i, extra = place.at, place.length
        refs = self.own(i)

        @pl.when(place.has_left())
        def _():
            self.along(i, i, place.partner()).wait_recv()

        @pl.when(place.has_right())
        def _():
            self.along(i, extra, place.partner()).wait_recv()

        both = jnp.logical_and(place.has_left(), place.has_right())

        @pl.when(both)
        def _():
            self.add(self.dst, refs + [self.lined.at[i], self.lined.at[extra]])

        @pl.when(jnp.logical_and(place.has_left(), jnp.logical_not(both)))
        def _():
            self.add(self.dst, refs + [self.lined.at[i]])

        @pl.when(jnp.logical_and(place.has_right(), jnp.logical_not(both)))
        def _():
            self.add(self.dst, refs + [self.lined.at[extra]])

    def finish(self):
        place = self.place

        def each(i, carry):
            self.across(i).wait_send()

            @pl.when(i != place.at)
            def _():
                self.along(i, i, place.partner()).wait_send()

            return carry

        lax.fori_loop(0, place.length, each, 0)


class Halo:
    scratch = staticmethod(lambda: [pltpu.SemaphoreType.DMA((2,)), pltpu.SemaphoreType.DMA((2,))])

    def __init__(self, place, src, mid, sems):
        self.place, self.src, self.mid = place, src, mid
        self.send, self.recv = sems
        self.after = place.me < place.n - 1
        self.before = place.me > 0

    def copy(self, way):
        rows, width = self.src.shape[0], self.mid.shape[1]
        at = rows - width if way == 0 else 0
        other = {self.place.axis: self.place.me + 1 - 2 * way}
        return remote(
            self.src.at[pl.ds(at, width)],
            self.mid.at[way],
            self.send.at[way],
            self.recv.at[way],
            other,
        )

    def start(self):
        @pl.when(self.after)
        def _():
            self.copy(0).start()

        @pl.when(self.before)
        def _():
            self.copy(1).start()

        @pl.when(jnp.logical_not(self.before))
        def _():
            self.mid[0] = jnp.zeros(self.mid.shape[1:], self.mid.dtype)

        @pl.when(jnp.logical_not(self.after))
        def _():
            self.mid[1] = jnp.zeros(self.mid.shape[1:], self.mid.dtype)

    def arrive(self):
        @pl.when(self.before)
        def _():
            self.copy(0).wait_recv()

        @pl.when(self.after)
        def _():
            self.copy(1).wait_recv()

    def finish(self):
        @pl.when(self.after)
        def _():
            self.copy(0).wait_send()

        @pl.when(self.before)
        def _():
            self.copy(1).wait_send()


def greet_all(places, slanted):
    barrier = pltpu.get_barrier_semaphore()
    extra = jnp.int32(0)
    if slanted:
        there, device = places[0].diagonal()
        extra = jnp.where(there, jnp.int32(1), jnp.int32(0))

        @pl.when(there)
        def _():
            pl.semaphore_signal(
                barrier, inc=1, device_id=device, device_id_type=pl.DeviceIdType.MESH
            )

    for place in places:
        place.greet(barrier)
    pl.semaphore_wait(barrier, extra + sum(place.peers() for place in places))


def steps(jobs, down, skip=0, stop=None):
    length = jobs[0].place.length
    stop = length - 1 if stop is None else min(stop, length - 1)

    def each(k, carry):
        d = length - 1 - k if down else k + 1
        for job in jobs:
            job.step(d)
        return carry

    if skip < stop:
        lax.fori_loop(skip, stop, each, 0)


def exchanges(jobs, skip=0, stop=None):
    length = jobs[0].place.length
    stop = length if stop is None else stop

    def each(k, carry):
        for job in jobs:
            job.exchange(length - 1 - k)
        return carry

    lax.fori_loop(skip, stop, each, 0)


B16, F32 = jnp.bfloat16, jnp.float32
LANES = 128
TILE = 256
CHUNK = 32


class Edge(Halo):
    def copy(self, way):
        other = {self.place.axis: self.place.me + 1 - 2 * way}
        return remote(
            self.src.at[way], self.mid.at[way], self.send.at[way], self.recv.at[way], other
        )


class Plan:
    def __init__(self):
        self.names, self.shapes = [], []

    def add(self, name, *items):
        self.names += [name] * len(items)
        self.shapes += items

    def vmem(self, name, shape, dtype):
        self.add(name, pltpu.VMEM(shape, dtype))


class Refs:
    def __init__(self, names, refs):
        self.groups = {}
        for name, ref in zip(names, refs):
            self.groups.setdefault(name, []).append(ref)

    def __getattr__(self, name):
        return self.groups[name][0]

    def all(self, name):
        return self.groups[name]


def nn(left, right):
    return jnp.dot(left, right, preferred_element_type=F32)


def nt(left, right):
    return lax.dot_general(left, right, (((1,), (1,)), ((), ())), preferred_element_type=F32)


def loop(count, body):
    def each(i, carry):
        body(i)
        return carry

    lax.fori_loop(0, count, each, 0)


def span(i, width):
    return pl.ds(pl.multiple_of(i * width, width), width)


def norm_forward(values, gain):
    mean = jnp.mean(values, axis=-1, keepdims=True)
    centred = values - mean
    inverse = lax.rsqrt(jnp.mean(centred * centred, axis=-1, keepdims=True) + EPSILON)
    scaled = centred * inverse
    return (scaled, inverse, (scaled * gain).astype(B16))


def norm_backward(grad, scaled, inverse, gain):
    weighted = grad * gain
    return inverse * (
        weighted
        - jnp.mean(weighted, axis=-1, keepdims=True)
        - scaled * jnp.mean(weighted * scaled, axis=-1, keepdims=True)
    )


def gelu_parts(inner):
    cdf = 0.5 * (1.0 + lax.erf(inner * 0.7071067811865476))
    density = jnp.exp(-0.5 * inner * inner) * 0.3989422804014327
    return (inner * cdf, cdf + inner * density)


def swap(field):
    lane = lax.broadcasted_iota(jnp.int32, field.shape, 1)
    half = HEAD // 2
    return jnp.where(
        lane % HEAD < half, pltpu.roll(field, LANES - half, 1), pltpu.roll(field, half, 1)
    )


def rotate(field, cosine, sine):
    return field * cosine + swap(field) * sine


def unrotate(field, cosine, sine):
    return field * cosine - swap(field) * sine


def halves(field):
    lane = lax.broadcasted_iota(jnp.int32, field.shape, 1)
    low = lane < HEAD
    zero = jnp.zeros_like(field)
    return jnp.concatenate([jnp.where(low, field, zero), jnp.where(low, zero, field)], axis=0)


def layer_kernel(names, count, *refs):
    r = Refs(names, refs)
    seq, fsdp = Place("seq"), Place("fsdp")
    rows, width = r.tok.shape
    streams = r.tok_all.shape[0]
    group = streams * rows
    quarter = r.att.shape[1]
    pairs = quarter // LANES
    n_blocks, part = r.a_all.shape[0], r.a_all.shape[1]
    reach, outer = WIN, rows + 2 * WIN
    main = count // LANES
    tail = count - main * LANES
    flat = main * LANES
    rim_at = 2 * flat
    blocks = TILE // part
    tiles = width // TILE
    per = rows // CHUNK
    scale = HEAD**-0.5
    three = 3 * quarter
    half_streams = TILE // rows

    tokens = Gather(fsdp, r.tok, r.tok_all, r.all("tok_g"))
    cots = Gather(fsdp, r.grd, r.grd_all, r.all("grd_g"))
    halo = Halo(seq, r.tok, r.rim_mid, r.all("halo_s"))
    rim = Gather(fsdp, r.rim_mid, r.rim_all, r.all("rim_g"))
    gains = Gather(seq, r.gains, r.gains_mid, r.all("gains_g"))
    gains2 = Gather(fsdp, r.gains_mid, r.gains_all, r.all("gains2_g"))
    get_a = Gather(seq, None, r.a_all, r.all("a_g"))
    get_b1 = Gather(seq, None, r.b1_all, r.all("b1_g"))
    get_b2 = Gather(seq, None, r.b2_all, r.all("b2_g"))
    attn = Reduce(fsdp, r.src_a, r.attn_mid, r.all("attn_r"))
    attn2 = Gather(fsdp, r.attn_mid, r.attn_all, r.all("attn_g"))
    back = Reduce(fsdp, r.src_a, r.back_mid, r.all("back_r"))
    back2 = Gather(fsdp, r.back_mid, r.back_all, r.all("back_g"))
    down = Reduce(fsdp, r.src_b, r.down_sum, r.all("down_r"))
    one = Reduce(fsdp, r.src_b, r.one_sum, r.all("one_r"))
    db1 = r.big.at[0:part, 0 : rim_at + LANES]
    db2 = r.big.at[part : 2 * part, 0:flat]
    da = r.big.at[2 * part : 3 * part, 0 : three + quarter]
    put_b1 = Reduce(seq, r.gb1, db1, r.all("b1_r"))
    put_b2 = Reduce(seq, r.gb2, db2, r.all("b2_r"))
    put_a = Reduce(seq, r.ga, da, r.all("a_r"))
    put_g = Reduce(seq, r.gain_parts, r.gain_mid, r.all("gain_r"))
    put_g2 = Gather(fsdp, r.gain_mid, r.gain_got, r.all("gain_g"))
    edge = Edge(seq, r.edge_src, r.edge_mid, r.all("edge_s"))

    r.a_all[seq.me, :, :three] = r.qkv[...]
    r.a_all[seq.me, :, three:] = r.out_t[...]
    greet_all((seq, fsdp), True)
    for job in (gains, get_a, tokens, halo):
        job.start()

    def spread(x, at):
        x = x.astype(F32)
        empty = jnp.zeros((part, LANES - tail), F32)
        return pltpu.roll(jnp.concatenate([x, empty], axis=1), at * tail, 1)

    for j in range(main):
        for k in range(2):
            at = (2 * j + k) * LANES
            r.b1_all[seq.me, :, at : at + LANES] = r.in_two[k, :, j * LANES : (j + 1) * LANES]
    last = spread(r.in_two[0, :, flat:], 0) + spread(r.in_two[1, :, flat:], 1)
    last = last + spread(r.down[:, flat:], 2)
    r.b1_all[seq.me, :, rim_at:] = last.astype(B16)
    r.b2_all[seq.me] = r.down[:, :flat]

    steps([gains, get_a], False, stop=1)
    halo.arrive()
    rim.start()
    steps([tokens], False)
    place = seq.me * rows - reach + lax.broadcasted_iota(jnp.int32, (outer, LANES), 0)
    spot = lax.broadcasted_iota(jnp.int32, (outer, LANES), 1) % HEAD
    angle = place.astype(F32) * r.freq[...]
    r.cosine[...] = jnp.cos(angle)
    sine = jnp.sin(angle)
    r.sine[...] = jnp.where(spot < HEAD // 2, -sine, sine)
    steps([gains, get_a], False, skip=1, stop=2)
    for job in (get_b1, get_b2):
        job.start_lines()
    steps([rim], False)
    steps([gains, get_a], False, skip=2)
    for job in (get_b1, get_b2):
        job.start_across()
    gains.finish()
    gains2.start()
    cots.start()
    steps([gains2], False)
    gains2.finish()

    for k in range(width // LANES):
        total = jnp.zeros((r.gains.shape[0], LANES), F32)
        for s in range(k * LANES // part, (k + 1) * LANES // part):
            for f in range(streams):
                total = total + r.gains_all[f, s].astype(F32)
        r.gain[:, k * LANES : (k + 1) * LANES] = total
    tokens.finish()
    rim.finish()
    halo.finish()

    def norm_own(i):
        s, h = i // per, i % per
        x = r.tok_all[s, span(h, CHUNK), :].astype(F32)
        at = pl.ds(pl.multiple_of(reach + h * CHUNK, CHUNK), CHUNK)
        r.nx[s, at, :] = norm_forward(x, r.gain[0:1, :])[2]

    loop(streams * per, norm_own)

    rims = reach // CHUNK

    def norm_rim(i):
        s, w, h = i // (2 * rims), i // rims % 2, i % rims
        x = r.rim_all[s, w, span(h, CHUNK), :].astype(F32)
        at = pl.ds(pl.multiple_of(w * (rows + reach) + h * CHUNK, CHUNK), CHUNK)
        r.nx[s, at, :] = norm_forward(x, r.gain[0:1, :])[2]

    loop(streams * 2 * rims, norm_rim)

    def turn_one(i):
        x = r.nx[:, reach : reach + rows, span(i, LANES)].reshape(group, LANES)
        r.n1t[span(i, LANES), :] = x.T

    def turn_grad(i):
        x = r.grd_all[:, :, span(i, LANES)].reshape(group, LANES)
        r.gt[span(i, LANES), :] = x.T

    get_a.finish()

    band = jnp.abs(
        lax.broadcasted_iota(jnp.int32, (rows, outer), 0)
        + reach
        - lax.broadcasted_iota(jnp.int32, (rows, outer), 1)
    )

    def lanes(p):
        return slice(p * LANES, (p + 1) * LANES)

    def project(s):
        x = r.nx[s]
        out = nn(x, r.a_all[:, :, quarter:three].reshape(width, 2 * quarter))
        for p in range(pairs):
            keys = rotate(out[:, lanes(p)], r.cosine[...], r.sine[...])
            r.k2[s, p] = halves(keys).astype(B16)
            r.v2[s, p] = halves(out[:, lanes(pairs + p)]).astype(B16)
        out = nn(x[reach : reach + rows], r.a_all[:, :, :quarter].reshape(width, quarter))
        for p in range(pairs):
            query = rotate(
                out[:, lanes(p)], r.cosine[reach : reach + rows], r.sine[reach : reach + rows]
            )
            r.qs[s, p] = query.astype(B16)
            r.q2[s, p] = halves(query).astype(B16)

    loop(streams, project)
    steps([get_b1, get_b2], False, stop=1)

    def visible(s):
        docs = r.lengths.shape[1]
        across = seq.me * rows - reach + lax.broadcasted_iota(jnp.int32, (1, outer), 1)
        along = seq.me * rows + lax.broadcasted_iota(jnp.int32, (rows, 1), 0)
        ids_key = jnp.zeros((1, outer), jnp.int32)
        ids_query = jnp.zeros((rows, 1), jnp.int32)
        start = jnp.int32(0)
        for k in range(docs + 1):
            ids_key = ids_key + (across >= start).astype(jnp.int32)
            ids_query = ids_query + (along >= start).astype(jnp.int32)
            if k < docs:
                start = start + r.lengths[s, k]
        return (band <= reach) & (ids_query == ids_key)

    def attend(s):
        allowed = visible(s)
        for p in range(pairs):
            scores = nt(r.qs[s, p], r.k2[s, p]) * scale
            probs = []
            for h in range(2):
                masked = jnp.where(allowed, scores[:, h * outer : (h + 1) * outer], -1e30)
                top = jnp.max(masked, axis=-1, keepdims=True)
                expd = jnp.exp(masked - top)
                total = jnp.sum(expd, axis=-1, keepdims=True)
                r.lse[s, 2 * p + h] = jnp.broadcast_to(top + jnp.log(total), (rows, LANES))
                probs.append((expd / total).astype(B16))
            out = nn(jnp.concatenate(probs, axis=1), r.v2[s, p])
            r.att[span(s, rows), lanes(p)] = out.astype(B16)

    loop(streams, attend)

    def out_project(j):
        w = r.a_all[span(j, blocks), :, three:].reshape(TILE, quarter)
        out = nt(r.att[...], w).astype(B16)
        r.src_a[:, :, span(j, TILE)] = out.reshape(streams, rows, TILE)

    loop(tiles, out_project)
    exchanges([attn])
    steps([attn], True)
    steps([cots], False)
    loop(width // LANES, turn_one)
    cots.finish()
    steps([get_b1, get_b2], False, skip=1, stop=2)
    attn.last()
    attn2.start()
    loop(width // LANES, turn_grad)
    steps([attn2], False)
    attn2.finish()
    attn.finish()
    steps([get_b1, get_b2], False, skip=2)

    def norm_two(i):
        s, h = i // per, i % per
        at = span(h, CHUNK)
        x = r.tok_all[s, at, :].astype(F32) + r.attn_all[s, at, :].astype(F32)
        scaled, inverse, normed = norm_forward(x, r.gain[1:2, :])
        r.scaled[span(i, CHUNK), :] = scaled
        r.inverse[span(i, CHUNK), :] = jnp.broadcast_to(inverse, (CHUNK, LANES))
        r.nx[s, pl.ds(pl.multiple_of(rows + h * CHUNK, CHUNK), CHUNK), :] = normed

    loop(streams * per, norm_two)

    def normed_two(m):
        return r.nx[span(m, half_streams), rows : 2 * rows, :].reshape(TILE, width)

    def turn_two(i):
        x = r.nx[:, rows : 2 * rows, span(i, LANES)].reshape(group, LANES)
        r.tt[span(i, LANES), :] = x.T

    loop(width // LANES, turn_two)
    get_b1.finish()

    sides = group // TILE
    rest = flat + LANES

    def hidden(i):
        m, j = i // main, i % main
        w = r.b1_all[:, :, span(j, TILE)].reshape(width, TILE)
        out = nn(normed_two(m), w)
        inner, gate = out[:, :LANES], out[:, LANES:]
        activated, slope = gelu_parts(inner)
        at = span(m, TILE)
        r.big[at, span(j, LANES)] = activated
        r.big[at, pl.ds(pl.multiple_of(rest + j * LANES, LANES), LANES)] = gate * slope
        r.mix[at, span(j, LANES)] = (activated * gate).astype(B16)

    loop(sides * main, hidden)
    lane = lax.broadcasted_iota(jnp.int32, (TILE, LANES), 1)

    def hidden_rim(m):
        w = r.b1_all[:, :, rim_at:].reshape(width, LANES)
        inner = nn(normed_two(m), w)
        gate = pltpu.roll(inner, LANES - tail, 1)
        activated, slope = gelu_parts(inner)
        at = span(m, TILE)
        zero = jnp.zeros((TILE, LANES), F32)
        mixed = jnp.where(lane < tail, activated * gate, zero)
        r.big[at, flat:rest] = jnp.where(lane < tail, activated, zero)
        r.big[at, rest + flat :] = jnp.where(lane < tail, gate * slope, zero)
        r.mix[at, flat:] = mixed.astype(B16)
        r.mix_rim[at, :] = pltpu.roll(mixed, 2 * tail, 1).astype(B16)

    loop(sides, hidden_rim)

    def grad_down(m):
        out = nn(r.gt[span(m, TILE), :], r.mix[:, :flat]).astype(B16)
        r.gb2[span(m, blocks), :, :] = out.reshape(blocks, part, flat)

    loop(tiles, grad_down)
    get_b2.finish()
    exchanges([put_b2])

    def unpack(j):
        at = span(j, TILE)
        r.dfull[at, :flat] = r.b2_all[span(j, blocks), :, :].reshape(TILE, flat)
        x = r.b1_all[span(j, blocks), :, rim_at:].reshape(TILE, LANES).astype(F32)
        x = jnp.where(lane < tail, pltpu.roll(x, LANES - 2 * tail, 1), jnp.zeros_like(x))
        r.dfull[at, flat:] = x.astype(B16)

    loop(tiles, unpack)

    def grad_hidden(m, t, grad):
        at = span(m, TILE)
        inner = grad * r.big[at, pl.ds(pl.multiple_of(rest + t * LANES, LANES), LANES)]
        gate = grad * r.big[at, span(t, LANES)]
        return at, inner, gate

    def grad_mixed(i):
        m, t = i // main, i % main
        g = r.grd_all[span(m, half_streams)].reshape(TILE, width)
        grad = nn(g, r.dfull[:, span(t, LANES)])
        at, inner, gate = grad_hidden(m, t, grad)
        r.gh[at, span(2 * t, LANES)] = inner.astype(B16)
        r.gh[at, span(2 * t + 1, LANES)] = gate.astype(B16)

    loop(sides * main, grad_mixed)

    def grad_mixed_rim(m):
        g = r.grd_all[span(m, half_streams)].reshape(TILE, width)
        grad = nn(g, r.dfull[:, flat:])
        at, inner, gate = grad_hidden(m, main, grad)
        r.gh[at, rim_at:] = (inner + pltpu.roll(gate, tail, 1)).astype(B16)

    loop(sides, grad_mixed_rim)

    def grad_in(i):
        m, j = i // main, i % main
        out = nn(r.tt[span(m, TILE), :], r.gh[:, span(j, TILE)]).astype(B16)
        r.gb1[span(m, blocks), :, span(j, TILE)] = out.reshape(blocks, part, TILE)

    loop(tiles * main, grad_in)

    def grad_in_rim(m):
        at = span(m, TILE)
        out = nn(r.tt[at, :], r.gh[:, rim_at:]) + nn(r.gt[at, :], r.mix_rim[...])
        r.gb1[span(m, blocks), :, rim_at:] = out.astype(B16).reshape(blocks, part, LANES)

    loop(tiles, grad_in_rim)
    ends = seq.length - 1
    exchanges([put_b1], stop=ends)
    steps([put_b2], True, stop=1)
    r.gain_row[...] = jnp.zeros(r.gain_row.shape, F32)

    def back_project(j):
        w = r.b1_all[span(j, blocks)].reshape(TILE, rim_at + LANES)
        out = nt(r.gh[...], w)
        at = span(j, TILE)
        r.gain_row[1:2, at] = jnp.sum(out * r.scaled[:, at], axis=0, keepdims=True)
        r.src_a[:, :, at] = out.astype(B16).reshape(streams, rows, TILE)

    loop(tiles, back_project)
    exchanges([back])

    def down_project(j):
        out = nt(r.mix[...], r.dfull[span(j, TILE), :]).astype(B16)
        r.src_b[:, :, span(j, TILE)] = out.reshape(streams, rows, TILE)

    loop(tiles, down_project)
    exchanges([down])
    steps([back], True)
    steps([put_b2], True, skip=1, stop=2)
    back.last()
    back2.start()
    steps([put_b2], True, skip=2)
    steps([put_b1], True, stop=1)
    steps([down], True)
    steps([back2], False)
    back2.finish()
    back.finish()

    def middle_grad(i):
        s, h = i // per, i % per
        at = span(h, CHUNK)
        here = span(i, CHUNK)
        got = norm_backward(
            r.back_all[s, at, :].astype(F32),
            r.scaled[here, :],
            r.inverse[here, 0:1],
            r.gain[1:2, :],
        )
        grad = r.grd_all[s, at, :].astype(F32) + got
        r.nx[s, at, :] = grad.astype(B16)

        @pl.when(s == fsdp.me)
        def _():
            r.own_grad[at, :] = grad

    loop(streams * per, middle_grad)

    def turn_middle(i):
        x = r.nx[:, :rows, span(i, LANES)].reshape(group, LANES)
        r.tt[span(i, LANES), :] = x.T

    loop(width // LANES, turn_middle)

    def grad_attended(s):
        w = r.a_all[:, :, three:].reshape(width, quarter)
        r.gatt[span(s, TILE), :] = nn(
            r.nx[span(s, half_streams), :rows, :].reshape(TILE, width), w
        ).astype(B16)

    loop(sides, grad_attended)
    steps([put_b1], True, skip=1, stop=2)

    def attend_back(s):
        allowed = visible(s)
        at = span(s, rows)
        low = lax.broadcasted_iota(jnp.int32, (rows, LANES), 1) < HEAD
        for p in range(pairs):
            scores = nt(r.qs[s, p], r.k2[s, p]) * scale
            grad = r.gatt[at, lanes(p)]
            grad_probs = nt(grad, r.v2[s, p])
            grad_f = grad.astype(F32)
            product = grad_f * r.att[at, lanes(p)].astype(F32)
            zero = jnp.zeros_like(product)
            agains, grads = [], []
            for h in range(2):
                cut = slice(h * outer, (h + 1) * outer)
                masked = jnp.where(allowed, scores[:, cut], -1e30)
                again = jnp.exp(masked - r.lse[s, 2 * p + h][:, 0:1])
                side = jnp.where(low, product, zero) if h == 0 else jnp.where(low, zero, product)
                delta = jnp.sum(side, axis=-1, keepdims=True)
                agains.append(again.astype(B16))
                grads.append((again * (grad_probs[:, cut] - delta) * scale).astype(B16))
            grad_query = nn(jnp.concatenate(grads, axis=1), r.k2[s, p])
            grad_keys = nn(jnp.concatenate(grads, axis=0).T, r.q2[s, p])
            grad_values = nn(jnp.concatenate(agains, axis=0).T, halves(grad_f).astype(B16))
            r.gp[at, lanes(p)] = unrotate(
                grad_query, r.cosine[reach : reach + rows], r.sine[reach : reach + rows]
            ).astype(B16)
            for k, value in ((p, grad_keys), (pairs + p, grad_values)):
                r.own_kv[s, :, lanes(k)] = value[reach : reach + rows]
                r.edge_src[0, span(s, reach), lanes(k)] = value[reach + rows :].astype(B16)
                r.edge_src[1, span(s, reach), lanes(k)] = value[:reach].astype(B16)

    loop(streams, attend_back)
    edge.start()
    exchanges([put_b1], skip=ends)
    down.last()

    def grad_out(m):
        out = nn(r.tt[span(m, TILE), :], r.att[...]).astype(B16)
        r.ga[span(m, blocks), :, three:] = out.reshape(blocks, part, quarter)

    loop(tiles, grad_out)

    def norm_again(i):
        s, h = i // per, i % per
        x = r.tok_all[s, span(h, CHUNK), :].astype(F32)
        scaled, inverse, _ = norm_forward(x, r.gain[0:1, :])
        r.scaled[span(i, CHUNK), :] = scaled
        r.inverse[span(i, CHUNK), :] = jnp.broadcast_to(inverse, (CHUNK, LANES))

    loop(streams * per, norm_again)
    down.finish()
    steps([put_b1], True, skip=2)
    edge.arrive()

    def join(s):
        for k in range(2 * pairs):
            value = r.own_kv[s, :, lanes(k)]
            first = value[:reach] + r.edge_mid[0, span(s, reach), lanes(k)].astype(F32)
            final = value[rows - reach :] + r.edge_mid[1, span(s, reach), lanes(k)].astype(F32)
            middle = [value[reach : rows - reach]] if rows > 2 * reach else []
            value = jnp.concatenate([first] + middle + [final], axis=0)
            if k < pairs:
                value = unrotate(
                    value, r.cosine[reach : reach + rows], r.sine[reach : reach + rows]
                )
            r.gp[span(s, rows), lanes(pairs + k)] = value.astype(B16)

    loop(streams, join)

    def grad_qkv(i):
        m, j = i // 3, i % 3
        out = nn(r.n1t[span(m, TILE), :], r.gp[:, span(j, quarter)]).astype(B16)
        r.ga[span(m, blocks), :, span(j, quarter)] = out.reshape(blocks, part, quarter)

    loop(tiles * 3, grad_qkv)

    def one_project(j):
        w = r.a_all[span(j, blocks), :, :three].reshape(TILE, three)
        out = nt(r.gp[...], w)
        at = span(j, TILE)
        r.gain_row[0:1, at] = jnp.sum(out * r.scaled[:, at], axis=0, keepdims=True)
        r.src_b[:, :, at] = out.astype(B16).reshape(streams, rows, TILE)

    loop(tiles, one_project)
    for s in range(seq.n):
        k = s * part // LANES
        r.gain_parts[s] = r.gain_row[:, k * LANES : (k + 1) * LANES]
    exchanges([put_g])
    exchanges([one])
    exchanges([put_a])
    steps([one], True)
    steps([put_g], True)
    put_b2.last()
    put_b1.last()
    put_g.last()
    put_g2.start()
    steps([put_a], True, stop=1)
    steps([put_g2], False)
    one.last()

    def final(h):
        at = span(h, CHUNK)
        here = pl.ds(pl.multiple_of(fsdp.me * rows + h * CHUNK, CHUNK), CHUNK)
        got = norm_backward(
            r.one_sum[at, :], r.scaled[here, :], r.inverse[here, 0:1], r.gain[0:1, :]
        )
        r.dinput[at, :] = r.own_grad[at, :] + got
        middle = r.tok[at, :].astype(F32) + r.attn_all[fsdp.me, at, :].astype(F32)
        r.out[at, :] = (middle + r.down_sum[at, :]).astype(B16)

    loop(per, final)
    put_g2.finish()
    total = r.gain_got[0]
    for f in range(1, fsdp.n):
        total = total + r.gain_got[f]
    r.dgain[...] = total
    for j in range(main):
        for k in range(2):
            at = (2 * j + k) * LANES
            r.din[k, :, j * LANES : (j + 1) * LANES] = db1[:, at : at + LANES]
    rim_sum = db1[:, rim_at:]
    r.din[0, :, flat:] = rim_sum[:, :tail]
    r.din[1, :, flat:] = pltpu.roll(rim_sum, LANES - tail, 1)[:, :tail]
    r.ddown[:, :flat] = db2[...]
    r.ddown[:, flat:] = pltpu.roll(rim_sum, LANES - 2 * tail, 1)[:, :tail]
    steps([put_a], True, skip=1)
    put_a.last()
    r.dqkv[...] = da[:, :three]
    r.dout[...] = da[:, three:]
    for job in (edge, one, put_b1, put_b2, put_a, put_g):
        job.finish()


def run_layer(tok, grd, gains, qkv, out_t, in_two, down, freq, lengths):
    n, nf = lax.axis_size("seq"), lax.axis_size("fsdp")
    rows, width = tok.shape
    part, count = down.shape
    quarter = out_t.shape[1]
    wide_a, wide_2 = 4 * quarter, count // LANES * LANES
    wide_1 = 2 * wide_2 + LANES
    block_a, block_1, block_2 = (part, wide_a), (part, wide_1), (part, wide_2)
    pairs = quarter // LANES
    streams = nf
    group = streams * rows
    outer = rows + 2 * WIN
    vmem = pl.BlockSpec(memory_space=pltpu.VMEM)
    ins = [
        ("tok", tok, vmem),
        ("grd", grd, vmem),
        ("gains", gains, vmem),
        ("qkv", qkv, vmem),
        ("out_t", out_t, vmem),
        ("in_two", in_two, vmem),
        ("down", down, vmem),
        ("freq", freq, vmem),
        ("lengths", lengths, pl.BlockSpec(memory_space=pltpu.SMEM)),
    ]
    outs = [
        ("out", (rows, width), B16),
        ("dinput", (rows, width), F32),
        ("dgain", (8, LANES), F32),
        ("dqkv", (part, 3 * quarter), F32),
        ("dout", (part, quarter), F32),
        ("din", (2, part, count), F32),
        ("ddown", (part, count), F32),
    ]
    plan = Plan()
    token_block = (rows, width)
    for name, count_, shape, dtype in (
        ("tok", nf, token_block, B16),
        ("grd", nf, token_block, B16),
        ("rim", nf, (2, WIN, width), B16),
        ("a", n, block_a, B16),
        ("b1", n, block_1, B16),
        ("b2", n, block_2, B16),
        ("attn", nf, token_block, B16),
        ("back", nf, token_block, B16),
    ):
        plan.vmem(name + "_all", (count_,) + shape, dtype)
        plan.add(name + "_g", *Gather.scratch(count_))
    for name, count_, shape, dtype in (
        ("attn", nf, token_block, B16),
        ("back", nf, token_block, B16),
        ("down", nf, token_block, B16),
        ("one", nf, token_block, B16),
        ("b1", n, block_1, B16),
        ("b2", n, block_2, B16),
        ("a", n, block_a, B16),
        ("gain", n, (8, LANES), F32),
    ):
        plan.add(name + "_r", *Reduce.scratch(count_, shape, dtype))
    plan.vmem("rim_mid", (2, WIN, width), B16)
    plan.add("halo_s", *Halo.scratch())
    plan.vmem("gains_mid", (n,) + gains.shape, B16)
    plan.add("gains_g", *Gather.scratch(n))
    plan.vmem("gains_all", (nf, n) + gains.shape, B16)
    plan.add("gains2_g", *Gather.scratch(nf))
    plan.vmem("gain_mid", (8, LANES), F32)
    plan.vmem("gain_got", (nf, 8, LANES), F32)
    plan.vmem("cosine", (outer, LANES), F32)
    plan.vmem("sine", (outer, LANES), F32)
    plan.add("gain_g", *Gather.scratch(nf))
    plan.add("edge_s", *Halo.scratch())
    for name, shape, dtype in (
        ("edge_src", (2, streams * WIN, 2 * quarter), B16),
        ("edge_mid", (2, streams * WIN, 2 * quarter), B16),
        ("gain", (gains.shape[0], width), F32),
        ("gain_row", (8, width), F32),
        ("gain_parts", (n, 8, LANES), F32),
        ("nx", (streams, outer, width), B16),
        ("n1t", (width, group), B16),
        ("gt", (width, group), B16),
        ("tt", (width, group), B16),
        ("qs", (streams, pairs, rows, LANES), B16),
        ("q2", (streams, pairs, 2 * rows, LANES), B16),
        ("k2", (streams, pairs, 2 * outer, LANES), B16),
        ("v2", (streams, pairs, 2 * outer, LANES), B16),
        ("lse", (streams, 2 * pairs, rows, LANES), F32),
        ("att", (group, quarter), B16),
        ("src_a", (streams,) + token_block, B16),
        ("src_b", (streams,) + token_block, B16),
        ("attn_mid", token_block, B16),
        ("back_mid", token_block, B16),
        ("down_sum", token_block, F32),
        ("one_sum", token_block, F32),
        ("scaled", (group, width), F32),
        ("inverse", (group, LANES), F32),
        ("big", (group, 2 * (wide_2 + LANES)), F32),
        ("mix", (group, wide_2 + LANES), B16),
        ("mix_rim", (group, LANES), B16),
        ("dfull", (width, wide_2 + LANES), B16),
        ("gh", (group, wide_1), B16),
        ("gb1", (n,) + block_1, B16),
        ("gb2", (n,) + block_2, B16),
        ("ga", (n,) + block_a, B16),
        ("own_grad", token_block, F32),
        ("own_kv", (streams, rows, 2 * quarter), F32),
        ("gatt", (group, quarter), B16),
        ("gp", (group, 3 * quarter), B16),
    ):
        plan.vmem(name, shape, dtype)
    names = [i[0] for i in ins] + [o[0] for o in outs] + plan.names
    return pl.pallas_call(
        functools.partial(layer_kernel, tuple(names), count),
        out_shape=[jax.ShapeDtypeStruct(s, d) for _, s, d in outs],
        in_specs=[i[2] for i in ins],
        out_specs=[vmem] * len(outs),
        scratch_shapes=plan.shapes,
        compiler_params=pltpu.CompilerParams(
            collective_id=1, has_side_effects=True, vmem_limit_bytes=63 * 1024 * 1024
        ),
    )(*[i[1] for i in ins])


def per_device(
    layer_input,
    doc_lengths,
    attn_gain,
    qkv_weight,
    out_weight,
    mlp_gain,
    in_weight,
    down_weight,
    out_grad,
):
    quarter = qkv_weight.shape[2]
    part, piece = qkv_weight.shape[0], attn_gain.shape[0]
    device, stream = lax.axis_index("seq"), lax.axis_index("fsdp")
    gains = jnp.zeros((16, LANES), B16)
    place = (device * lax.axis_size("fsdp") + stream) * piece % LANES
    gains = lax.dynamic_update_slice(gains, jnp.stack([attn_gain, mlp_gain]), (0, place))
    half = np.arange(LANES)[None, :] % (HEAD // 2)
    freq = 10000.0 ** (-(2.0 / HEAD) * half)
    output, input_grad, dgain, dqkv, dout, din, ddown = run_layer(
        layer_input[0],
        out_grad[0],
        gains,
        qkv_weight.reshape(part, 3 * quarter),
        out_weight.T,
        in_weight.transpose(1, 0, 2),
        down_weight,
        jnp.asarray(freq, F32),
        doc_lengths,
    )
    gain = lax.dynamic_slice_in_dim(dgain, place, piece, axis=1)
    return (
        output[None],
        input_grad[None],
        gain[0],
        dqkv.reshape(part, 3, quarter),
        dout.T,
        gain[1],
        din.transpose(1, 0, 2),
        ddown,
    )


def solution(mesh):
    in_specs = (
        P("fsdp", "seq", None),
        P(),
        P(("seq", "fsdp")),
        P("seq", None, "fsdp"),
        P("fsdp", "seq"),
        P(("seq", "fsdp")),
        P("seq", None, "fsdp"),
        P("seq", "fsdp"),
        P("fsdp", "seq", None),
    )
    out_specs = (
        P("fsdp", "seq", None),
        P("fsdp", "seq", None),
        P(("seq", "fsdp")),
        P("seq", None, "fsdp"),
        P("fsdp", "seq"),
        P(("seq", "fsdp")),
        P("seq", None, "fsdp"),
        P("seq", "fsdp"),
    )
    return jax.shard_map(
        per_device, mesh=mesh, in_specs=in_specs, out_specs=out_specs, check_vma=False
    )
```

```python
import functools

import jax
import jax.numpy as jnp
import numpy as np
from jax import lax
from jax.experimental import pallas as pl
from jax.experimental.pallas import tpu as pltpu
from jax.sharding import PartitionSpec as P

HEAD = 64
WIN = 64


EPSILON = 1e-05


class Place:
    def __init__(self, axis):
        self.axis = axis
        self.n = lax.axis_size(axis)
        self.length = self.n // 2
        me = lax.axis_index(axis)
        self.me = me
        self.at = me // 2
        self.side = me % 2

    def partner(self):
        return {self.axis: self.at * 2 + (1 - self.side)}

    def right(self):
        return {self.axis: self.me + 2}

    def left(self):
        return {self.axis: self.me - 2}

    def has_right(self):
        return self.at < self.length - 1

    def has_left(self):
        return self.at > 0

    def greet(self, barrier):
        mesh = pl.DeviceIdType.MESH
        pl.semaphore_signal(barrier, inc=1, device_id=self.partner(), device_id_type=mesh)

        @pl.when(self.has_left())
        def _():
            pl.semaphore_signal(barrier, inc=1, device_id=self.left(), device_id_type=mesh)

        @pl.when(self.has_right())
        def _():
            pl.semaphore_signal(barrier, inc=1, device_id=self.right(), device_id_type=mesh)

    def diagonal(self):
        there = jnp.where(self.side == 1, self.has_right(), self.has_left())
        return there, {self.axis: self.me + 2 * self.side - 1}

    def peers(self):
        one, none = jnp.int32(1), jnp.int32(0)
        return 1 + jnp.where(self.has_left(), one, none) + jnp.where(self.has_right(), one, none)


def when(condition, action):
    if condition is True:
        action()
    else:
        pl.when(condition)(action)


def remote(src, dst, send, recv, device):
    return pltpu.make_async_remote_copy(
        src_ref=src,
        dst_ref=dst,
        send_sem=send,
        recv_sem=recv,
        device_id=device,
        device_id_type=pl.DeviceIdType.MESH,
    )


class Gather:
    scratch = staticmethod(
        lambda n: [
            pltpu.SemaphoreType.DMA((3, n)),
            pltpu.SemaphoreType.DMA((n,)),
            pltpu.SemaphoreType.DMA,
        ]
    )

    def __init__(self, place, src, dst, sems, relayed=False):
        self.place, self.src, self.dst = place, src, dst
        self.send, self.recv, self.local = sems
        self.relayed = relayed

    def crosses(self, i):
        if not self.relayed:
            return True
        inner = jnp.logical_and(i > 0, i < self.place.length - 1)
        return jnp.logical_or(inner, i == self.place.at)

    def relay(self, d):
        place = self.place
        ends = ((d, 0, 1), (place.length - 1 - d, place.length - 1, 2))
        for at, end, way in ends:
            block = 2 * end + 1 - place.side

            @pl.when(place.at == at)
            def _(block=block, way=way):
                self.copy(0, block, place.partner()).wait_recv()
                (self.ahead if way == 1 else self.behind)(block, False, lambda c: c.start())

    def copy(self, way, block, device, own=False):
        src = self.src if own else self.dst.at[block]
        return remote(src, self.dst.at[block], self.send.at[way, block], self.recv.at[block], device)

    def onward(self, block, own, act):
        place = self.place
        act(self.copy(0, block, place.partner(), own))

    def start(self):
        place = self.place
        if self.src is not None:
            pltpu.make_async_copy(self.src, self.dst.at[place.me], self.local).start()
        self.start_lines()
        self.start_across()

    def start_lines(self):
        place = self.place
        self.ahead(place.me, self.src is not None, lambda c: c.start())
        self.behind(place.me, self.src is not None, lambda c: c.start())

    def start_across(self):
        self.onward(self.place.me, self.src is not None, lambda c: c.start())

    def ahead(self, block, own, act):
        place = self.place

        @pl.when(place.has_right())
        def _():
            act(self.copy(1, block, place.right(), own))

    def behind(self, block, own, act):
        place = self.place

        @pl.when(place.has_left())
        def _():
            act(self.copy(2, block, place.left(), own))

    def step(self, d):
        place = self.place

        @pl.when(place.at - d >= 0)
        def _():
            block = place.me - 2 * d
            self.copy(1, block, place.partner()).wait_recv()
            self.ahead(block, False, lambda c: c.start())
            when(
                self.crosses(place.at - d),
                lambda: self.onward(block, False, lambda c: c.start()),
            )

        @pl.when(place.at + d < place.length)
        def _():
            block = place.me + 2 * d
            self.copy(2, block, place.partner()).wait_recv()
            self.behind(block, False, lambda c: c.start())
            when(
                self.crosses(place.at + d),
                lambda: self.onward(block, False, lambda c: c.start()),
            )

    def finish(self):
        place = self.place
        if self.src is not None:
            pltpu.make_async_copy(self.src, self.dst.at[place.me], self.local).wait()

        def arrived(i, carry):
            inner = True
            if self.relayed:
                inner = jnp.logical_and(i > 0, i < place.length - 1)
            when(
                inner,
                lambda: self.copy(0, 2 * i + 1 - place.side, place.partner()).wait_recv(),
            )
            when(
                self.crosses(i),
                lambda: self.onward(2 * i + place.side, False, lambda c: c.wait_send()),
            )

            @pl.when(i <= place.at)
            def _():
                self.ahead(2 * i + place.side, False, lambda c: c.wait_send())

            @pl.when(i >= place.at)
            def _():
                self.behind(2 * i + place.side, False, lambda c: c.wait_send())

            return carry

        lax.fori_loop(0, place.length, arrived, 0)
        if self.relayed:
            self.ahead(1 - place.side, False, lambda c: c.wait_send())
            self.behind(2 * place.length - 1 - place.side, False, lambda c: c.wait_send())


class Reduce:
    @staticmethod
    def scratch(n, block, dtype):
        length = n // 2
        return [
            pltpu.VMEM((length,) + block, dtype),
            pltpu.VMEM((length + 1,) + block, dtype),
            pltpu.SemaphoreType.DMA((2, length)),
            pltpu.SemaphoreType.DMA((length,)),
            pltpu.SemaphoreType.DMA((length + 1,)),
        ]

    @staticmethod
    def relay_scratch(block, dtype):
        return [
            pltpu.VMEM((2,) + block, dtype),
            pltpu.SemaphoreType.DMA((2,)),
            pltpu.SemaphoreType.DMA((2,)),
        ]

    def __init__(self, place, src, dst, scratch, relays=None):
        self.place, self.src, self.dst = place, src, dst
        self.paired, self.lined, self.send, self.pair_recv, self.line_recv = scratch
        self.relays = relays

    def crosses(self, i):
        if self.relays is None:
            return True
        return jnp.logical_and(i > 0, i < self.place.length - 1)

    def pass_on(self, end, device):
        held, send, recv = self.relays
        block = 2 * (end * (self.place.length - 1)) + 1 - self.place.side
        return self.src.at[block], remote(
            self.src.at[block], held.at[end], send.at[end], recv.at[end], device
        )

    def relay(self, d):
        place = self.place
        finish = place.length - 1
        for end, at in ((0, finish - d), (1, d)):
            device = place.right() if end else place.left()
            final = finish if end else 0

            @pl.when(place.at == at)
            def _(end=end, device=device, final=final):
                block, copy = self.pass_on(end, device)

                @pl.when(d > 0)
                def _():
                    copy.wait_recv()
                    self.add(block, [block, self.relays[0].at[end]])

                @pl.when(place.at != final)
                def _():
                    copy.start()

                @pl.when(place.at == final)
                def _():
                    self.across(final).start()

    def mine(self, i):
        return self.src.at[2 * i + self.place.side]

    def across(self, i):
        place = self.place
        return remote(
            self.src.at[2 * i + 1 - place.side],
            self.paired.at[i],
            self.send.at[0, i],
            self.pair_recv.at[i],
            place.partner(),
        )

    def along(self, i, slot, device):
        return remote(
            self.mine(i), self.lined.at[slot], self.send.at[1, i], self.line_recv.at[slot], device
        )

    def exchange(self, d):
        place = self.place

        @pl.when(place.at + d < place.length)
        def _():
            when(self.crosses(place.at + d), lambda: self.across(place.at + d).start())

        @pl.when(jnp.logical_and(d > 0, place.at - d >= 0))
        def _():
            when(self.crosses(place.at - d), lambda: self.across(place.at - d).start())

    def add(self, out, refs):
        rows = out.shape[0]
        tile = 16 if rows % 16 == 0 else 8

        def each(i, carry):
            at = pl.ds(pl.multiple_of(i * tile, tile), tile)
            total = refs[0][at, :].astype(jnp.float32)
            for ref in refs[1:]:
                total = total + ref[at, :].astype(jnp.float32)
            out[at, :] = total.astype(out.dtype)
            return carry

        lax.fori_loop(0, rows // tile, each, 0)

    def own(self, i):
        self.across(i).wait_recv()
        return [self.mine(i), self.paired.at[i]]

    def combine(self, i, paired, lined):
        def total(pair):
            refs = self.own(i) if pair else [self.mine(i)]

            @pl.when(lined)
            def _():
                self.along(i, i, self.place.partner()).wait_recv()
                self.add(self.mine(i), refs + [self.lined.at[i]])

            if pair:

                @pl.when(jnp.logical_not(lined))
                def _():
                    self.add(self.mine(i), refs)

        when(paired, lambda: total(True))
        if paired is not True:
            pl.when(jnp.logical_not(paired))(lambda: total(False))

    def step(self, d):
        place = self.place

        @pl.when(place.at + d < place.length)
        def _():
            i = place.at + d
            self.combine(i, self.crosses(i), place.has_left())
            self.along(i, i, place.right()).start()

        @pl.when(place.at - d >= 0)
        def _():
            i = place.at - d
            self.combine(i, self.crosses(i), place.has_right())
            slot = jnp.where(d == 1, place.length, i)
            self.along(i, slot, place.left()).start()

    def last(self):
        place = self.place
        i, extra = place.at, place.length
        refs = self.own(i)

        @pl.when(place.has_left())
        def _():
            self.along(i, i, place.partner()).wait_recv()

        @pl.when(place.has_right())
        def _():
            self.along(i, extra, place.partner()).wait_recv()

        both = jnp.logical_and(place.has_left(), place.has_right())

        @pl.when(both)
        def _():
            self.add(self.dst, refs + [self.lined.at[i], self.lined.at[extra]])

        @pl.when(jnp.logical_and(place.has_left(), jnp.logical_not(both)))
        def _():
            self.add(self.dst, refs + [self.lined.at[i]])

        @pl.when(jnp.logical_and(place.has_right(), jnp.logical_not(both)))
        def _():
            self.add(self.dst, refs + [self.lined.at[extra]])

    def finish(self):
        place = self.place

        def each(i, carry):
            crosses = self.crosses(i)
            if crosses is not True:
                crosses = jnp.logical_or(crosses, i == place.at)
            when(crosses, lambda: self.across(i).wait_send())

            @pl.when(i != place.at)
            def _():
                self.along(i, i, place.partner()).wait_send()

            return carry

        lax.fori_loop(0, place.length, each, 0)
        if self.relays is not None:

            @pl.when(place.has_left())
            def _():
                self.pass_on(0, place.left())[1].wait_send()

            @pl.when(place.has_right())
            def _():
                self.pass_on(1, place.right())[1].wait_send()


class Halo:
    scratch = staticmethod(lambda: [pltpu.SemaphoreType.DMA((2,)), pltpu.SemaphoreType.DMA((2,))])

    def __init__(self, place, src, mid, sems):
        self.place, self.src, self.mid = place, src, mid
        self.send, self.recv = sems
        self.after = place.me < place.n - 1
        self.before = place.me > 0

    def copy(self, way):
        rows, width = self.src.shape[0], self.mid.shape[1]
        at = rows - width if way == 0 else 0
        other = {self.place.axis: self.place.me + 1 - 2 * way}
        return remote(
            self.src.at[pl.ds(at, width)],
            self.mid.at[way],
            self.send.at[way],
            self.recv.at[way],
            other,
        )

    def start(self):
        @pl.when(self.after)
        def _():
            self.copy(0).start()

        @pl.when(self.before)
        def _():
            self.copy(1).start()

        @pl.when(jnp.logical_not(self.before))
        def _():
            self.mid[0] = jnp.zeros(self.mid.shape[1:], self.mid.dtype)

        @pl.when(jnp.logical_not(self.after))
        def _():
            self.mid[1] = jnp.zeros(self.mid.shape[1:], self.mid.dtype)

    def arrive(self):
        @pl.when(self.before)
        def _():
            self.copy(0).wait_recv()

        @pl.when(self.after)
        def _():
            self.copy(1).wait_recv()

    def finish(self):
        @pl.when(self.after)
        def _():
            self.copy(0).wait_send()

        @pl.when(self.before)
        def _():
            self.copy(1).wait_send()


def greet_all(places, slanted):
    barrier = pltpu.get_barrier_semaphore()
    extra = jnp.int32(0)
    if slanted:
        there, device = places[0].diagonal()
        extra = jnp.where(there, jnp.int32(1), jnp.int32(0))

        @pl.when(there)
        def _():
            pl.semaphore_signal(
                barrier, inc=1, device_id=device, device_id_type=pl.DeviceIdType.MESH
            )

    for place in places:
        place.greet(barrier)
    pl.semaphore_wait(barrier, extra + sum(place.peers() for place in places))


def steps(jobs, down, skip=0, stop=None):
    length = jobs[0].place.length
    stop = length - 1 if stop is None else min(stop, length - 1)

    def each(k, carry):
        d = length - 1 - k if down else k + 1
        for job in jobs:
            job.step(d)
        return carry

    if skip < stop:
        lax.fori_loop(skip, stop, each, 0)


def relays(job, skip=0, stop=None):
    length = job.place.length
    stop = length if stop is None else stop

    def each(k, carry):
        job.relay(k)
        return carry

    lax.fori_loop(skip, stop, each, 0)


def exchanges(jobs, skip=0, stop=None):
    length = jobs[0].place.length
    stop = length if stop is None else stop

    def each(k, carry):
        for job in jobs:
            job.exchange(length - 1 - k)
        return carry

    lax.fori_loop(skip, stop, each, 0)


B16, F32 = jnp.bfloat16, jnp.float32
LANES = 128
TILE = 256
CHUNK = 32
UNROLL = 4


class Edge(Halo):
    def copy(self, way):
        other = {self.place.axis: self.place.me + 1 - 2 * way}
        return remote(
            self.src.at[way], self.mid.at[way], self.send.at[way], self.recv.at[way], other
        )


class Plan:
    def __init__(self):
        self.names, self.shapes = [], []

    def add(self, name, *items):
        self.names += [name] * len(items)
        self.shapes += items

    def vmem(self, name, shape, dtype):
        self.add(name, pltpu.VMEM(shape, dtype))


class Refs:
    def __init__(self, names, refs):
        self.groups = {}
        for name, ref in zip(names, refs):
            self.groups.setdefault(name, []).append(ref)

    def __getattr__(self, name):
        return self.groups[name][0]

    def all(self, name):
        return self.groups[name]


def nn(left, right):
    return jnp.dot(left, right, preferred_element_type=F32)


def nt(left, right):
    return lax.dot_general(left, right, (((1,), (1,)), ((), ())), preferred_element_type=F32)


def loop(count, body, unroll=1):
    def each(i, carry):
        for k in range(unroll):
            body(i * unroll + k)
        return carry

    lax.fori_loop(0, count // unroll, each, 0)


def span(i, width):
    return pl.ds(pl.multiple_of(i * width, width), width)


def norm_forward(values, gain):
    mean = jnp.mean(values, axis=-1, keepdims=True)
    centred = values - mean
    inverse = lax.rsqrt(jnp.mean(centred * centred, axis=-1, keepdims=True) + EPSILON)
    scaled = centred * inverse
    return (scaled, inverse, (scaled * gain).astype(B16))


def norm_backward(grad, scaled, inverse, gain):
    weighted = grad * gain
    return inverse * (
        weighted
        - jnp.mean(weighted, axis=-1, keepdims=True)
        - scaled * jnp.mean(weighted * scaled, axis=-1, keepdims=True)
    )


def gelu_parts(inner):
    cdf = 0.5 * (1.0 + lax.erf(inner * 0.7071067811865476))
    density = jnp.exp(-0.5 * inner * inner) * 0.3989422804014327
    return (inner * cdf, cdf + inner * density)


def swap(field):
    lane = lax.broadcasted_iota(jnp.int32, field.shape, 1)
    half = HEAD // 2
    return jnp.where(
        lane % HEAD < half, pltpu.roll(field, LANES - half, 1), pltpu.roll(field, half, 1)
    )


def rotate(field, cosine, sine):
    return field * cosine + swap(field) * sine


def unrotate(field, cosine, sine):
    return field * cosine - swap(field) * sine


def halves(field):
    lane = lax.broadcasted_iota(jnp.int32, field.shape, 1)
    low = lane < HEAD
    zero = jnp.zeros_like(field)
    return jnp.concatenate([jnp.where(low, field, zero), jnp.where(low, zero, field)], axis=0)


def layer_kernel(names, *refs):
    r = Refs(names, refs)
    seq, fsdp = Place("seq"), Place("fsdp")
    rows, width = r.tok.shape
    count = r.down_t.shape[0]
    streams = r.tok_all.shape[0]
    group = streams * rows
    quarter = r.att.shape[1]
    pairs = quarter // LANES
    part = r.a_all.shape[1]
    reach, outer = WIN, rows + 2 * WIN
    main = count // LANES
    tail = count - main * LANES
    flat = main * LANES
    rim_at = 2 * flat
    blocks = TILE // part
    tiles = width // TILE
    per = rows // CHUNK
    scale = HEAD**-0.5
    three = 3 * quarter
    half_streams = TILE // rows

    tokens = Gather(fsdp, r.tok, r.tok_all, r.all("tok_g"))
    cots = Gather(fsdp, r.grd, r.grd_all, r.all("grd_g"))
    halo = Halo(seq, r.tok, r.rim_mid, r.all("halo_s"))
    rim = Gather(fsdp, r.rim_mid, r.rim_all, r.all("rim_g"))
    gains = Gather(seq, r.gains, r.gains_mid, r.all("gains_g"))
    gains2 = Gather(fsdp, r.gains_mid, r.gains_all, r.all("gains2_g"))
    get_a = Gather(seq, None, r.a_all, r.all("a_g"), True)
    get_b1 = Gather(seq, None, r.b1_all, r.all("b1_g"))
    get_b2 = Gather(seq, None, r.b2_all, r.all("b2_g"))
    attn = Reduce(fsdp, r.src_a, r.attn_mid, r.all("attn_r"))
    attn2 = Gather(fsdp, r.attn_mid, r.attn_all, r.all("attn_g"))
    back = Reduce(fsdp, r.src_a, r.back_mid, r.all("back_r"))
    back2 = Gather(fsdp, r.back_mid, r.back_all, r.all("back_g"))
    down = Reduce(fsdp, r.src_b, r.down_sum, r.all("down_r"))
    one = Reduce(fsdp, r.src_b, r.one_sum, r.all("one_r"))
    db1 = r.big.at[0:part, 0 : rim_at + LANES]
    db2 = r.big.at[part : 2 * part, 0:flat]
    da = r.big.at[2 * part : 3 * part, 0 : 2 * quarter]
    dc = r.big.at[2 * part : 3 * part, 2 * quarter : 4 * quarter]
    put_b1 = Reduce(seq, r.gb1, db1, r.all("b1_r"))
    put_b2 = Reduce(seq, r.gb2, db2, r.all("b2_r"))
    put_a = Reduce(seq, r.ga, da, r.all("a_r"))
    put_c = Reduce(seq, r.gc, dc, r.all("c_r"))
    put_g = Reduce(seq, r.gain_parts, r.gain_mid, r.all("gain_r"))
    put_g2 = Gather(fsdp, r.gain_mid, r.gain_got, r.all("gain_g"))
    edge = Edge(seq, r.edge_src, r.edge_mid, r.all("edge_s"))

    piece = r.gain_in.shape[1]
    shift = (seq.me * fsdp.n + fsdp.me) * piece % LANES
    filled = [jnp.zeros((8, LANES - piece), F32)] if piece < LANES else []
    wide = jnp.concatenate([r.gain_in[...].astype(F32)] + filled, axis=1)
    wide = jnp.concatenate([pltpu.roll(wide, shift, 1), jnp.zeros((8, LANES), F32)], axis=0)
    r.gains[...] = wide.astype(B16)
    for k in range(3):
        r.a_all[seq.me, :, k * quarter : (k + 1) * quarter] = r.qkv[k]
    for k in range(pairs):
        at = three + k * LANES
        r.a_all[seq.me, :, at : at + LANES] = r.out_w[k * LANES : (k + 1) * LANES, :].T
    greet_all((seq, fsdp), True)
    for job in (gains, get_a, tokens, halo):
        job.start()

    for j in range(main):
        cut = slice(j * LANES, (j + 1) * LANES)
        for k in range(2):
            at = (2 * j + k) * LANES
            r.b1_all[seq.me, :, at : at + LANES] = r.in_two[k, cut, :].T
        r.b2_all[seq.me, :, cut] = r.down_t[cut, :].T
    last = [r.in_two[0, flat:, :], r.in_two[1, flat:, :], r.down_t[flat:, :]]
    last.append(jnp.zeros((LANES - 3 * tail, part), B16))
    r.b1_all[seq.me, :, rim_at:] = jnp.concatenate(last, axis=0).T

    steps([gains, get_a], False, stop=1)
    relays(get_a, stop=1)
    halo.arrive()
    rim.start()
    steps([tokens], False)
    place = seq.me * rows - reach + lax.broadcasted_iota(jnp.int32, (outer, LANES), 0)
    spot = lax.broadcasted_iota(jnp.int32, (outer, LANES), 1) % HEAD
    angle = place.astype(F32) * r.freq[...]
    r.cosine[...] = jnp.cos(angle)
    sine = jnp.sin(angle)
    r.sine[...] = jnp.where(spot < HEAD // 2, -sine, sine)
    steps([gains, get_a], False, skip=1, stop=2)
    relays(get_a, skip=1, stop=2)
    steps([rim], False)
    steps([gains, get_a], False, skip=2)
    relays(get_a, skip=2, stop=3)
    get_b1.start_lines()
    get_b1.start_across()
    gains.finish()
    gains2.start()
    cots.start()
    steps([gains2], False)
    gains2.finish()

    for k in range(width // LANES):
        total = jnp.zeros((r.gains.shape[0], LANES), F32)
        for s in range(k * LANES // part, (k + 1) * LANES // part):
            for f in range(streams):
                total = total + r.gains_all[f, s].astype(F32)
        r.gain[:, k * LANES : (k + 1) * LANES] = total
    tokens.finish()
    rim.finish()
    halo.finish()

    def norm_own(i):
        s, h = i // per, i % per
        x = r.tok_all[s, span(h, CHUNK), :].astype(F32)
        at = pl.ds(pl.multiple_of(reach + h * CHUNK, CHUNK), CHUNK)
        r.nx[s, at, :] = norm_forward(x, r.gain[0:1, :])[2]

    loop(streams * per, norm_own, UNROLL)

    rims = reach // CHUNK

    def norm_rim(i):
        s, w, h = i // (2 * rims), i // rims % 2, i % rims
        x = r.rim_all[s, w, span(h, CHUNK), :].astype(F32)
        at = pl.ds(pl.multiple_of(w * (rows + reach) + h * CHUNK, CHUNK), CHUNK)
        r.nx[s, at, :] = norm_forward(x, r.gain[0:1, :])[2]

    loop(streams * 2 * rims, norm_rim, UNROLL)

    def turn_one(i):
        x = r.nx[:, reach : reach + rows, span(i, LANES)].reshape(group, LANES)
        r.n1t[span(i, LANES), :] = x.T

    def turn_grad(i):
        x = r.grd_all[:, :, span(i, LANES)].reshape(group, LANES)
        r.gt[span(i, LANES), :] = x.T

    relays(get_a, skip=3)
    get_a.finish()

    band = jnp.abs(
        lax.broadcasted_iota(jnp.int32, (rows, outer), 0)
        + reach
        - lax.broadcasted_iota(jnp.int32, (rows, outer), 1)
    )

    def lanes(p):
        return slice(p * LANES, (p + 1) * LANES)

    def project(s):
        x = r.nx[s]
        out = nn(x, r.a_all[:, :, quarter:three].reshape(width, 2 * quarter))
        for p in range(pairs):
            keys = rotate(out[:, lanes(p)], r.cosine[...], r.sine[...])
            r.k2[s, p] = halves(keys).astype(B16)
            r.v2[s, p] = halves(out[:, lanes(pairs + p)]).astype(B16)
        out = nn(x[reach : reach + rows], r.a_all[:, :, :quarter].reshape(width, quarter))
        for p in range(pairs):
            query = rotate(
                out[:, lanes(p)], r.cosine[reach : reach + rows], r.sine[reach : reach + rows]
            )
            r.qs[s, p] = query.astype(B16)
            r.q2[s, p] = halves(query).astype(B16)

    loop(streams // 2, project)
    steps([get_b1], False, stop=1)
    loop(streams - streams // 2, lambda i: project(i + streams // 2))

    def visible(s):
        docs = r.lengths.shape[1]
        across = seq.me * rows - reach + lax.broadcasted_iota(jnp.int32, (1, outer), 1)
        along = seq.me * rows + lax.broadcasted_iota(jnp.int32, (rows, 1), 0)
        ids_key = jnp.zeros((1, outer), jnp.int32)
        ids_query = jnp.zeros((rows, 1), jnp.int32)
        start = jnp.int32(0)
        for k in range(docs + 1):
            ids_key = ids_key + (across >= start).astype(jnp.int32)
            ids_query = ids_query + (along >= start).astype(jnp.int32)
            if k < docs:
                start = start + r.lengths[s, k]
        return (band <= reach) & (ids_query == ids_key)

    def attend(s):
        allowed = visible(s)
        for p in range(pairs):
            scores = nt(r.qs[s, p], r.k2[s, p]) * scale
            probs = []
            for h in range(2):
                masked = jnp.where(allowed, scores[:, h * outer : (h + 1) * outer], -1e30)
                top = jnp.max(masked, axis=-1, keepdims=True)
                expd = jnp.exp(masked - top)
                total = jnp.sum(expd, axis=-1, keepdims=True)
                r.lse[s, 2 * p + h] = jnp.broadcast_to(top + jnp.log(total), (rows, LANES))
                probs.append((expd / total).astype(B16))
            out = nn(jnp.concatenate(probs, axis=1), r.v2[s, p])
            r.att[span(s, rows), lanes(p)] = out.astype(B16)

    loop(streams, attend)
    steps([get_b1], False, skip=1, stop=2)
    get_b2.start_lines()

    def out_project(j):
        w = r.a_all[span(j, blocks), :, three:].reshape(TILE, quarter)
        out = nt(r.att[...], w).astype(B16)
        r.src_a[:, :, span(j, TILE)] = out.reshape(streams, rows, TILE)

    loop(tiles, out_project)
    exchanges([attn])
    steps([attn], True)
    steps([cots], False)
    loop(width // LANES, turn_one)
    cots.finish()
    steps([get_b1], False, skip=2)
    get_b2.start_across()
    attn.last()
    attn2.start()
    loop(width // LANES, turn_grad)
    steps([get_b2], False, stop=1)
    steps([attn2], False)
    steps([get_b2], False, skip=1, stop=2)
    attn2.finish()
    attn.finish()
    steps([get_b2], False, skip=2)

    def norm_two(i):
        s, h = i // per, i % per
        at = span(h, CHUNK)
        x = r.tok_all[s, at, :].astype(F32) + r.attn_all[s, at, :].astype(F32)
        scaled, inverse, normed = norm_forward(x, r.gain[1:2, :])
        r.scaled[span(i, CHUNK), :] = scaled
        r.inverse[span(i, CHUNK), :] = jnp.broadcast_to(inverse, (CHUNK, LANES))
        r.nx[s, pl.ds(pl.multiple_of(rows + h * CHUNK, CHUNK), CHUNK), :] = normed

    loop(streams * per, norm_two, UNROLL)

    def normed_two(m):
        return r.nx[span(m, half_streams), rows : 2 * rows, :].reshape(TILE, width)

    def turn_two(i):
        x = r.nx[:, rows : 2 * rows, span(i, LANES)].reshape(group, LANES)
        r.tt[span(i, LANES), :] = x.T

    loop(width // LANES, turn_two)
    get_b1.finish()

    sides = group // TILE
    rest = flat + LANES

    def hidden(i):
        m, j = i // main, i % main
        w = r.b1_all[:, :, span(j, TILE)].reshape(width, TILE)
        out = nn(normed_two(m), w)
        inner, gate = out[:, :LANES], out[:, LANES:]
        activated, slope = gelu_parts(inner)
        at = span(m, TILE)
        r.big[at, span(j, LANES)] = activated
        r.big[at, pl.ds(pl.multiple_of(rest + j * LANES, LANES), LANES)] = gate * slope
        r.mix[at, span(j, LANES)] = (activated * gate).astype(B16)

    loop(sides * main, hidden)
    lane = lax.broadcasted_iota(jnp.int32, (TILE, LANES), 1)

    def hidden_rim(m):
        w = r.b1_all[:, :, rim_at:].reshape(width, LANES)
        inner = nn(normed_two(m), w)
        gate = pltpu.roll(inner, LANES - tail, 1)
        activated, slope = gelu_parts(inner)
        at = span(m, TILE)
        zero = jnp.zeros((TILE, LANES), F32)
        mixed = jnp.where(lane < tail, activated * gate, zero)
        r.big[at, flat:rest] = jnp.where(lane < tail, activated, zero)
        r.big[at, rest + flat :] = jnp.where(lane < tail, gate * slope, zero)
        r.mix[at, flat:] = mixed.astype(B16)
        r.mix_rim[at, :] = pltpu.roll(mixed, 2 * tail, 1).astype(B16)

    loop(sides, hidden_rim)

    def grad_down(m):
        out = nn(r.gt[span(m, TILE), :], r.mix[:, :flat]).astype(B16)
        r.gb2[span(m, blocks), :, :] = out.reshape(blocks, part, flat)

    loop(tiles, grad_down)
    get_b2.finish()
    exchanges([put_b2])

    def unpack(j):
        at = span(j, TILE)
        r.dfull[at, :flat] = r.b2_all[span(j, blocks), :, :].reshape(TILE, flat)
        x = r.b1_all[span(j, blocks), :, rim_at:].reshape(TILE, LANES).astype(F32)
        x = jnp.where(lane < tail, pltpu.roll(x, LANES - 2 * tail, 1), jnp.zeros_like(x))
        r.dfull[at, flat:] = x.astype(B16)

    loop(tiles, unpack)

    def grad_hidden(m, t, grad):
        at = span(m, TILE)
        inner = grad * r.big[at, pl.ds(pl.multiple_of(rest + t * LANES, LANES), LANES)]
        gate = grad * r.big[at, span(t, LANES)]
        return at, inner, gate

    def grad_mixed(i):
        m, t = i // main, i % main
        g = r.grd_all[span(m, half_streams)].reshape(TILE, width)
        grad = nn(g, r.dfull[:, span(t, LANES)])
        at, inner, gate = grad_hidden(m, t, grad)
        r.gh[at, span(2 * t, LANES)] = inner.astype(B16)
        r.gh[at, span(2 * t + 1, LANES)] = gate.astype(B16)

    loop(sides * main, grad_mixed)

    def grad_mixed_rim(m):
        g = r.grd_all[span(m, half_streams)].reshape(TILE, width)
        grad = nn(g, r.dfull[:, flat:])
        at, inner, gate = grad_hidden(m, main, grad)
        r.gh[at, rim_at:] = (inner + pltpu.roll(gate, tail, 1)).astype(B16)

    loop(sides, grad_mixed_rim)
    steps([put_b2], True, stop=1)

    r.gain_row[...] = jnp.zeros(r.gain_row.shape, F32)

    def back_project(j):
        w = r.b1_all[span(j, blocks)].reshape(TILE, rim_at + LANES)
        out = nt(r.gh[...], w)
        at = span(j, TILE)
        r.gain_row[1:2, at] = jnp.sum(out * r.scaled[:, at], axis=0, keepdims=True)
        r.src_a[:, :, at] = out.astype(B16).reshape(streams, rows, TILE)

    loop(tiles, back_project)
    exchanges([back])

    def grad_in(i):
        m, j = i // main, i % main
        out = nn(r.tt[span(m, TILE), :], r.gh[:, span(j, TILE)]).astype(B16)
        r.gb1[span(m, blocks), :, span(j, TILE)] = out.reshape(blocks, part, TILE)

    loop(tiles * main, grad_in)

    def grad_in_rim(m):
        at = span(m, TILE)
        out = nn(r.tt[at, :], r.gh[:, rim_at:]) + nn(r.gt[at, :], r.mix_rim[...])
        r.gb1[span(m, blocks), :, rim_at:] = out.astype(B16).reshape(blocks, part, LANES)

    loop(tiles, grad_in_rim)
    ends = seq.length - 1
    exchanges([put_b1], stop=ends)
    def down_project(j):
        out = nt(r.mix[...], r.dfull[span(j, TILE), :]).astype(B16)
        r.src_b[:, :, span(j, TILE)] = out.reshape(streams, rows, TILE)

    loop(tiles, down_project)
    exchanges([down])
    steps([back], True)
    steps([put_b2], True, skip=1, stop=2)
    back.last()
    back2.start()
    steps([put_b2], True, skip=2)
    steps([put_b1], True, stop=1)
    steps([down], True)
    steps([back2], False)
    back2.finish()
    back.finish()

    def middle_grad(i):
        s, h = i // per, i % per
        at = span(h, CHUNK)
        here = span(i, CHUNK)
        got = norm_backward(
            r.back_all[s, at, :].astype(F32),
            r.scaled[here, :],
            r.inverse[here, 0:1],
            r.gain[1:2, :],
        )
        grad = r.grd_all[s, at, :].astype(F32) + got
        r.nx[s, at, :] = grad.astype(B16)

        @pl.when(s == fsdp.me)
        def _():
            r.own_grad[at, :] = grad

    loop(streams * per, middle_grad, UNROLL)

    def turn_middle(i):
        x = r.nx[:, :rows, span(i, LANES)].reshape(group, LANES)
        r.tt[span(i, LANES), :] = x.T

    loop(width // LANES, turn_middle)

    def grad_attended(s):
        w = r.a_all[:, :, three:].reshape(width, quarter)
        r.gatt[span(s, TILE), :] = nn(
            r.nx[span(s, half_streams), :rows, :].reshape(TILE, width), w
        ).astype(B16)

    loop(sides, grad_attended)
    steps([put_b1], True, skip=1, stop=2)

    def attend_back(s):
        allowed = visible(s)
        at = span(s, rows)
        low = lax.broadcasted_iota(jnp.int32, (rows, LANES), 1) < HEAD
        for p in range(pairs):
            scores = nt(r.qs[s, p], r.k2[s, p]) * scale
            grad = r.gatt[at, lanes(p)]
            grad_probs = nt(grad, r.v2[s, p])
            grad_f = grad.astype(F32)
            product = grad_f * r.att[at, lanes(p)].astype(F32)
            zero = jnp.zeros_like(product)
            agains, grads = [], []
            for h in range(2):
                cut = slice(h * outer, (h + 1) * outer)
                masked = jnp.where(allowed, scores[:, cut], -1e30)
                again = jnp.exp(masked - r.lse[s, 2 * p + h][:, 0:1])
                side = jnp.where(low, product, zero) if h == 0 else jnp.where(low, zero, product)
                delta = jnp.sum(side, axis=-1, keepdims=True)
                agains.append(again.astype(B16))
                grads.append((again * (grad_probs[:, cut] - delta) * scale).astype(B16))
            grad_query = nn(jnp.concatenate(grads, axis=1), r.k2[s, p])
            grad_keys = nn(jnp.concatenate(grads, axis=0).T, r.q2[s, p])
            grad_values = nn(jnp.concatenate(agains, axis=0).T, halves(grad_f).astype(B16))
            r.gp[at, lanes(p)] = unrotate(
                grad_query, r.cosine[reach : reach + rows], r.sine[reach : reach + rows]
            ).astype(B16)
            for k, value in ((p, grad_keys), (pairs + p, grad_values)):
                r.own_kv[s, :, lanes(k)] = value[reach : reach + rows]
                r.edge_src[0, span(s, reach), lanes(k)] = value[reach + rows :].astype(B16)
                r.edge_src[1, span(s, reach), lanes(k)] = value[:reach].astype(B16)

    loop(streams, attend_back)
    edge.start()
    exchanges([put_b1], skip=ends)
    down.last()

    def grad_out(m):
        out = nn(r.tt[span(m, TILE), :], r.att[...]).astype(B16)
        r.ga[span(m, blocks), :, quarter:] = out.reshape(blocks, part, quarter)

    loop(tiles, grad_out)

    def grad_query(m):
        out = nn(r.n1t[span(m, TILE), :], r.gp[:, :quarter]).astype(B16)
        r.ga[span(m, blocks), :, :quarter] = out.reshape(blocks, part, quarter)

    loop(tiles, grad_query)
    exchanges([put_a])

    def norm_again(i):
        s, h = i // per, i % per
        x = r.tok_all[s, span(h, CHUNK), :].astype(F32)
        scaled, inverse, _ = norm_forward(x, r.gain[0:1, :])
        r.scaled[span(i, CHUNK), :] = scaled
        r.inverse[span(i, CHUNK), :] = jnp.broadcast_to(inverse, (CHUNK, LANES))

    loop(streams * per, norm_again, UNROLL)
    down.finish()
    steps([put_b1], True, skip=2)
    edge.arrive()

    def join(s):
        for k in range(2 * pairs):
            value = r.own_kv[s, :, lanes(k)]
            first = value[:reach] + r.edge_mid[0, span(s, reach), lanes(k)].astype(F32)
            final = value[rows - reach :] + r.edge_mid[1, span(s, reach), lanes(k)].astype(F32)
            middle = [value[reach : rows - reach]] if rows > 2 * reach else []
            value = jnp.concatenate([first] + middle + [final], axis=0)
            if k < pairs:
                value = unrotate(
                    value, r.cosine[reach : reach + rows], r.sine[reach : reach + rows]
                )
            r.gp[span(s, rows), lanes(pairs + k)] = value.astype(B16)

    loop(streams, join)

    def grad_pair(i):
        m, j = i // 2, i % 2
        at = pl.ds(pl.multiple_of((j + 1) * quarter, quarter), quarter)
        out = nn(r.n1t[span(m, TILE), :], r.gp[:, at]).astype(B16)
        r.gc[span(m, blocks), :, span(j, quarter)] = out.reshape(blocks, part, quarter)

    loop(tiles * 2, grad_pair)
    steps([put_a], True, stop=1)

    def one_project(j):
        w = r.a_all[span(j, blocks), :, :three].reshape(TILE, three)
        out = nt(r.gp[...], w)
        at = span(j, TILE)
        r.gain_row[0:1, at] = jnp.sum(out * r.scaled[:, at], axis=0, keepdims=True)
        r.src_b[:, :, at] = out.astype(B16).reshape(streams, rows, TILE)

    loop(tiles, one_project)
    for s in range(seq.n):
        k = s * part // LANES
        r.gain_parts[s] = r.gain_row[:, k * LANES : (k + 1) * LANES]
    exchanges([one])
    exchanges([put_g])
    exchanges([put_c])
    put_b2.last()
    put_b1.last()
    steps([one], True)
    steps([put_a], True, skip=1, stop=2)
    steps([put_g], True, stop=1)
    for j in range(main):
        cut = slice(j * LANES, (j + 1) * LANES)
        for k in range(2):
            at = (2 * j + k) * LANES
            r.din[k, cut, :] = db1[:, at : at + LANES].T
        r.ddown_t[cut, :] = db2[:, cut].T
    rim_sum = db1[:, rim_at:].T
    r.din[0, flat:, :] = rim_sum[:tail]
    r.din[1, flat:, :] = rim_sum[tail : 2 * tail]
    r.ddown_t[flat:, :] = rim_sum[2 * tail : 3 * tail]
    steps([put_c], True, stop=1)
    steps([put_a], True, skip=2)
    steps([put_g], True, skip=1, stop=2)
    one.last()

    def final(h):
        at = span(h, CHUNK)
        here = pl.ds(pl.multiple_of(fsdp.me * rows + h * CHUNK, CHUNK), CHUNK)
        got = norm_backward(
            r.one_sum[at, :], r.scaled[here, :], r.inverse[here, 0:1], r.gain[0:1, :]
        )
        r.dinput[at, :] = r.own_grad[at, :] + got
        middle = r.tok[at, :].astype(F32) + r.attn_all[fsdp.me, at, :].astype(F32)
        r.out[at, :] = (middle + r.down_sum[at, :]).astype(B16)

    loop(per, final)
    steps([put_c], True, skip=1, stop=2)
    steps([put_g], True, skip=2)
    put_a.last()
    put_g.last()
    put_g2.start()
    r.dqkv[0] = da[:, :quarter]
    for k in range(pairs):
        at = quarter + k * LANES
        r.dout[k * LANES : (k + 1) * LANES, :] = da[:, at : at + LANES].T
    steps([put_c], True, skip=2)
    steps([put_g2], False)
    put_g2.finish()
    total = r.gain_got[0]
    for f in range(1, fsdp.n):
        total = total + r.gain_got[f]
    total = pltpu.roll(total, (LANES - shift) % LANES, 1)
    r.dgain_one[...] = total[0:1, :piece]
    r.dgain_two[...] = total[1:2, :piece]
    put_c.last()
    r.dqkv[1] = dc[:, :quarter]
    r.dqkv[2] = dc[:, quarter:]
    for job in (edge, one, put_b1, put_b2, put_a, put_c, put_g):
        job.finish()


def run_layer(tok, grd, gain_in, qkv, out_w, in_two, down_t, freq, lengths):
    n, nf = lax.axis_size("seq"), lax.axis_size("fsdp")
    rows, width = tok.shape
    count, part = down_t.shape
    quarter, piece = out_w.shape[0], gain_in.shape[1]
    gain_block = (16, LANES)
    wide_a, wide_2 = 4 * quarter, count // LANES * LANES
    wide_1 = 2 * wide_2 + LANES
    block_c = (part, 2 * quarter)
    block_a, block_1, block_2 = (part, wide_a), (part, wide_1), (part, wide_2)
    pairs = quarter // LANES
    streams = nf
    group = streams * rows
    outer = rows + 2 * WIN
    vmem = pl.BlockSpec(memory_space=pltpu.VMEM)
    ins = [
        ("tok", tok, vmem),
        ("grd", grd, vmem),
        ("gain_in", gain_in, vmem),
        ("qkv", qkv, vmem),
        ("out_w", out_w, vmem),
        ("in_two", in_two, vmem),
        ("down_t", down_t, vmem),
        ("freq", freq, vmem),
        ("lengths", lengths, pl.BlockSpec(memory_space=pltpu.SMEM)),
    ]
    outs = [
        ("out", (rows, width), B16),
        ("dinput", (rows, width), F32),
        ("dgain_one", (1, piece), F32),
        ("dgain_two", (1, piece), F32),
        ("dqkv", (3, part, quarter), F32),
        ("dout", (quarter, part), F32),
        ("din", (2, count, part), F32),
        ("ddown_t", (count, part), F32),
    ]
    plan = Plan()
    token_block = (rows, width)
    for name, count_, shape, dtype in (
        ("tok", nf, token_block, B16),
        ("grd", nf, token_block, B16),
        ("rim", nf, (2, WIN, width), B16),
        ("a", n, block_a, B16),
        ("b1", n, block_1, B16),
        ("b2", n, block_2, B16),
        ("attn", nf, token_block, B16),
        ("back", nf, token_block, B16),
    ):
        plan.vmem(name + "_all", (count_,) + shape, dtype)
        plan.add(name + "_g", *Gather.scratch(count_))
    for name, count_, shape, dtype in (
        ("attn", nf, token_block, B16),
        ("back", nf, token_block, B16),
        ("down", nf, token_block, B16),
        ("one", nf, token_block, B16),
        ("b1", n, block_1, B16),
        ("b2", n, block_2, B16),
        ("a", n, block_c, B16),
        ("c", n, block_c, B16),
        ("gain", n, (8, LANES), F32),
    ):
        plan.add(name + "_r", *Reduce.scratch(count_, shape, dtype))
    plan.add("b1_relay", *Reduce.relay_scratch(block_1, B16))
    plan.vmem("rim_mid", (2, WIN, width), B16)
    plan.add("halo_s", *Halo.scratch())
    plan.vmem("gains", gain_block, B16)
    plan.vmem("gains_mid", (n,) + gain_block, B16)
    plan.add("gains_g", *Gather.scratch(n))
    plan.vmem("gains_all", (nf, n) + gain_block, B16)
    plan.add("gains2_g", *Gather.scratch(nf))
    plan.vmem("gain_mid", (8, LANES), F32)
    plan.vmem("gain_got", (nf, 8, LANES), F32)
    plan.vmem("cosine", (outer, LANES), F32)
    plan.vmem("sine", (outer, LANES), F32)
    plan.add("gain_g", *Gather.scratch(nf))
    plan.add("edge_s", *Halo.scratch())
    for name, shape, dtype in (
        ("edge_src", (2, streams * WIN, 2 * quarter), B16),
        ("edge_mid", (2, streams * WIN, 2 * quarter), B16),
        ("gain", (gain_block[0], width), F32),
        ("gain_row", (8, width), F32),
        ("gain_parts", (n, 8, LANES), F32),
        ("nx", (streams, outer, width), B16),
        ("n1t", (width, group), B16),
        ("gt", (width, group), B16),
        ("tt", (width, group), B16),
        ("qs", (streams, pairs, rows, LANES), B16),
        ("q2", (streams, pairs, 2 * rows, LANES), B16),
        ("k2", (streams, pairs, 2 * outer, LANES), B16),
        ("v2", (streams, pairs, 2 * outer, LANES), B16),
        ("lse", (streams, 2 * pairs, rows, LANES), F32),
        ("att", (group, quarter), B16),
        ("src_a", (streams,) + token_block, B16),
        ("src_b", (streams,) + token_block, B16),
        ("attn_mid", token_block, B16),
        ("back_mid", token_block, B16),
        ("down_sum", token_block, F32),
        ("one_sum", token_block, F32),
        ("scaled", (group, width), F32),
        ("inverse", (group, LANES), F32),
        ("big", (group, 2 * (wide_2 + LANES)), F32),
        ("mix", (group, wide_2 + LANES), B16),
        ("mix_rim", (group, LANES), B16),
        ("dfull", (width, wide_2 + LANES), B16),
        ("gh", (group, wide_1), B16),
        ("gb1", (n,) + block_1, B16),
        ("gb2", (n,) + block_2, B16),
        ("ga", (n,) + block_c, B16),
        ("gc", (n,) + block_c, B16),
        ("own_grad", token_block, F32),
        ("own_kv", (streams, rows, 2 * quarter), F32),
        ("gatt", (group, quarter), B16),
        ("gp", (group, 3 * quarter), B16),
    ):
        plan.vmem(name, shape, dtype)
    names = [i[0] for i in ins] + [o[0] for o in outs] + plan.names
    return pl.pallas_call(
        functools.partial(layer_kernel, tuple(names)),
        out_shape=[jax.ShapeDtypeStruct(s, d) for _, s, d in outs],
        in_specs=[i[2] for i in ins],
        out_specs=[vmem] * len(outs),
        scratch_shapes=plan.shapes,
        compiler_params=pltpu.CompilerParams(
            collective_id=1, has_side_effects=True, vmem_limit_bytes=63 * 1024 * 1024
        ),
    )(*[i[1] for i in ins])


def per_device(
    layer_input,
    doc_lengths,
    attn_gain,
    qkv_weight,
    out_weight,
    mlp_gain,
    in_weight,
    down_weight,
    out_grad,
):
    gain_in = jnp.stack([attn_gain, mlp_gain])
    gain_in = jnp.pad(gain_in, ((0, 6), (0, 0)))
    half = np.arange(LANES)[None, :] % (HEAD // 2)
    freq = 10000.0 ** (-(2.0 / HEAD) * half)
    output, input_grad, dgain_one, dgain_two, dqkv, dout, din, ddown_t = run_layer(
        layer_input[0],
        out_grad[0],
        gain_in,
        qkv_weight.transpose(1, 0, 2),
        out_weight,
        in_weight.transpose(1, 2, 0),
        down_weight.T,
        jnp.asarray(freq, F32),
        doc_lengths,
    )
    return (
        output[None],
        input_grad[None],
        dgain_one[0],
        dqkv.transpose(1, 0, 2),
        dout,
        dgain_two[0],
        din.transpose(2, 0, 1),
        ddown_t.T,
    )


def solution(mesh):
    in_specs = (
        P("fsdp", "seq", None),
        P(),
        P(("seq", "fsdp")),
        P("seq", None, "fsdp"),
        P("fsdp", "seq"),
        P(("seq", "fsdp")),
        P("seq", None, "fsdp"),
        P("seq", "fsdp"),
        P("fsdp", "seq", None),
    )
    out_specs = (
        P("fsdp", "seq", None),
        P("fsdp", "seq", None),
        P(("seq", "fsdp")),
        P("seq", None, "fsdp"),
        P("fsdp", "seq"),
        P(("seq", "fsdp")),
        P("seq", None, "fsdp"),
        P("seq", "fsdp"),
    )
    return jax.shard_map(
        per_device, mesh=mesh, in_specs=in_specs, out_specs=out_specs, check_vma=False
    )
```

```python
import functools

import jax
import jax.numpy as jnp
import numpy as np
from jax import lax
from jax.experimental import pallas as pl
from jax.experimental.pallas import tpu as pltpu
from jax.sharding import PartitionSpec as P

HEAD = 64
WIN = 64


EPSILON = 1e-05


class Place:
    def __init__(self, axis):
        self.axis = axis
        self.n = lax.axis_size(axis)
        self.length = self.n // 2
        me = lax.axis_index(axis)
        self.me = me
        self.at = me // 2
        self.side = me % 2

    def partner(self):
        return {self.axis: self.at * 2 + (1 - self.side)}

    def right(self):
        return {self.axis: self.me + 2}

    def left(self):
        return {self.axis: self.me - 2}

    def has_right(self):
        return self.at < self.length - 1

    def has_left(self):
        return self.at > 0

    def greet(self, barrier):
        mesh = pl.DeviceIdType.MESH
        pl.semaphore_signal(barrier, inc=1, device_id=self.partner(), device_id_type=mesh)

        @pl.when(self.has_left())
        def _():
            pl.semaphore_signal(barrier, inc=1, device_id=self.left(), device_id_type=mesh)

        @pl.when(self.has_right())
        def _():
            pl.semaphore_signal(barrier, inc=1, device_id=self.right(), device_id_type=mesh)

    def diagonal(self):
        there = jnp.where(self.side == 1, self.has_right(), self.has_left())
        return there, {self.axis: self.me + 2 * self.side - 1}

    def peers(self):
        one, none = jnp.int32(1), jnp.int32(0)
        return 1 + jnp.where(self.has_left(), one, none) + jnp.where(self.has_right(), one, none)


def when(condition, action):
    if condition is True:
        action()
    else:
        pl.when(condition)(action)


def remote(src, dst, send, recv, device):
    return pltpu.make_async_remote_copy(
        src_ref=src,
        dst_ref=dst,
        send_sem=send,
        recv_sem=recv,
        device_id=device,
        device_id_type=pl.DeviceIdType.MESH,
    )


class Gather:
    scratch = staticmethod(
        lambda n: [
            pltpu.SemaphoreType.DMA((3, n)),
            pltpu.SemaphoreType.DMA((n,)),
            pltpu.SemaphoreType.DMA,
        ]
    )

    def __init__(self, place, src, dst, sems, relayed=False):
        self.place, self.src, self.dst = place, src, dst
        self.send, self.recv, self.local = sems
        self.relayed = relayed

    def crosses(self, i):
        if not self.relayed:
            return True
        inner = jnp.logical_and(i > 0, i < self.place.length - 1)
        return jnp.logical_or(inner, i == self.place.at)

    def relay(self, d):
        place = self.place
        ends = ((d, 0, 1), (place.length - 1 - d, place.length - 1, 2))
        for at, end, way in ends:
            block = 2 * end + 1 - place.side

            @pl.when(place.at == at)
            def _(block=block, way=way):
                self.copy(0, block, place.partner()).wait_recv()
                (self.ahead if way == 1 else self.behind)(block, False, lambda c: c.start())

    def copy(self, way, block, device, own=False):
        src = self.src if own else self.dst.at[block]
        return remote(src, self.dst.at[block], self.send.at[way, block], self.recv.at[block], device)

    def onward(self, block, own, act):
        place = self.place
        act(self.copy(0, block, place.partner(), own))

    def start(self):
        place = self.place
        if self.src is not None:
            pltpu.make_async_copy(self.src, self.dst.at[place.me], self.local).start()
        self.start_lines()
        self.start_across()

    def start_lines(self):
        place = self.place
        self.ahead(place.me, self.src is not None, lambda c: c.start())
        self.behind(place.me, self.src is not None, lambda c: c.start())

    def start_across(self):
        self.onward(self.place.me, self.src is not None, lambda c: c.start())

    def ahead(self, block, own, act):
        place = self.place

        @pl.when(place.has_right())
        def _():
            act(self.copy(1, block, place.right(), own))

    def behind(self, block, own, act):
        place = self.place

        @pl.when(place.has_left())
        def _():
            act(self.copy(2, block, place.left(), own))

    def step(self, d):
        place = self.place

        @pl.when(place.at - d >= 0)
        def _():
            block = place.me - 2 * d
            self.copy(1, block, place.partner()).wait_recv()
            self.ahead(block, False, lambda c: c.start())
            when(
                self.crosses(place.at - d),
                lambda: self.onward(block, False, lambda c: c.start()),
            )

        @pl.when(place.at + d < place.length)
        def _():
            block = place.me + 2 * d
            self.copy(2, block, place.partner()).wait_recv()
            self.behind(block, False, lambda c: c.start())
            when(
                self.crosses(place.at + d),
                lambda: self.onward(block, False, lambda c: c.start()),
            )

    def finish(self):
        place = self.place
        if self.src is not None:
            pltpu.make_async_copy(self.src, self.dst.at[place.me], self.local).wait()

        def arrived(i, carry):
            inner = True
            if self.relayed:
                inner = jnp.logical_and(i > 0, i < place.length - 1)
            when(
                inner,
                lambda: self.copy(0, 2 * i + 1 - place.side, place.partner()).wait_recv(),
            )
            when(
                self.crosses(i),
                lambda: self.onward(2 * i + place.side, False, lambda c: c.wait_send()),
            )

            @pl.when(i <= place.at)
            def _():
                self.ahead(2 * i + place.side, False, lambda c: c.wait_send())

            @pl.when(i >= place.at)
            def _():
                self.behind(2 * i + place.side, False, lambda c: c.wait_send())

            return carry

        lax.fori_loop(0, place.length, arrived, 0)
        if self.relayed:
            self.ahead(1 - place.side, False, lambda c: c.wait_send())
            self.behind(2 * place.length - 1 - place.side, False, lambda c: c.wait_send())


class Reduce:
    @staticmethod
    def scratch(n, block, dtype):
        length = n // 2
        return [
            pltpu.VMEM((length,) + block, dtype),
            pltpu.VMEM((length + 1,) + block, dtype),
            pltpu.SemaphoreType.DMA((2, length)),
            pltpu.SemaphoreType.DMA((length,)),
            pltpu.SemaphoreType.DMA((length + 1,)),
        ]

    @staticmethod
    def relay_scratch(block, dtype):
        return [
            pltpu.VMEM((2,) + block, dtype),
            pltpu.SemaphoreType.DMA((2,)),
            pltpu.SemaphoreType.DMA((2,)),
        ]

    def __init__(self, place, src, dst, scratch, relays=None):
        self.place, self.src, self.dst = place, src, dst
        self.paired, self.lined, self.send, self.pair_recv, self.line_recv = scratch
        self.relays = relays

    def crosses(self, i):
        if self.relays is None:
            return True
        return jnp.logical_and(i > 0, i < self.place.length - 1)

    def pass_on(self, end, device):
        held, send, recv = self.relays
        block = 2 * (end * (self.place.length - 1)) + 1 - self.place.side
        return self.src.at[block], remote(
            self.src.at[block], held.at[end], send.at[end], recv.at[end], device
        )

    def relay(self, d):
        place = self.place
        finish = place.length - 1
        for end, at in ((0, finish - d), (1, d)):
            device = place.right() if end else place.left()
            final = finish if end else 0

            @pl.when(place.at == at)
            def _(end=end, device=device, final=final):
                block, copy = self.pass_on(end, device)

                @pl.when(d > 0)
                def _():
                    copy.wait_recv()
                    self.add(block, [block, self.relays[0].at[end]])

                @pl.when(place.at != final)
                def _():
                    copy.start()

                @pl.when(place.at == final)
                def _():
                    self.across(final).start()

    def mine(self, i):
        return self.src.at[2 * i + self.place.side]

    def across(self, i):
        place = self.place
        return remote(
            self.src.at[2 * i + 1 - place.side],
            self.paired.at[i],
            self.send.at[0, i],
            self.pair_recv.at[i],
            place.partner(),
        )

    def along(self, i, slot, device):
        return remote(
            self.mine(i), self.lined.at[slot], self.send.at[1, i], self.line_recv.at[slot], device
        )

    def exchange(self, d):
        place = self.place

        @pl.when(place.at + d < place.length)
        def _():
            when(self.crosses(place.at + d), lambda: self.across(place.at + d).start())

        @pl.when(jnp.logical_and(d > 0, place.at - d >= 0))
        def _():
            when(self.crosses(place.at - d), lambda: self.across(place.at - d).start())

    def add(self, out, refs):
        rows = out.shape[0]
        tile = 16 if rows % 16 == 0 else 8

        def each(i, carry):
            at = pl.ds(pl.multiple_of(i * tile, tile), tile)
            total = refs[0][at, :].astype(jnp.float32)
            for ref in refs[1:]:
                total = total + ref[at, :].astype(jnp.float32)
            out[at, :] = total.astype(out.dtype)
            return carry

        lax.fori_loop(0, rows // tile, each, 0)

    def own(self, i):
        self.across(i).wait_recv()
        return [self.mine(i), self.paired.at[i]]

    def combine(self, i, paired, lined):
        def total(pair):
            refs = self.own(i) if pair else [self.mine(i)]

            @pl.when(lined)
            def _():
                self.along(i, i, self.place.partner()).wait_recv()
                self.add(self.mine(i), refs + [self.lined.at[i]])

            if pair:

                @pl.when(jnp.logical_not(lined))
                def _():
                    self.add(self.mine(i), refs)

        when(paired, lambda: total(True))
        if paired is not True:
            pl.when(jnp.logical_not(paired))(lambda: total(False))

    def step(self, d):
        place = self.place

        @pl.when(place.at + d < place.length)
        def _():
            i = place.at + d
            self.combine(i, self.crosses(i), place.has_left())
            self.along(i, i, place.right()).start()

        @pl.when(place.at - d >= 0)
        def _():
            i = place.at - d
            self.combine(i, self.crosses(i), place.has_right())
            slot = jnp.where(d == 1, place.length, i)
            self.along(i, slot, place.left()).start()

    def last(self):
        place = self.place
        i, extra = place.at, place.length
        refs = self.own(i)

        @pl.when(place.has_left())
        def _():
            self.along(i, i, place.partner()).wait_recv()

        @pl.when(place.has_right())
        def _():
            self.along(i, extra, place.partner()).wait_recv()

        both = jnp.logical_and(place.has_left(), place.has_right())

        @pl.when(both)
        def _():
            self.add(self.dst, refs + [self.lined.at[i], self.lined.at[extra]])

        @pl.when(jnp.logical_and(place.has_left(), jnp.logical_not(both)))
        def _():
            self.add(self.dst, refs + [self.lined.at[i]])

        @pl.when(jnp.logical_and(place.has_right(), jnp.logical_not(both)))
        def _():
            self.add(self.dst, refs + [self.lined.at[extra]])

    def finish(self):
        place = self.place

        def each(i, carry):
            crosses = self.crosses(i)
            if crosses is not True:
                crosses = jnp.logical_or(crosses, i == place.at)
            when(crosses, lambda: self.across(i).wait_send())

            @pl.when(i != place.at)
            def _():
                self.along(i, i, place.partner()).wait_send()

            return carry

        lax.fori_loop(0, place.length, each, 0)
        if self.relays is not None:

            @pl.when(place.has_left())
            def _():
                self.pass_on(0, place.left())[1].wait_send()

            @pl.when(place.has_right())
            def _():
                self.pass_on(1, place.right())[1].wait_send()


class Halo:
    scratch = staticmethod(lambda: [pltpu.SemaphoreType.DMA((2,)), pltpu.SemaphoreType.DMA((2,))])

    def __init__(self, place, src, mid, sems):
        self.place, self.src, self.mid = place, src, mid
        self.send, self.recv = sems
        self.after = place.me < place.n - 1
        self.before = place.me > 0

    def copy(self, way):
        rows, width = self.src.shape[0], self.mid.shape[1]
        at = rows - width if way == 0 else 0
        other = {self.place.axis: self.place.me + 1 - 2 * way}
        return remote(
            self.src.at[pl.ds(at, width)],
            self.mid.at[way],
            self.send.at[way],
            self.recv.at[way],
            other,
        )

    def start(self):
        @pl.when(self.after)
        def _():
            self.copy(0).start()

        @pl.when(self.before)
        def _():
            self.copy(1).start()

        @pl.when(jnp.logical_not(self.before))
        def _():
            self.mid[0] = jnp.zeros(self.mid.shape[1:], self.mid.dtype)

        @pl.when(jnp.logical_not(self.after))
        def _():
            self.mid[1] = jnp.zeros(self.mid.shape[1:], self.mid.dtype)

    def arrive(self):
        @pl.when(self.before)
        def _():
            self.copy(0).wait_recv()

        @pl.when(self.after)
        def _():
            self.copy(1).wait_recv()

    def finish(self):
        @pl.when(self.after)
        def _():
            self.copy(0).wait_send()

        @pl.when(self.before)
        def _():
            self.copy(1).wait_send()


def greet_all(places, slanted):
    barrier = pltpu.get_barrier_semaphore()
    extra = jnp.int32(0)
    if slanted:
        there, device = places[0].diagonal()
        extra = jnp.where(there, jnp.int32(1), jnp.int32(0))

        @pl.when(there)
        def _():
            pl.semaphore_signal(
                barrier, inc=1, device_id=device, device_id_type=pl.DeviceIdType.MESH
            )

    for place in places:
        place.greet(barrier)
    pl.semaphore_wait(barrier, extra + sum(place.peers() for place in places))


def steps(jobs, down, skip=0, stop=None):
    length = jobs[0].place.length
    stop = length - 1 if stop is None else min(stop, length - 1)

    def each(k, carry):
        d = length - 1 - k if down else k + 1
        for job in jobs:
            job.step(d)
        return carry

    if skip < stop:
        lax.fori_loop(skip, stop, each, 0)


def relays(job, skip=0, stop=None):
    length = job.place.length
    stop = length if stop is None else stop

    def each(k, carry):
        job.relay(k)
        return carry

    lax.fori_loop(skip, stop, each, 0)


def exchanges(jobs, skip=0, stop=None):
    length = jobs[0].place.length
    stop = length if stop is None else stop

    def each(k, carry):
        for job in jobs:
            job.exchange(length - 1 - k)
        return carry

    lax.fori_loop(skip, stop, each, 0)


B16, F32 = jnp.bfloat16, jnp.float32
LANES = 128
TILE = 256
CHUNK = 32
UNROLL = 4


class Edge(Halo):
    def copy(self, way):
        other = {self.place.axis: self.place.me + 1 - 2 * way}
        return remote(
            self.src.at[way], self.mid.at[way], self.send.at[way], self.recv.at[way], other
        )


class Plan:
    def __init__(self):
        self.names, self.shapes = [], []

    def add(self, name, *items):
        self.names += [name] * len(items)
        self.shapes += items

    def vmem(self, name, shape, dtype):
        self.add(name, pltpu.VMEM(shape, dtype))


class Refs:
    def __init__(self, names, refs):
        self.groups = {}
        for name, ref in zip(names, refs):
            self.groups.setdefault(name, []).append(ref)

    def __getattr__(self, name):
        return self.groups[name][0]

    def all(self, name):
        return self.groups[name]


def nn(left, right):
    return jnp.dot(left, right, preferred_element_type=F32)


def nt(left, right):
    return lax.dot_general(left, right, (((1,), (1,)), ((), ())), preferred_element_type=F32)


def loop(count, body, unroll=1):
    def each(i, carry):
        for k in range(unroll):
            body(i * unroll + k)
        return carry

    lax.fori_loop(0, count // unroll, each, 0)


def span(i, width):
    return pl.ds(pl.multiple_of(i * width, width), width)


def norm_forward(values, gain):
    mean = jnp.mean(values, axis=-1, keepdims=True)
    centred = values - mean
    inverse = lax.rsqrt(jnp.mean(centred * centred, axis=-1, keepdims=True) + EPSILON)
    scaled = centred * inverse
    return (scaled, inverse, (scaled * gain).astype(B16))


def norm_backward(grad, scaled, inverse, gain):
    weighted = grad * gain
    return inverse * (
        weighted
        - jnp.mean(weighted, axis=-1, keepdims=True)
        - scaled * jnp.mean(weighted * scaled, axis=-1, keepdims=True)
    )


def gelu_parts(inner):
    cdf = 0.5 * (1.0 + lax.erf(inner * 0.7071067811865476))
    density = jnp.exp(-0.5 * inner * inner) * 0.3989422804014327
    return (inner * cdf, cdf + inner * density)


def swap(field):
    lane = lax.broadcasted_iota(jnp.int32, field.shape, 1)
    half = HEAD // 2
    return jnp.where(
        lane % HEAD < half, pltpu.roll(field, LANES - half, 1), pltpu.roll(field, half, 1)
    )


def rotate(field, cosine, sine):
    return field * cosine + swap(field) * sine


def unrotate(field, cosine, sine):
    return field * cosine - swap(field) * sine


def halves(field):
    lane = lax.broadcasted_iota(jnp.int32, field.shape, 1)
    low = lane < HEAD
    zero = jnp.zeros_like(field)
    return jnp.concatenate([jnp.where(low, field, zero), jnp.where(low, zero, field)], axis=0)


def layer_kernel(names, *refs):
    r = Refs(names, refs)
    seq, fsdp = Place("seq"), Place("fsdp")
    rows, width = r.tok.shape
    count = r.down_t.shape[0]
    streams = r.tok_all.shape[0]
    group = streams * rows
    quarter = r.att.shape[1]
    pairs = quarter // LANES
    part = r.a_all.shape[1]
    reach, outer = WIN, rows + 2 * WIN
    main = count // LANES
    tail = count - main * LANES
    flat = main * LANES
    rim_at = 2 * flat
    blocks = TILE // part
    tiles = width // TILE
    per = rows // CHUNK
    scale = HEAD**-0.5
    three = 3 * quarter
    half_streams = TILE // rows

    tokens = Gather(fsdp, r.tok, r.tok_all, r.all("tok_g"))
    cots = Gather(fsdp, r.grd, r.grd_all, r.all("grd_g"))
    halo = Halo(seq, r.tok, r.rim_mid, r.all("halo_s"))
    rim = Gather(fsdp, r.rim_mid, r.rim_all, r.all("rim_g"))
    gains = Gather(seq, r.gains, r.gains_mid, r.all("gains_g"))
    gains2 = Gather(fsdp, r.gains_mid, r.gains_all, r.all("gains2_g"))
    get_a = Gather(seq, None, r.a_all, r.all("a_g"), True)
    get_b1 = Gather(seq, None, r.b1_all, r.all("b1_g"))
    get_b2 = Gather(seq, None, r.b2_all, r.all("b2_g"))
    attn = Reduce(fsdp, r.src_a, r.attn_mid, r.all("attn_r"))
    attn2 = Gather(fsdp, r.attn_mid, r.attn_all, r.all("attn_g"))
    back = Reduce(fsdp, r.src_a, r.back_mid, r.all("back_r"))
    back2 = Gather(fsdp, r.back_mid, r.back_all, r.all("back_g"))
    down = Reduce(fsdp, r.src_b, r.down_sum, r.all("down_r"))
    one = Reduce(fsdp, r.src_b, r.one_sum, r.all("one_r"))
    db1 = r.big.at[0:part, 0 : rim_at + LANES]
    db2 = r.big.at[part : 2 * part, 0:flat]
    da = r.big.at[2 * part : 3 * part, 0 : 2 * quarter]
    dc = r.big.at[2 * part : 3 * part, 2 * quarter : 4 * quarter]
    put_b1 = Reduce(seq, r.gb1, db1, r.all("b1_r"), r.all("b1_relay"))
    put_b2 = Reduce(seq, r.gb2, db2, r.all("b2_r"))
    put_a = Reduce(seq, r.ga, da, r.all("a_r"))
    put_c = Reduce(seq, r.gc, dc, r.all("c_r"))
    put_g = Reduce(seq, r.gain_parts, r.gain_mid, r.all("gain_r"))
    put_g2 = Gather(fsdp, r.gain_mid, r.gain_got, r.all("gain_g"))
    edge = Edge(seq, r.edge_src, r.edge_mid, r.all("edge_s"))
    stat = Edge(seq, r.stat_src, r.stat_mid, r.all("stat_s"))

    piece = r.gain_in.shape[1]
    shift = (seq.me * fsdp.n + fsdp.me) * piece % LANES
    filled = [jnp.zeros((8, LANES - piece), F32)] if piece < LANES else []
    wide = jnp.concatenate([r.gain_in[...].astype(F32)] + filled, axis=1)
    wide = jnp.concatenate([pltpu.roll(wide, shift, 1), jnp.zeros((8, LANES), F32)], axis=0)
    r.gains[...] = wide.astype(B16)
    for k in range(3):
        r.a_all[seq.me, :, k * quarter : (k + 1) * quarter] = r.qkv[k]
    for k in range(pairs):
        at = three + k * LANES
        r.a_all[seq.me, :, at : at + LANES] = r.out_w[k * LANES : (k + 1) * LANES, :].T
    greet_all((seq, fsdp), True)
    for job in (gains, get_a, tokens, halo):
        job.start()

    for j in range(main):
        cut = slice(j * LANES, (j + 1) * LANES)
        for k in range(2):
            at = (2 * j + k) * LANES
            r.b1_all[seq.me, :, at : at + LANES] = r.in_two[k, cut, :].T
        r.b2_all[seq.me, :, cut] = r.down_t[cut, :].T
    last = [r.in_two[0, flat:, :], r.in_two[1, flat:, :], r.down_t[flat:, :]]
    last.append(jnp.zeros((LANES - 3 * tail, part), B16))
    r.b1_all[seq.me, :, rim_at:] = jnp.concatenate(last, axis=0).T

    steps([gains, get_a], False, stop=1)
    relays(get_a, stop=1)
    halo.arrive()
    rim.start()
    steps([tokens], False)
    place = seq.me * rows - reach + lax.broadcasted_iota(jnp.int32, (outer, LANES), 0)
    spot = lax.broadcasted_iota(jnp.int32, (outer, LANES), 1) % HEAD
    angle = place.astype(F32) * r.freq[...]
    r.cosine[...] = jnp.cos(angle)
    sine = jnp.sin(angle)
    r.sine[...] = jnp.where(spot < HEAD // 2, -sine, sine)
    steps([gains, get_a], False, skip=1, stop=2)
    relays(get_a, skip=1, stop=2)
    steps([rim], False)
    steps([gains, get_a], False, skip=2)
    relays(get_a, skip=2, stop=3)
    get_b1.start_lines()
    get_b1.start_across()
    gains.finish()
    gains2.start()
    cots.start()
    steps([gains2], False)
    gains2.finish()

    for k in range(width // LANES):
        total = jnp.zeros((r.gains.shape[0], LANES), F32)
        for s in range(k * LANES // part, (k + 1) * LANES // part):
            for f in range(streams):
                total = total + r.gains_all[f, s].astype(F32)
        r.gain[:, k * LANES : (k + 1) * LANES] = total
    tokens.finish()
    rim.finish()
    halo.finish()

    def norm_own(i):
        s, h = i // per, i % per
        x = r.tok_all[s, span(h, CHUNK), :].astype(F32)
        at = pl.ds(pl.multiple_of(reach + h * CHUNK, CHUNK), CHUNK)
        r.nx[s, at, :] = norm_forward(x, r.gain[0:1, :])[2]

    loop(streams * per, norm_own, UNROLL)

    rims = reach // CHUNK

    def norm_rim(i):
        s, w, h = i // (2 * rims), i // rims % 2, i % rims
        x = r.rim_all[s, w, span(h, CHUNK), :].astype(F32)
        at = pl.ds(pl.multiple_of(w * (rows + reach) + h * CHUNK, CHUNK), CHUNK)
        r.nx[s, at, :] = norm_forward(x, r.gain[0:1, :])[2]

    loop(streams * 2 * rims, norm_rim, UNROLL)

    def turn_one(i):
        x = r.nx[:, reach : reach + rows, span(i, LANES)].reshape(group, LANES)
        r.n1t[span(i, LANES), :] = x.T

    def turn_grad(i):
        x = r.grd_all[:, :, span(i, LANES)].reshape(group, LANES)
        r.gt[span(i, LANES), :] = x.T

    relays(get_a, skip=3)
    get_a.finish()

    band = jnp.abs(
        lax.broadcasted_iota(jnp.int32, (rows, outer), 0)
        + reach
        - lax.broadcasted_iota(jnp.int32, (rows, outer), 1)
    )

    def lanes(p):
        return slice(p * LANES, (p + 1) * LANES)

    def project(s):
        x = r.nx[s]
        out = nn(x, r.a_all[:, :, quarter:three].reshape(width, 2 * quarter))
        for p in range(pairs):
            keys = rotate(out[:, lanes(p)], r.cosine[...], r.sine[...])
            r.k2[s, p] = halves(keys).astype(B16)
            r.v2[s, p] = halves(out[:, lanes(pairs + p)]).astype(B16)
        out = nn(x, r.a_all[:, :, :quarter].reshape(width, quarter))
        for p in range(pairs):
            query = rotate(out[:, lanes(p)], r.cosine[...], r.sine[...])
            own = query[reach : reach + rows]
            rims = jnp.concatenate([query[:reach], query[reach + rows :]], axis=0)
            r.qs[s, p] = own.astype(B16)
            r.q2[s, p] = halves(own).astype(B16)
            r.hq[s, p] = rims.astype(B16)
            r.hq2[s, p] = halves(rims).astype(B16)

    loop(streams // 2, project)
    steps([get_b1], False, stop=1)
    loop(streams - streams // 2, lambda i: project(i + streams // 2))

    def documents(s, place):
        docs = r.lengths.shape[1]
        ids = jnp.zeros(place.shape, jnp.int32)
        start = jnp.int32(0)
        for k in range(docs + 1):
            ids = ids + (place >= start).astype(jnp.int32)
            if k < docs:
                start = start + r.lengths[s, k]
        return ids

    first = seq.me * rows

    def visible(s):
        across = first - reach + lax.broadcasted_iota(jnp.int32, (1, outer), 1)
        along = first + lax.broadcasted_iota(jnp.int32, (rows, 1), 0)
        return (band <= reach) & (documents(s, along) == documents(s, across))

    def visible_rims(s):
        along = lax.broadcasted_iota(jnp.int32, (2 * reach, 1), 0)
        along = first + jnp.where(along < reach, along - reach, along - reach + rows)
        across = first + lax.broadcasted_iota(jnp.int32, (1, rows), 1)
        near = jnp.abs(along - across) <= reach
        return near & (documents(s, along) == documents(s, across))

    def delta_of(product, h):
        low = lax.broadcasted_iota(jnp.int32, product.shape, 1) < HEAD
        zero = jnp.zeros_like(product)
        side = jnp.where(low, product, zero) if h == 0 else jnp.where(low, zero, product)
        return jnp.sum(side, axis=-1, keepdims=True)

    def attend(s):
        allowed = visible(s)
        for p in range(pairs):
            scores = nt(r.qs[s, p], r.k2[s, p]) * scale
            probs = []
            for h in range(2):
                masked = jnp.where(allowed, scores[:, h * outer : (h + 1) * outer], -1e30)
                top = jnp.max(masked, axis=-1, keepdims=True)
                expd = jnp.exp(masked - top)
                total = jnp.sum(expd, axis=-1, keepdims=True)
                r.lse[s, 2 * p + h] = jnp.broadcast_to(top + jnp.log(total), (rows, LANES))
                probs.append((expd / total).astype(B16))
            out = nn(jnp.concatenate(probs, axis=1), r.v2[s, p])
            r.att[span(s, rows), lanes(p)] = out.astype(B16)

    loop(streams, attend)
    steps([get_b1], False, skip=1, stop=2)
    get_b2.start_lines()

    def out_project(j):
        w = r.a_all[span(j, blocks), :, three:].reshape(TILE, quarter)
        out = nt(r.att[...], w).astype(B16)
        r.src_a[:, :, span(j, TILE)] = out.reshape(streams, rows, TILE)

    loop(tiles, out_project)
    exchanges([attn])
    steps([attn], True)
    steps([cots], False)
    loop(width // LANES, turn_one)
    cots.finish()
    steps([get_b1], False, skip=2)
    get_b2.start_across()
    attn.last()
    attn2.start()
    loop(width // LANES, turn_grad)
    steps([get_b2], False, stop=1)
    steps([attn2], False)
    steps([get_b2], False, skip=1, stop=2)
    attn2.finish()
    attn.finish()
    steps([get_b2], False, skip=2)

    def norm_two(i):
        s, h = i // per, i % per
        at = span(h, CHUNK)
        x = r.tok_all[s, at, :].astype(F32) + r.attn_all[s, at, :].astype(F32)
        scaled, inverse, normed = norm_forward(x, r.gain[1:2, :])
        r.scaled[span(i, CHUNK), :] = scaled
        r.inverse[span(i, CHUNK), :] = jnp.broadcast_to(inverse, (CHUNK, LANES))
        r.nx[s, pl.ds(pl.multiple_of(rows + h * CHUNK, CHUNK), CHUNK), :] = normed

    loop(streams * per, norm_two, UNROLL)

    def normed_two(m):
        return r.nx[span(m, half_streams), rows : 2 * rows, :].reshape(TILE, width)

    def turn_two(i):
        x = r.nx[:, rows : 2 * rows, span(i, LANES)].reshape(group, LANES)
        r.tt[span(i, LANES), :] = x.T

    loop(width // LANES, turn_two)
    get_b1.finish()

    sides = group // TILE
    rest = flat + LANES

    def hidden(i):
        m, j = i // main, i % main
        w = r.b1_all[:, :, span(j, TILE)].reshape(width, TILE)
        out = nn(normed_two(m), w)
        inner, gate = out[:, :LANES], out[:, LANES:]
        activated, slope = gelu_parts(inner)
        at = span(m, TILE)
        r.big[at, span(j, LANES)] = activated
        r.big[at, pl.ds(pl.multiple_of(rest + j * LANES, LANES), LANES)] = gate * slope
        r.mix[at, span(j, LANES)] = (activated * gate).astype(B16)

    loop(sides * main, hidden)
    lane = lax.broadcasted_iota(jnp.int32, (TILE, LANES), 1)

    def hidden_rim(m):
        w = r.b1_all[:, :, rim_at:].reshape(width, LANES)
        inner = nn(normed_two(m), w)
        gate = pltpu.roll(inner, LANES - tail, 1)
        activated, slope = gelu_parts(inner)
        at = span(m, TILE)
        zero = jnp.zeros((TILE, LANES), F32)
        mixed = jnp.where(lane < tail, activated * gate, zero)
        r.big[at, flat:rest] = jnp.where(lane < tail, activated, zero)
        r.big[at, rest + flat :] = jnp.where(lane < tail, gate * slope, zero)
        r.mix[at, flat:] = mixed.astype(B16)
        r.mix_rim[at, :] = pltpu.roll(mixed, 2 * tail, 1).astype(B16)

    loop(sides, hidden_rim)

    def grad_down(m):
        out = nn(r.gt[span(m, TILE), :], r.mix[:, :flat]).astype(B16)
        r.gb2[span(m, blocks), :, :] = out.reshape(blocks, part, flat)

    loop(tiles, grad_down)
    get_b2.finish()
    exchanges([put_b2])

    def unpack(j):
        at = span(j, TILE)
        r.dfull[at, :flat] = r.b2_all[span(j, blocks), :, :].reshape(TILE, flat)
        x = r.b1_all[span(j, blocks), :, rim_at:].reshape(TILE, LANES).astype(F32)
        x = jnp.where(lane < tail, pltpu.roll(x, LANES - 2 * tail, 1), jnp.zeros_like(x))
        r.dfull[at, flat:] = x.astype(B16)

    loop(tiles, unpack)

    def grad_hidden(m, t, grad):
        at = span(m, TILE)
        inner = grad * r.big[at, pl.ds(pl.multiple_of(rest + t * LANES, LANES), LANES)]
        gate = grad * r.big[at, span(t, LANES)]
        return at, inner, gate

    def grad_mixed(i):
        m, t = i // main, i % main
        g = r.grd_all[span(m, half_streams)].reshape(TILE, width)
        grad = nn(g, r.dfull[:, span(t, LANES)])
        at, inner, gate = grad_hidden(m, t, grad)
        r.gh[at, span(2 * t, LANES)] = inner.astype(B16)
        r.gh[at, span(2 * t + 1, LANES)] = gate.astype(B16)

    loop(sides * main, grad_mixed)

    def grad_mixed_rim(m):
        g = r.grd_all[span(m, half_streams)].reshape(TILE, width)
        grad = nn(g, r.dfull[:, flat:])
        at, inner, gate = grad_hidden(m, main, grad)
        r.gh[at, rim_at:] = (inner + pltpu.roll(gate, tail, 1)).astype(B16)

    loop(sides, grad_mixed_rim)
    steps([put_b2], True, stop=1)

    r.gain_row[...] = jnp.zeros(r.gain_row.shape, F32)

    def back_project(j):
        w = r.b1_all[span(j, blocks)].reshape(TILE, rim_at + LANES)
        out = nt(r.gh[...], w)
        at = span(j, TILE)
        r.gain_row[1:2, at] = jnp.sum(out * r.scaled[:, at], axis=0, keepdims=True)
        r.src_a[:, :, at] = out.astype(B16).reshape(streams, rows, TILE)

    loop(tiles, back_project)
    exchanges([back])

    def grad_in(i):
        m, j = i // main, i % main
        out = nn(r.tt[span(m, TILE), :], r.gh[:, span(j, TILE)]).astype(B16)
        r.gb1[span(m, blocks), :, span(j, TILE)] = out.reshape(blocks, part, TILE)

    loop(tiles * main, grad_in)

    def grad_in_rim(m):
        at = span(m, TILE)
        out = nn(r.tt[at, :], r.gh[:, rim_at:]) + nn(r.gt[at, :], r.mix_rim[...])
        r.gb1[span(m, blocks), :, rim_at:] = out.astype(B16).reshape(blocks, part, LANES)

    loop(tiles, grad_in_rim)
    relays(put_b1, stop=1)
    exchanges([put_b1])
    def down_project(j):
        out = nt(r.mix[...], r.dfull[span(j, TILE), :]).astype(B16)
        r.src_b[:, :, span(j, TILE)] = out.reshape(streams, rows, TILE)

    loop(tiles, down_project)
    exchanges([down])
    steps([back], True)
    steps([put_b2], True, skip=1, stop=2)
    back.last()
    back2.start()
    relays(put_b1, skip=1, stop=2)
    steps([put_b2], True, skip=2)
    steps([put_b1], True, stop=1)
    steps([down], True)
    steps([back2], False)
    back2.finish()
    back.finish()

    def middle_grad(i):
        s, h = i // per, i % per
        at = span(h, CHUNK)
        here = span(i, CHUNK)
        got = norm_backward(
            r.back_all[s, at, :].astype(F32),
            r.scaled[here, :],
            r.inverse[here, 0:1],
            r.gain[1:2, :],
        )
        grad = r.grd_all[s, at, :].astype(F32) + got
        r.nx[s, at, :] = grad.astype(B16)

        @pl.when(s == fsdp.me)
        def _():
            r.own_grad[at, :] = grad

    relays(put_b1, skip=2, stop=3)
    loop(streams * per, middle_grad, UNROLL)

    def turn_middle(i):
        x = r.nx[:, :rows, span(i, LANES)].reshape(group, LANES)
        r.tt[span(i, LANES), :] = x.T

    loop(width // LANES, turn_middle)

    def grad_attended(s):
        w = r.a_all[:, :, three:].reshape(width, quarter)
        r.gatt[span(s, TILE), :] = nn(
            r.nx[span(s, half_streams), :rows, :].reshape(TILE, width), w
        ).astype(B16)

    loop(sides, grad_attended)
    steps([put_b1], True, skip=1, stop=2)

    def edges(s):
        at = span(s, rows)
        lane = lax.broadcasted_iota(jnp.int32, (rows, LANES), 1)
        total = jnp.zeros((rows, LANES), F32)
        for p in range(pairs):
            product = r.gatt[at, lanes(p)].astype(F32) * r.att[at, lanes(p)].astype(F32)
            for h in range(2):
                k = 2 * p + h
                total = jnp.where(lane == k, r.lse[s, k], total)
                total = jnp.where(lane == 2 * pairs + k, delta_of(product, h), total)
        total = total.T
        head_at = pl.ds(pl.multiple_of(s * rows, reach), reach)
        tail_at = pl.ds(pl.multiple_of(s * rows + rows - reach, reach), reach)
        r.edge_src[0, span(s, reach), :] = r.gatt[tail_at, :]
        r.edge_src[1, span(s, reach), :] = r.gatt[head_at, :]
        for way in range(2):
            r.stat_src[way, s] = total[: 4 * pairs]

    loop(streams, edges)
    stat.start()
    edge.start()

    def attend_back(s):
        allowed = visible(s)
        at = span(s, rows)
        for p in range(pairs):
            scores = nt(r.qs[s, p], r.k2[s, p]) * scale
            grad = r.gatt[at, lanes(p)]
            grad_probs = nt(grad, r.v2[s, p])
            grad_f = grad.astype(F32)
            product = grad_f * r.att[at, lanes(p)].astype(F32)
            agains, grads = [], []
            for h in range(2):
                cut = slice(h * outer, (h + 1) * outer)
                masked = jnp.where(allowed, scores[:, cut], -1e30)
                again = jnp.exp(masked - r.lse[s, 2 * p + h][:, 0:1])
                delta = delta_of(product, h)
                agains.append(again.astype(B16))
                grads.append((again * (grad_probs[:, cut] - delta) * scale).astype(B16))
            grad_query = nn(jnp.concatenate(grads, axis=1), r.k2[s, p])
            grad_keys = nn(jnp.concatenate(grads, axis=0).T, r.q2[s, p])
            grad_values = nn(jnp.concatenate(agains, axis=0).T, halves(grad_f).astype(B16))
            r.gp[at, lanes(p)] = unrotate(
                grad_query, r.cosine[reach : reach + rows], r.sine[reach : reach + rows]
            ).astype(B16)
            for k, value in ((p, grad_keys), (pairs + p, grad_values)):
                r.own_kv[s, :, lanes(k)] = value[reach : reach + rows]

    loop(streams, attend_back)
    relays(put_b1, skip=3)
    down.last()

    def grad_out(m):
        out = nn(r.tt[span(m, TILE), :], r.att[...]).astype(B16)
        r.ga[span(m, blocks), :, quarter:] = out.reshape(blocks, part, quarter)

    loop(tiles, grad_out)

    def grad_query(m):
        out = nn(r.n1t[span(m, TILE), :], r.gp[:, :quarter]).astype(B16)
        r.ga[span(m, blocks), :, :quarter] = out.reshape(blocks, part, quarter)

    loop(tiles, grad_query)
    exchanges([put_a])

    def norm_again(i):
        s, h = i // per, i % per
        x = r.tok_all[s, span(h, CHUNK), :].astype(F32)
        scaled, inverse, _ = norm_forward(x, r.gain[0:1, :])
        r.scaled[span(i, CHUNK), :] = scaled
        r.inverse[span(i, CHUNK), :] = jnp.broadcast_to(inverse, (CHUNK, LANES))

    loop(streams * per, norm_again, UNROLL)
    down.finish()
    steps([put_b1], True, skip=2)
    edge.arrive()
    stat.arrive()

    def join(s):
        allowed = visible_rims(s)
        empty = jnp.zeros((LANES - 4 * pairs, rows), F32)
        before = jnp.concatenate([r.stat_mid[0, s], empty], axis=0).T[rows - reach :]
        after = jnp.concatenate([r.stat_mid[1, s], empty], axis=0).T[:reach]
        stats = jnp.concatenate([before, after], axis=0)
        for p in range(pairs):
            keys, vals = [
                jnp.concatenate(
                    [ref[s, p, h * outer + reach : h * outer + reach + rows] for h in range(2)],
                    axis=0,
                )
                for ref in (r.k2, r.v2)
            ]
            grad = jnp.concatenate(
                [r.edge_mid[way, span(s, reach), lanes(p)] for way in range(2)], axis=0
            )
            scores = nt(r.hq[s, p], keys) * scale
            grad_probs = nt(grad, vals)
            agains, grads = [], []
            for h in range(2):
                k = 2 * p + h
                cut = slice(h * rows, (h + 1) * rows)
                masked = jnp.where(allowed, scores[:, cut], -1e30)
                again = jnp.exp(masked - stats[:, k : k + 1])
                delta = stats[:, 2 * pairs + k : 2 * pairs + k + 1]
                agains.append(again.astype(B16))
                grads.append((again * (grad_probs[:, cut] - delta) * scale).astype(B16))
            grad_keys = nn(jnp.concatenate(grads, axis=0).T, r.hq2[s, p])
            grad_values = nn(
                jnp.concatenate(agains, axis=0).T, halves(grad.astype(F32)).astype(B16)
            )
            grad_keys = unrotate(
                grad_keys + r.own_kv[s, :, lanes(p)],
                r.cosine[reach : reach + rows],
                r.sine[reach : reach + rows],
            )
            grad_values = grad_values + r.own_kv[s, :, lanes(pairs + p)]
            r.gp[span(s, rows), lanes(pairs + p)] = grad_keys.astype(B16)
            r.gp[span(s, rows), lanes(2 * pairs + p)] = grad_values.astype(B16)

    loop(streams, join)

    def grad_pair(i):
        m, j = i // 2, i % 2
        at = pl.ds(pl.multiple_of((j + 1) * quarter, quarter), quarter)
        out = nn(r.n1t[span(m, TILE), :], r.gp[:, at]).astype(B16)
        r.gc[span(m, blocks), :, span(j, quarter)] = out.reshape(blocks, part, quarter)

    loop(tiles * 2, grad_pair)
    steps([put_a], True, stop=1)

    def one_project(j):
        w = r.a_all[span(j, blocks), :, :three].reshape(TILE, three)
        out = nt(r.gp[...], w)
        at = span(j, TILE)
        r.gain_row[0:1, at] = jnp.sum(out * r.scaled[:, at], axis=0, keepdims=True)
        r.src_b[:, :, at] = out.astype(B16).reshape(streams, rows, TILE)

    loop(tiles, one_project)
    for s in range(seq.n):
        k = s * part // LANES
        r.gain_parts[s] = r.gain_row[:, k * LANES : (k + 1) * LANES]
    exchanges([one])
    exchanges([put_g])
    exchanges([put_c])
    put_b2.last()
    put_b1.last()
    steps([one], True)
    steps([put_a], True, skip=1, stop=2)
    steps([put_g], True, stop=1)
    for j in range(main):
        cut = slice(j * LANES, (j + 1) * LANES)
        for k in range(2):
            at = (2 * j + k) * LANES
            r.din[k, cut, :] = db1[:, at : at + LANES].T
        r.ddown_t[cut, :] = db2[:, cut].T
    rim_sum = db1[:, rim_at:].T
    r.din[0, flat:, :] = rim_sum[:tail]
    r.din[1, flat:, :] = rim_sum[tail : 2 * tail]
    r.ddown_t[flat:, :] = rim_sum[2 * tail : 3 * tail]
    steps([put_c], True, stop=1)
    steps([put_a], True, skip=2)
    steps([put_g], True, skip=1, stop=2)
    one.last()

    def final(h):
        at = span(h, CHUNK)
        here = pl.ds(pl.multiple_of(fsdp.me * rows + h * CHUNK, CHUNK), CHUNK)
        got = norm_backward(
            r.one_sum[at, :], r.scaled[here, :], r.inverse[here, 0:1], r.gain[0:1, :]
        )
        r.dinput[at, :] = r.own_grad[at, :] + got
        middle = r.tok[at, :].astype(F32) + r.attn_all[fsdp.me, at, :].astype(F32)
        r.out[at, :] = (middle + r.down_sum[at, :]).astype(B16)

    loop(per, final)
    steps([put_c], True, skip=1, stop=2)
    steps([put_g], True, skip=2)
    put_a.last()
    put_g.last()
    put_g2.start()
    r.dqkv[0] = da[:, :quarter]
    for k in range(pairs):
        at = quarter + k * LANES
        r.dout[k * LANES : (k + 1) * LANES, :] = da[:, at : at + LANES].T
    steps([put_c], True, skip=2)
    steps([put_g2], False)
    put_g2.finish()
    total = r.gain_got[0]
    for f in range(1, fsdp.n):
        total = total + r.gain_got[f]
    total = pltpu.roll(total, (LANES - shift) % LANES, 1)
    r.dgain_one[...] = total[0:1, :piece]
    r.dgain_two[...] = total[1:2, :piece]
    put_c.last()
    r.dqkv[1] = dc[:, :quarter]
    r.dqkv[2] = dc[:, quarter:]
    for job in (edge, stat, one, put_b1, put_b2, put_a, put_c, put_g):
        job.finish()


def run_layer(tok, grd, gain_in, qkv, out_w, in_two, down_t, freq, lengths):
    n, nf = lax.axis_size("seq"), lax.axis_size("fsdp")
    rows, width = tok.shape
    count, part = down_t.shape
    quarter, piece = out_w.shape[0], gain_in.shape[1]
    gain_block = (16, LANES)
    wide_a, wide_2 = 4 * quarter, count // LANES * LANES
    wide_1 = 2 * wide_2 + LANES
    block_c = (part, 2 * quarter)
    block_a, block_1, block_2 = (part, wide_a), (part, wide_1), (part, wide_2)
    pairs = quarter // LANES
    streams = nf
    group = streams * rows
    outer = rows + 2 * WIN
    vmem = pl.BlockSpec(memory_space=pltpu.VMEM)
    ins = [
        ("tok", tok, vmem),
        ("grd", grd, vmem),
        ("gain_in", gain_in, vmem),
        ("qkv", qkv, vmem),
        ("out_w", out_w, vmem),
        ("in_two", in_two, vmem),
        ("down_t", down_t, vmem),
        ("freq", freq, vmem),
        ("lengths", lengths, pl.BlockSpec(memory_space=pltpu.SMEM)),
    ]
    outs = [
        ("out", (rows, width), B16),
        ("dinput", (rows, width), F32),
        ("dgain_one", (1, piece), F32),
        ("dgain_two", (1, piece), F32),
        ("dqkv", (3, part, quarter), F32),
        ("dout", (quarter, part), F32),
        ("din", (2, count, part), F32),
        ("ddown_t", (count, part), F32),
    ]
    plan = Plan()
    token_block = (rows, width)
    for name, count_, shape, dtype in (
        ("tok", nf, token_block, B16),
        ("grd", nf, token_block, B16),
        ("rim", nf, (2, WIN, width), B16),
        ("a", n, block_a, B16),
        ("b1", n, block_1, B16),
        ("b2", n, block_2, B16),
        ("attn", nf, token_block, B16),
        ("back", nf, token_block, B16),
    ):
        plan.vmem(name + "_all", (count_,) + shape, dtype)
        plan.add(name + "_g", *Gather.scratch(count_))
    for name, count_, shape, dtype in (
        ("attn", nf, token_block, B16),
        ("back", nf, token_block, B16),
        ("down", nf, token_block, B16),
        ("one", nf, token_block, B16),
        ("b1", n, block_1, B16),
        ("b2", n, block_2, B16),
        ("a", n, block_c, B16),
        ("c", n, block_c, B16),
        ("gain", n, (8, LANES), F32),
    ):
        plan.add(name + "_r", *Reduce.scratch(count_, shape, dtype))
    plan.add("b1_relay", *Reduce.relay_scratch(block_1, B16))
    plan.vmem("rim_mid", (2, WIN, width), B16)
    plan.add("halo_s", *Halo.scratch())
    plan.vmem("gains", gain_block, B16)
    plan.vmem("gains_mid", (n,) + gain_block, B16)
    plan.add("gains_g", *Gather.scratch(n))
    plan.vmem("gains_all", (nf, n) + gain_block, B16)
    plan.add("gains2_g", *Gather.scratch(nf))
    plan.vmem("gain_mid", (8, LANES), F32)
    plan.vmem("gain_got", (nf, 8, LANES), F32)
    plan.vmem("cosine", (outer, LANES), F32)
    plan.vmem("sine", (outer, LANES), F32)
    plan.add("gain_g", *Gather.scratch(nf))
    plan.add("edge_s", *Halo.scratch())
    plan.add("stat_s", *Halo.scratch())
    for name, shape, dtype in (
        ("edge_src", (2, streams * WIN, quarter), B16),
        ("edge_mid", (2, streams * WIN, quarter), B16),
        ("stat_src", (2, streams, 4 * pairs, LANES), F32),
        ("stat_mid", (2, streams, 4 * pairs, LANES), F32),
        ("hq", (streams, pairs, 2 * WIN, LANES), B16),
        ("hq2", (streams, pairs, 4 * WIN, LANES), B16),
        ("gain", (gain_block[0], width), F32),
        ("gain_row", (8, width), F32),
        ("gain_parts", (n, 8, LANES), F32),
        ("nx", (streams, outer, width), B16),
        ("n1t", (width, group), B16),
        ("gt", (width, group), B16),
        ("tt", (width, group), B16),
        ("qs", (streams, pairs, rows, LANES), B16),
        ("q2", (streams, pairs, 2 * rows, LANES), B16),
        ("k2", (streams, pairs, 2 * outer, LANES), B16),
        ("v2", (streams, pairs, 2 * outer, LANES), B16),
        ("lse", (streams, 2 * pairs, rows, LANES), F32),
        ("att", (group, quarter), B16),
        ("src_a", (streams,) + token_block, B16),
        ("src_b", (streams,) + token_block, B16),
        ("attn_mid", token_block, B16),
        ("back_mid", token_block, B16),
        ("down_sum", token_block, F32),
        ("one_sum", token_block, F32),
        ("scaled", (group, width), F32),
        ("inverse", (group, LANES), F32),
        ("big", (group, 2 * (wide_2 + LANES)), F32),
        ("mix", (group, wide_2 + LANES), B16),
        ("mix_rim", (group, LANES), B16),
        ("dfull", (width, wide_2 + LANES), B16),
        ("gh", (group, wide_1), B16),
        ("gb1", (n,) + block_1, B16),
        ("gb2", (n,) + block_2, B16),
        ("ga", (n,) + block_c, B16),
        ("gc", (n,) + block_c, B16),
        ("own_grad", token_block, F32),
        ("own_kv", (streams, rows, 2 * quarter), F32),
        ("gatt", (group, quarter), B16),
        ("gp", (group, 3 * quarter), B16),
    ):
        plan.vmem(name, shape, dtype)
    names = [i[0] for i in ins] + [o[0] for o in outs] + plan.names
    return pl.pallas_call(
        functools.partial(layer_kernel, tuple(names)),
        out_shape=[jax.ShapeDtypeStruct(s, d) for _, s, d in outs],
        in_specs=[i[2] for i in ins],
        out_specs=[vmem] * len(outs),
        scratch_shapes=plan.shapes,
        compiler_params=pltpu.CompilerParams(
            collective_id=1, has_side_effects=True, vmem_limit_bytes=63 * 1024 * 1024
        ),
    )(*[i[1] for i in ins])


def settle_kernel(*refs):
    count = len(refs) // 2
    copies = [
        pltpu.make_async_copy(*refs[k : 2 * count : count], refs[2 * count].at[k])
        for k in range(count)
    ]
    for copy in copies:
        copy.start()
    for copy in copies:
        copy.wait()


def settle(arrays):
    anywhere = pl.BlockSpec(memory_space=pl.ANY)
    return pl.pallas_call(
        settle_kernel,
        out_shape=[jax.ShapeDtypeStruct(x.shape, x.dtype) for x in arrays],
        in_specs=[anywhere] * len(arrays),
        out_specs=[pl.BlockSpec(memory_space=pltpu.VMEM)] * len(arrays),
        scratch_shapes=[pltpu.SemaphoreType.DMA((len(arrays),))],
    )(*arrays)


def per_device(
    layer_input,
    doc_lengths,
    attn_gain,
    qkv_weight,
    out_weight,
    mlp_gain,
    in_weight,
    down_weight,
    out_grad,
):
    gain_in = jnp.stack([attn_gain, mlp_gain])
    gain_in = jnp.pad(gain_in, ((0, 6), (0, 0)))
    half = np.arange(LANES)[None, :] % (HEAD // 2)
    freq = 10000.0 ** (-(2.0 / HEAD) * half)
    made = run_layer(
        layer_input[0],
        out_grad[0],
        gain_in,
        qkv_weight.transpose(1, 0, 2),
        out_weight,
        in_weight.transpose(1, 2, 0),
        down_weight.T,
        jnp.asarray(freq, F32),
        doc_lengths,
    )
    output, input_grad, dgain_one, dgain_two, dqkv, dout, din, ddown_t = settle(made)
    return (
        output[None],
        input_grad[None],
        dgain_one[0],
        dqkv.transpose(1, 0, 2),
        dout,
        dgain_two[0],
        din.transpose(2, 0, 1),
        ddown_t.T,
    )


def solution(mesh):
    in_specs = (
        P("fsdp", "seq", None),
        P(),
        P(("seq", "fsdp")),
        P("seq", None, "fsdp"),
        P("fsdp", "seq"),
        P(("seq", "fsdp")),
        P("seq", None, "fsdp"),
        P("seq", "fsdp"),
        P("fsdp", "seq", None),
    )
    out_specs = (
        P("fsdp", "seq", None),
        P("fsdp", "seq", None),
        P(("seq", "fsdp")),
        P("seq", None, "fsdp"),
        P("fsdp", "seq"),
        P(("seq", "fsdp")),
        P("seq", None, "fsdp"),
        P("seq", "fsdp"),
    )
    return jax.shard_map(
        per_device, mesh=mesh, in_specs=in_specs, out_specs=out_specs, check_vma=False
    )
```

```python
import functools

import jax
import jax.numpy as jnp
import numpy as np
from jax import lax
from jax.experimental import pallas as pl
from jax.experimental.pallas import tpu as pltpu
from jax.sharding import PartitionSpec as P

HEAD = 64
WIN = 64


EPSILON = 1e-05


class Place:
    def __init__(self, axis):
        self.axis = axis
        self.n = lax.axis_size(axis)
        self.length = self.n // 2
        me = lax.axis_index(axis)
        self.me = me
        self.at = me // 2
        self.side = me % 2

    def partner(self):
        return {self.axis: self.at * 2 + (1 - self.side)}

    def right(self):
        return {self.axis: self.me + 2}

    def left(self):
        return {self.axis: self.me - 2}

    def has_right(self):
        return self.at < self.length - 1

    def has_left(self):
        return self.at > 0

    def greet(self, barrier):
        mesh = pl.DeviceIdType.MESH
        pl.semaphore_signal(barrier, inc=1, device_id=self.partner(), device_id_type=mesh)

        @pl.when(self.has_left())
        def _():
            pl.semaphore_signal(barrier, inc=1, device_id=self.left(), device_id_type=mesh)

        @pl.when(self.has_right())
        def _():
            pl.semaphore_signal(barrier, inc=1, device_id=self.right(), device_id_type=mesh)

    def diagonal(self):
        there = jnp.where(self.side == 1, self.has_right(), self.has_left())
        return there, {self.axis: self.me + 2 * self.side - 1}

    def peers(self):
        one, none = jnp.int32(1), jnp.int32(0)
        return 1 + jnp.where(self.has_left(), one, none) + jnp.where(self.has_right(), one, none)


def when(condition, action):
    if condition is True:
        action()
    else:
        pl.when(condition)(action)


def remote(src, dst, send, recv, device):
    return pltpu.make_async_remote_copy(
        src_ref=src,
        dst_ref=dst,
        send_sem=send,
        recv_sem=recv,
        device_id=device,
        device_id_type=pl.DeviceIdType.MESH,
    )


class Gather:
    scratch = staticmethod(
        lambda n: [
            pltpu.SemaphoreType.DMA((3, n)),
            pltpu.SemaphoreType.DMA((n,)),
            pltpu.SemaphoreType.DMA,
        ]
    )

    def __init__(self, place, src, dst, sems, relayed=False):
        self.place, self.src, self.dst = place, src, dst
        self.send, self.recv, self.local = sems
        self.relayed = relayed

    def crosses(self, i):
        if not self.relayed:
            return True
        inner = jnp.logical_and(i > 0, i < self.place.length - 1)
        return jnp.logical_or(inner, i == self.place.at)

    def relay(self, d):
        place = self.place
        ends = ((d, 0, 1), (place.length - 1 - d, place.length - 1, 2))
        for at, end, way in ends:
            block = 2 * end + 1 - place.side

            @pl.when(place.at == at)
            def _(block=block, way=way):
                self.copy(0, block, place.partner()).wait_recv()
                (self.ahead if way == 1 else self.behind)(block, False, lambda c: c.start())

    def copy(self, way, block, device, own=False):
        src = self.src if own else self.dst.at[block]
        return remote(src, self.dst.at[block], self.send.at[way, block], self.recv.at[block], device)

    def onward(self, block, own, act):
        place = self.place
        act(self.copy(0, block, place.partner(), own))

    def start(self):
        place = self.place
        if self.src is not None:
            pltpu.make_async_copy(self.src, self.dst.at[place.me], self.local).start()
        self.start_lines()
        self.start_across()

    def start_lines(self):
        place = self.place
        self.ahead(place.me, self.src is not None, lambda c: c.start())
        self.behind(place.me, self.src is not None, lambda c: c.start())

    def start_across(self):
        self.onward(self.place.me, self.src is not None, lambda c: c.start())

    def ahead(self, block, own, act):
        place = self.place

        @pl.when(place.has_right())
        def _():
            act(self.copy(1, block, place.right(), own))

    def behind(self, block, own, act):
        place = self.place

        @pl.when(place.has_left())
        def _():
            act(self.copy(2, block, place.left(), own))

    def step(self, d):
        place = self.place

        @pl.when(place.at - d >= 0)
        def _():
            block = place.me - 2 * d
            self.copy(1, block, place.partner()).wait_recv()
            self.ahead(block, False, lambda c: c.start())
            when(
                self.crosses(place.at - d),
                lambda: self.onward(block, False, lambda c: c.start()),
            )

        @pl.when(place.at + d < place.length)
        def _():
            block = place.me + 2 * d
            self.copy(2, block, place.partner()).wait_recv()
            self.behind(block, False, lambda c: c.start())
            when(
                self.crosses(place.at + d),
                lambda: self.onward(block, False, lambda c: c.start()),
            )

    def finish(self):
        place = self.place
        if self.src is not None:
            pltpu.make_async_copy(self.src, self.dst.at[place.me], self.local).wait()

        def arrived(i, carry):
            inner = True
            if self.relayed:
                inner = jnp.logical_and(i > 0, i < place.length - 1)
            when(
                inner,
                lambda: self.copy(0, 2 * i + 1 - place.side, place.partner()).wait_recv(),
            )
            when(
                self.crosses(i),
                lambda: self.onward(2 * i + place.side, False, lambda c: c.wait_send()),
            )

            @pl.when(i <= place.at)
            def _():
                self.ahead(2 * i + place.side, False, lambda c: c.wait_send())

            @pl.when(i >= place.at)
            def _():
                self.behind(2 * i + place.side, False, lambda c: c.wait_send())

            return carry

        lax.fori_loop(0, place.length, arrived, 0)
        if self.relayed:
            self.ahead(1 - place.side, False, lambda c: c.wait_send())
            self.behind(2 * place.length - 1 - place.side, False, lambda c: c.wait_send())


class Reduce:
    @staticmethod
    def scratch(n, block, dtype):
        length = n // 2
        return [
            pltpu.VMEM((length,) + block, dtype),
            pltpu.VMEM((length + 1,) + block, dtype),
            pltpu.SemaphoreType.DMA((2, length)),
            pltpu.SemaphoreType.DMA((length,)),
            pltpu.SemaphoreType.DMA((length + 1,)),
        ]

    @staticmethod
    def relay_scratch(block, dtype):
        return [
            pltpu.VMEM((2,) + block, dtype),
            pltpu.SemaphoreType.DMA((2,)),
            pltpu.SemaphoreType.DMA((2,)),
        ]

    def __init__(self, place, src, dst, scratch, relays=None):
        self.place, self.src, self.dst = place, src, dst
        self.paired, self.lined, self.send, self.pair_recv, self.line_recv = scratch
        self.relays = relays

    def crosses(self, i):
        if self.relays is None:
            return True
        return jnp.logical_and(i > 0, i < self.place.length - 1)

    def pass_on(self, end, device):
        held, send, recv = self.relays
        block = 2 * (end * (self.place.length - 1)) + 1 - self.place.side
        return self.src.at[block], remote(
            self.src.at[block], held.at[end], send.at[end], recv.at[end], device
        )

    def relay(self, d):
        place = self.place
        finish = place.length - 1
        for end, at in ((0, finish - d), (1, d)):
            device = place.right() if end else place.left()
            final = finish if end else 0

            @pl.when(place.at == at)
            def _(end=end, device=device, final=final):
                block, copy = self.pass_on(end, device)

                @pl.when(d > 0)
                def _():
                    copy.wait_recv()
                    self.add(block, [block, self.relays[0].at[end]])

                @pl.when(place.at != final)
                def _():
                    copy.start()

                @pl.when(place.at == final)
                def _():
                    self.across(final).start()

    def mine(self, i):
        return self.src.at[2 * i + self.place.side]

    def across(self, i):
        place = self.place
        return remote(
            self.src.at[2 * i + 1 - place.side],
            self.paired.at[i],
            self.send.at[0, i],
            self.pair_recv.at[i],
            place.partner(),
        )

    def along(self, i, slot, device):
        return remote(
            self.mine(i), self.lined.at[slot], self.send.at[1, i], self.line_recv.at[slot], device
        )

    def exchange(self, d):
        place = self.place

        @pl.when(place.at + d < place.length)
        def _():
            when(self.crosses(place.at + d), lambda: self.across(place.at + d).start())

        @pl.when(jnp.logical_and(d > 0, place.at - d >= 0))
        def _():
            when(self.crosses(place.at - d), lambda: self.across(place.at - d).start())

    def add(self, out, refs):
        rows = out.shape[0]
        tile = 16 if rows % 16 == 0 else 8

        def each(i, carry):
            at = pl.ds(pl.multiple_of(i * tile, tile), tile)
            total = refs[0][at, :].astype(jnp.float32)
            for ref in refs[1:]:
                total = total + ref[at, :].astype(jnp.float32)
            out[at, :] = total.astype(out.dtype)
            return carry

        lax.fori_loop(0, rows // tile, each, 0)

    def own(self, i):
        self.across(i).wait_recv()
        return [self.mine(i), self.paired.at[i]]

    def combine(self, i, paired, lined):
        def total(pair):
            refs = self.own(i) if pair else [self.mine(i)]

            @pl.when(lined)
            def _():
                self.along(i, i, self.place.partner()).wait_recv()
                self.add(self.mine(i), refs + [self.lined.at[i]])

            if pair:

                @pl.when(jnp.logical_not(lined))
                def _():
                    self.add(self.mine(i), refs)

        when(paired, lambda: total(True))
        if paired is not True:
            pl.when(jnp.logical_not(paired))(lambda: total(False))

    def step(self, d):
        place = self.place

        @pl.when(place.at + d < place.length)
        def _():
            i = place.at + d
            self.combine(i, self.crosses(i), place.has_left())
            self.along(i, i, place.right()).start()

        @pl.when(place.at - d >= 0)
        def _():
            i = place.at - d
            self.combine(i, self.crosses(i), place.has_right())
            slot = jnp.where(d == 1, place.length, i)
            self.along(i, slot, place.left()).start()

    def last(self):
        place = self.place
        i, extra = place.at, place.length
        refs = self.own(i)

        @pl.when(place.has_left())
        def _():
            self.along(i, i, place.partner()).wait_recv()

        @pl.when(place.has_right())
        def _():
            self.along(i, extra, place.partner()).wait_recv()

        both = jnp.logical_and(place.has_left(), place.has_right())

        @pl.when(both)
        def _():
            self.add(self.dst, refs + [self.lined.at[i], self.lined.at[extra]])

        @pl.when(jnp.logical_and(place.has_left(), jnp.logical_not(both)))
        def _():
            self.add(self.dst, refs + [self.lined.at[i]])

        @pl.when(jnp.logical_and(place.has_right(), jnp.logical_not(both)))
        def _():
            self.add(self.dst, refs + [self.lined.at[extra]])

    def finish(self):
        place = self.place

        def each(i, carry):
            crosses = self.crosses(i)
            if crosses is not True:
                crosses = jnp.logical_or(crosses, i == place.at)
            when(crosses, lambda: self.across(i).wait_send())

            @pl.when(i != place.at)
            def _():
                self.along(i, i, place.partner()).wait_send()

            return carry

        lax.fori_loop(0, place.length, each, 0)
        if self.relays is not None:

            @pl.when(place.has_left())
            def _():
                self.pass_on(0, place.left())[1].wait_send()

            @pl.when(place.has_right())
            def _():
                self.pass_on(1, place.right())[1].wait_send()


class Halo:
    scratch = staticmethod(lambda: [pltpu.SemaphoreType.DMA((2,)), pltpu.SemaphoreType.DMA((2,))])

    def __init__(self, place, src, mid, sems):
        self.place, self.src, self.mid = place, src, mid
        self.send, self.recv = sems
        self.after = place.me < place.n - 1
        self.before = place.me > 0

    def copy(self, way):
        rows, width = self.src.shape[0], self.mid.shape[1]
        at = rows - width if way == 0 else 0
        other = {self.place.axis: self.place.me + 1 - 2 * way}
        return remote(
            self.src.at[pl.ds(at, width)],
            self.mid.at[way],
            self.send.at[way],
            self.recv.at[way],
            other,
        )

    def start(self):
        @pl.when(self.after)
        def _():
            self.copy(0).start()

        @pl.when(self.before)
        def _():
            self.copy(1).start()

        @pl.when(jnp.logical_not(self.before))
        def _():
            self.mid[0] = jnp.zeros(self.mid.shape[1:], self.mid.dtype)

        @pl.when(jnp.logical_not(self.after))
        def _():
            self.mid[1] = jnp.zeros(self.mid.shape[1:], self.mid.dtype)

    def arrive(self):
        @pl.when(self.before)
        def _():
            self.copy(0).wait_recv()

        @pl.when(self.after)
        def _():
            self.copy(1).wait_recv()

    def finish(self):
        @pl.when(self.after)
        def _():
            self.copy(0).wait_send()

        @pl.when(self.before)
        def _():
            self.copy(1).wait_send()


def greet_all(places, slanted):
    barrier = pltpu.get_barrier_semaphore()
    extra = jnp.int32(0)
    if slanted:
        there, device = places[0].diagonal()
        extra = jnp.where(there, jnp.int32(1), jnp.int32(0))

        @pl.when(there)
        def _():
            pl.semaphore_signal(
                barrier, inc=1, device_id=device, device_id_type=pl.DeviceIdType.MESH
            )

    for place in places:
        place.greet(barrier)
    pl.semaphore_wait(barrier, extra + sum(place.peers() for place in places))


def steps(jobs, down, skip=0, stop=None):
    length = jobs[0].place.length
    stop = length - 1 if stop is None else min(stop, length - 1)

    def each(k, carry):
        d = length - 1 - k if down else k + 1
        for job in jobs:
            job.step(d)
        return carry

    if skip < stop:
        lax.fori_loop(skip, stop, each, 0)


def relays(job, skip=0, stop=None):
    length = job.place.length
    stop = length if stop is None else stop

    def each(k, carry):
        job.relay(k)
        return carry

    lax.fori_loop(skip, stop, each, 0)


def exchanges(jobs, skip=0, stop=None):
    length = jobs[0].place.length
    stop = length if stop is None else stop

    def each(k, carry):
        for job in jobs:
            job.exchange(length - 1 - k)
        return carry

    lax.fori_loop(skip, stop, each, 0)


B16, F32 = jnp.bfloat16, jnp.float32
LANES = 128
TILE = 256
CHUNK = 32
UNROLL = 4


class Edge(Halo):
    def copy(self, way):
        other = {self.place.axis: self.place.me + 1 - 2 * way}
        return remote(
            self.src.at[way], self.mid.at[way], self.send.at[way], self.recv.at[way], other
        )


class Plan:
    def __init__(self):
        self.names, self.shapes = [], []

    def add(self, name, *items):
        self.names += [name] * len(items)
        self.shapes += items

    def vmem(self, name, shape, dtype):
        self.add(name, pltpu.VMEM(shape, dtype))


class Refs:
    def __init__(self, names, refs):
        self.groups = {}
        for name, ref in zip(names, refs):
            self.groups.setdefault(name, []).append(ref)

    def __getattr__(self, name):
        return self.groups[name][0]

    def all(self, name):
        return self.groups[name]


def nn(left, right):
    return jnp.dot(left, right, preferred_element_type=F32)


def nt(left, right):
    return lax.dot_general(left, right, (((1,), (1,)), ((), ())), preferred_element_type=F32)


def loop(count, body, unroll=1):
    def each(i, carry):
        for k in range(unroll):
            body(i * unroll + k)
        return carry

    lax.fori_loop(0, count // unroll, each, 0)


def span(i, width):
    return pl.ds(pl.multiple_of(i * width, width), width)


def norm_forward(values, gain):
    mean = jnp.mean(values, axis=-1, keepdims=True)
    centred = values - mean
    inverse = lax.rsqrt(jnp.mean(centred * centred, axis=-1, keepdims=True) + EPSILON)
    scaled = centred * inverse
    return (scaled, inverse, (scaled * gain).astype(B16))


def norm_backward(grad, scaled, inverse, gain):
    weighted = grad * gain
    return inverse * (
        weighted
        - jnp.mean(weighted, axis=-1, keepdims=True)
        - scaled * jnp.mean(weighted * scaled, axis=-1, keepdims=True)
    )


def gelu_parts(inner):
    cdf = 0.5 * (1.0 + lax.erf(inner * 0.7071067811865476))
    density = jnp.exp(-0.5 * inner * inner) * 0.3989422804014327
    return (inner * cdf, cdf + inner * density)


def swap(field):
    lane = lax.broadcasted_iota(jnp.int32, field.shape, 1)
    half = HEAD // 2
    return jnp.where(
        lane % HEAD < half, pltpu.roll(field, LANES - half, 1), pltpu.roll(field, half, 1)
    )


def rotate(field, cosine, sine):
    return field * cosine + swap(field) * sine


def unrotate(field, cosine, sine):
    return field * cosine - swap(field) * sine


def halves(field):
    lane = lax.broadcasted_iota(jnp.int32, field.shape, 1)
    low = lane < HEAD
    zero = jnp.zeros_like(field)
    return jnp.concatenate([jnp.where(low, field, zero), jnp.where(low, zero, field)], axis=0)


def layer_kernel(names, *refs):
    r = Refs(names, refs)
    seq, fsdp = Place("seq"), Place("fsdp")
    rows, width = r.tok.shape
    count = r.down_t.shape[0]
    streams = r.tok_all.shape[0]
    group = streams * rows
    quarter = r.att.shape[1]
    pairs = quarter // LANES
    part = r.a_all.shape[1]
    reach, outer = WIN, rows + 2 * WIN
    main = count // LANES
    tail = count - main * LANES
    flat = main * LANES
    rim_at = 2 * flat
    blocks = TILE // part
    tiles = width // TILE
    per = rows // CHUNK
    scale = HEAD**-0.5
    three = 3 * quarter
    half_streams = TILE // rows

    tokens = Gather(fsdp, r.tok, r.tok_all, r.all("tok_g"))
    cots = Gather(fsdp, r.grd, r.grd_all, r.all("grd_g"))
    halo = Halo(seq, r.tok, r.rim_mid, r.all("halo_s"))
    rim = Gather(fsdp, r.rim_mid, r.rim_all, r.all("rim_g"))
    gains = Gather(seq, r.gains, r.gains_mid, r.all("gains_g"))
    gains2 = Gather(fsdp, r.gains_mid, r.gains_all, r.all("gains2_g"))
    get_a = Gather(seq, None, r.a_all, r.all("a_g"), True)
    get_b1 = Gather(seq, None, r.b1_all, r.all("b1_g"))
    get_b2 = Gather(seq, None, r.b2_all, r.all("b2_g"))
    attn = Reduce(fsdp, r.src_a, r.attn_mid, r.all("attn_r"))
    attn2 = Gather(fsdp, r.attn_mid, r.attn_all, r.all("attn_g"))
    back = Reduce(fsdp, r.src_a, r.back_mid, r.all("back_r"))
    back2 = Gather(fsdp, r.back_mid, r.back_all, r.all("back_g"))
    down = Reduce(fsdp, r.src_b, r.down_sum, r.all("down_r"))
    one = Reduce(fsdp, r.src_b, r.one_sum, r.all("one_r"))
    db1 = r.big.at[0:part, 0 : rim_at + LANES]
    db2 = r.big.at[part : 2 * part, 0:flat]
    da = r.big.at[2 * part : 3 * part, 0 : 2 * quarter]
    dc = r.big.at[2 * part : 3 * part, 2 * quarter : 4 * quarter]
    put_b1 = Reduce(seq, r.gb1, db1, r.all("b1_r"), r.all("b1_relay"))
    put_b2 = Reduce(seq, r.gb2, db2, r.all("b2_r"))
    put_a = Reduce(seq, r.ga, da, r.all("a_r"))
    put_c = Reduce(seq, r.gc, dc, r.all("c_r"))
    put_g = Reduce(seq, r.gain_parts, r.gain_mid, r.all("gain_r"))
    put_g2 = Gather(fsdp, r.gain_mid, r.gain_got, r.all("gain_g"))
    edge = Edge(seq, r.edge_src, r.edge_mid, r.all("edge_s"))
    stat = Edge(seq, r.stat_src, r.stat_mid, r.all("stat_s"))

    piece = r.gain_in.shape[1]
    shift = (seq.me * fsdp.n + fsdp.me) * piece % LANES
    filled = [jnp.zeros((8, LANES - piece), F32)] if piece < LANES else []
    wide = jnp.concatenate([r.gain_in[...].astype(F32)] + filled, axis=1)
    wide = jnp.concatenate([pltpu.roll(wide, shift, 1), jnp.zeros((8, LANES), F32)], axis=0)
    r.gains[...] = wide.astype(B16)
    for k in range(3):
        r.a_all[seq.me, :, k * quarter : (k + 1) * quarter] = r.qkv[k]
    for k in range(pairs):
        at = three + k * LANES
        r.a_all[seq.me, :, at : at + LANES] = r.out_w[k * LANES : (k + 1) * LANES, :].T
    greet_all((seq, fsdp), True)
    for job in (gains, get_a, tokens, halo):
        job.start()

    for j in range(main):
        cut = slice(j * LANES, (j + 1) * LANES)
        for k in range(2):
            at = (2 * j + k) * LANES
            r.b1_all[seq.me, :, at : at + LANES] = r.in_two[k, cut, :].T
        r.b2_all[seq.me, :, cut] = r.down_t[cut, :].T
    last = [r.in_two[0, flat:, :], r.in_two[1, flat:, :], r.down_t[flat:, :]]
    last.append(jnp.zeros((LANES - 3 * tail, part), B16))
    r.b1_all[seq.me, :, rim_at:] = jnp.concatenate(last, axis=0).T

    steps([gains, get_a], False, stop=1)
    relays(get_a, stop=1)
    halo.arrive()
    rim.start()
    steps([tokens], False)
    place = seq.me * rows - reach + lax.broadcasted_iota(jnp.int32, (outer, LANES), 0)
    spot = lax.broadcasted_iota(jnp.int32, (outer, LANES), 1) % HEAD
    angle = place.astype(F32) * r.freq[...]
    r.cosine[...] = jnp.cos(angle)
    sine = jnp.sin(angle)
    r.sine[...] = jnp.where(spot < HEAD // 2, -sine, sine)
    steps([gains, get_a], False, skip=1, stop=2)
    relays(get_a, skip=1, stop=2)
    steps([rim], False)
    steps([gains, get_a], False, skip=2)
    relays(get_a, skip=2, stop=3)
    get_b1.start_lines()
    get_b1.start_across()
    gains.finish()
    gains2.start()
    cots.start()
    steps([gains2], False)
    gains2.finish()

    for k in range(width // LANES):
        total = jnp.zeros((r.gains.shape[0], LANES), F32)
        for s in range(k * LANES // part, (k + 1) * LANES // part):
            for f in range(streams):
                total = total + r.gains_all[f, s].astype(F32)
        r.gain[:, k * LANES : (k + 1) * LANES] = total
    tokens.finish()
    rim.finish()
    halo.finish()

    def norm_own(i):
        s, h = i // per, i % per
        x = r.tok_all[s, span(h, CHUNK), :].astype(F32)
        at = pl.ds(pl.multiple_of(reach + h * CHUNK, CHUNK), CHUNK)
        r.nx[s, at, :] = norm_forward(x, r.gain[0:1, :])[2]

    loop(streams * per, norm_own, UNROLL)

    rims = reach // CHUNK

    def norm_rim(i):
        s, w, h = i // (2 * rims), i // rims % 2, i % rims
        x = r.rim_all[s, w, span(h, CHUNK), :].astype(F32)
        at = pl.ds(pl.multiple_of(w * (rows + reach) + h * CHUNK, CHUNK), CHUNK)
        r.nx[s, at, :] = norm_forward(x, r.gain[0:1, :])[2]

    loop(streams * 2 * rims, norm_rim, UNROLL)

    def turn_one(i):
        x = r.nx[:, reach : reach + rows, span(i, LANES)].reshape(group, LANES)
        r.n1t[span(i, LANES), :] = x.T

    def turn_grad(i):
        x = r.grd_all[:, :, span(i, LANES)].reshape(group, LANES)
        r.gt[span(i, LANES), :] = x.T

    relays(get_a, skip=3)
    get_a.finish()

    band = jnp.abs(
        lax.broadcasted_iota(jnp.int32, (rows, outer), 0)
        + reach
        - lax.broadcasted_iota(jnp.int32, (rows, outer), 1)
    )

    def lanes(p):
        return slice(p * LANES, (p + 1) * LANES)

    def project(s):
        x = r.nx[s]
        out = nn(x, r.a_all[:, :, quarter:three].reshape(width, 2 * quarter))
        for p in range(pairs):
            keys = rotate(out[:, lanes(p)], r.cosine[...], r.sine[...])
            r.k2[s, p] = halves(keys).astype(B16)
            r.v2[s, p] = halves(out[:, lanes(pairs + p)]).astype(B16)
        out = nn(x, r.a_all[:, :, :quarter].reshape(width, quarter))
        for p in range(pairs):
            query = rotate(out[:, lanes(p)], r.cosine[...], r.sine[...])
            own = query[reach : reach + rows]
            rims = jnp.concatenate([query[:reach], query[reach + rows :]], axis=0)
            r.qs[s, p] = own.astype(B16)
            r.q2[s, p] = halves(own).astype(B16)
            r.hq[s, p] = rims.astype(B16)
            r.hq2[s, p] = halves(rims).astype(B16)

    loop(streams // 2, project)
    steps([get_b1], False, stop=1)
    loop(streams - streams // 2, lambda i: project(i + streams // 2))

    def documents(s, place):
        docs = r.lengths.shape[1]
        ids = jnp.zeros(place.shape, jnp.int32)
        start = jnp.int32(0)
        for k in range(docs + 1):
            ids = ids + (place >= start).astype(jnp.int32)
            if k < docs:
                start = start + r.lengths[s, k]
        return ids

    first = seq.me * rows

    def visible(s):
        across = first - reach + lax.broadcasted_iota(jnp.int32, (1, outer), 1)
        along = first + lax.broadcasted_iota(jnp.int32, (rows, 1), 0)
        return (band <= reach) & (documents(s, along) == documents(s, across))

    def visible_rims(s):
        along = lax.broadcasted_iota(jnp.int32, (2 * reach, 1), 0)
        along = first + jnp.where(along < reach, along - reach, along - reach + rows)
        across = first + lax.broadcasted_iota(jnp.int32, (1, rows), 1)
        near = jnp.abs(along - across) <= reach
        return near & (documents(s, along) == documents(s, across))

    def delta_of(product, h):
        low = lax.broadcasted_iota(jnp.int32, product.shape, 1) < HEAD
        zero = jnp.zeros_like(product)
        side = jnp.where(low, product, zero) if h == 0 else jnp.where(low, zero, product)
        return jnp.sum(side, axis=-1, keepdims=True)

    def attend(s):
        allowed = visible(s)
        for p in range(pairs):
            scores = nt(r.qs[s, p], r.k2[s, p]) * scale
            probs = []
            for h in range(2):
                masked = jnp.where(allowed, scores[:, h * outer : (h + 1) * outer], -1e30)
                top = jnp.max(masked, axis=-1, keepdims=True)
                expd = jnp.exp(masked - top)
                total = jnp.sum(expd, axis=-1, keepdims=True)
                r.lse[s, 2 * p + h] = jnp.broadcast_to(top + jnp.log(total), (rows, LANES))
                probs.append((expd / total).astype(B16))
            out = nn(jnp.concatenate(probs, axis=1), r.v2[s, p])
            r.att[span(s, rows), lanes(p)] = out.astype(B16)

    loop(streams, attend)
    steps([get_b1], False, skip=1, stop=2)
    get_b2.start_lines()

    def out_project(j):
        w = r.a_all[span(j, blocks), :, three:].reshape(TILE, quarter)
        out = nt(r.att[...], w).astype(B16)
        r.src_a[:, :, span(j, TILE)] = out.reshape(streams, rows, TILE)

    loop(tiles, out_project)
    exchanges([attn])
    steps([attn], True)
    steps([cots], False)
    loop(width // LANES, turn_one)
    cots.finish()
    steps([get_b1], False, skip=2)
    get_b2.start_across()
    attn.last()
    attn2.start()
    loop(width // LANES, turn_grad)
    steps([get_b2], False, stop=1)
    steps([attn2], False)
    steps([get_b2], False, skip=1, stop=2)
    attn2.finish()
    attn.finish()
    steps([get_b2], False, skip=2)

    def norm_two(i):
        s, h = i // per, i % per
        at = span(h, CHUNK)
        x = r.tok_all[s, at, :].astype(F32) + r.attn_all[s, at, :].astype(F32)
        scaled, inverse, normed = norm_forward(x, r.gain[1:2, :])
        r.scaled[span(i, CHUNK), :] = scaled
        r.inverse[span(i, CHUNK), :] = jnp.broadcast_to(inverse, (CHUNK, LANES))
        r.nx[s, pl.ds(pl.multiple_of(rows + h * CHUNK, CHUNK), CHUNK), :] = normed

    loop(streams * per, norm_two, UNROLL)

    def normed_two(m):
        return r.nx[span(m, half_streams), rows : 2 * rows, :].reshape(TILE, width)

    def turn_two(i):
        x = r.nx[:, rows : 2 * rows, span(i, LANES)].reshape(group, LANES)
        r.tt[span(i, LANES), :] = x.T

    loop(width // LANES, turn_two)
    get_b1.finish()

    sides = group // TILE
    rest = flat + LANES

    def hidden(i):
        m, j = i // main, i % main
        w = r.b1_all[:, :, span(j, TILE)].reshape(width, TILE)
        out = nn(normed_two(m), w)
        inner, gate = out[:, :LANES], out[:, LANES:]
        activated, slope = gelu_parts(inner)
        at = span(m, TILE)
        r.big[at, span(j, LANES)] = activated
        r.big[at, pl.ds(pl.multiple_of(rest + j * LANES, LANES), LANES)] = gate * slope
        r.mix[at, span(j, LANES)] = (activated * gate).astype(B16)

    loop(sides * main, hidden)
    lane = lax.broadcasted_iota(jnp.int32, (TILE, LANES), 1)

    def hidden_rim(m):
        w = r.b1_all[:, :, rim_at:].reshape(width, LANES)
        inner = nn(normed_two(m), w)
        gate = pltpu.roll(inner, LANES - tail, 1)
        activated, slope = gelu_parts(inner)
        at = span(m, TILE)
        zero = jnp.zeros((TILE, LANES), F32)
        mixed = jnp.where(lane < tail, activated * gate, zero)
        r.big[at, flat:rest] = jnp.where(lane < tail, activated, zero)
        r.big[at, rest + flat :] = jnp.where(lane < tail, gate * slope, zero)
        r.mix[at, flat:] = mixed.astype(B16)
        r.mix_rim[at, :] = pltpu.roll(mixed, 2 * tail, 1).astype(B16)

    loop(sides, hidden_rim)

    def grad_down(m):
        out = nn(r.gt[span(m, TILE), :], r.mix[:, :flat]).astype(B16)
        r.gb2[span(m, blocks), :, :] = out.reshape(blocks, part, flat)

    loop(tiles, grad_down)
    get_b2.finish()
    exchanges([put_b2])

    def unpack(j):
        at = span(j, TILE)
        r.dfull[at, :flat] = r.b2_all[span(j, blocks), :, :].reshape(TILE, flat)
        x = r.b1_all[span(j, blocks), :, rim_at:].reshape(TILE, LANES).astype(F32)
        x = jnp.where(lane < tail, pltpu.roll(x, LANES - 2 * tail, 1), jnp.zeros_like(x))
        r.dfull[at, flat:] = x.astype(B16)

    loop(tiles, unpack)

    def grad_hidden(m, t, grad):
        at = span(m, TILE)
        inner = grad * r.big[at, pl.ds(pl.multiple_of(rest + t * LANES, LANES), LANES)]
        gate = grad * r.big[at, span(t, LANES)]
        return at, inner, gate

    def grad_mixed(m, first, tiles_of):
        g = r.grd_all[span(m, half_streams)].reshape(TILE, width)
        wide = len(tiles_of) * LANES
        grads = nn(g, r.dfull[:, pl.ds(first, wide)])
        for k, t in enumerate(tiles_of):
            at, inner, gate = grad_hidden(m, t, grads[:, k * LANES : (k + 1) * LANES])
            if t is main:
                r.gh[at, rim_at:] = (inner + pltpu.roll(gate, tail, 1)).astype(B16)
            else:
                r.gh[at, span(2 * t, LANES)] = inner.astype(B16)
                r.gh[at, span(2 * t + 1, LANES)] = gate.astype(B16)

    twos = main // 2

    def grad_two(i):
        m, j = i // twos, i % twos
        grad_mixed(m, pl.multiple_of(j * 2 * LANES, 2 * LANES), [2 * j, 2 * j + 1])

    loop(sides * twos, grad_two)
    loop(sides, lambda m: grad_mixed(m, 2 * twos * LANES, list(range(2 * twos, main)) + [main]))
    steps([put_b2], True, stop=1)

    r.gain_row[...] = jnp.zeros(r.gain_row.shape, F32)

    def back_project(j):
        w = r.b1_all[span(j, blocks)].reshape(TILE, rim_at + LANES)
        out = nt(r.gh[...], w)
        at = span(j, TILE)
        r.gain_row[1:2, at] = jnp.sum(out * r.scaled[:, at], axis=0, keepdims=True)
        r.src_a[:, :, at] = out.astype(B16).reshape(streams, rows, TILE)

    loop(tiles, back_project)
    exchanges([back])

    def grad_in(i):
        m, j = i // main, i % main
        out = nn(r.tt[span(m, 2 * TILE), :], r.gh[:, span(j, TILE)]).astype(B16)
        r.gb1[span(m, 2 * blocks), :, span(j, TILE)] = out.reshape(2 * blocks, part, TILE)

    part_way = tiles // 2 * main // 2
    loop(part_way, grad_in)
    steps([back], True)
    loop(tiles // 2 * main - part_way, lambda i: grad_in(i + part_way))

    def grad_in_rim(m):
        at = span(m, TILE)
        out = nn(r.tt[at, :], r.gh[:, rim_at:]) + nn(r.gt[at, :], r.mix_rim[...])
        r.gb1[span(m, blocks), :, rim_at:] = out.astype(B16).reshape(blocks, part, LANES)

    loop(tiles, grad_in_rim)
    relays(put_b1, stop=1)
    exchanges([put_b1])
    def down_project(j):
        out = nt(r.mix[...], r.dfull[span(j, TILE), :]).astype(B16)
        r.src_b[:, :, span(j, TILE)] = out.reshape(streams, rows, TILE)

    loop(tiles, down_project)
    exchanges([down])
    steps([put_b2], True, skip=1, stop=2)
    back.last()
    back2.start()
    relays(put_b1, skip=1, stop=2)
    steps([put_b2], True, skip=2)
    steps([put_b1], True, stop=1)
    steps([down], True)
    steps([back2], False)
    back2.finish()
    back.finish()

    def middle_grad(i):
        s, h = i // per, i % per
        at = span(h, CHUNK)
        here = span(i, CHUNK)
        got = norm_backward(
            r.back_all[s, at, :].astype(F32),
            r.scaled[here, :],
            r.inverse[here, 0:1],
            r.gain[1:2, :],
        )
        grad = r.grd_all[s, at, :].astype(F32) + got
        r.nx[s, at, :] = grad.astype(B16)

        @pl.when(s == fsdp.me)
        def _():
            r.own_grad[at, :] = grad

    relays(put_b1, skip=2, stop=3)
    loop(streams * per, middle_grad, UNROLL)

    def turn_middle(i):
        x = r.nx[:, :rows, span(i, LANES)].reshape(group, LANES)
        r.tt[span(i, LANES), :] = x.T

    loop(width // LANES, turn_middle)

    def grad_attended(s):
        w = r.a_all[:, :, three:].reshape(width, quarter)
        r.gatt[span(s, TILE), :] = nn(
            r.nx[span(s, half_streams), :rows, :].reshape(TILE, width), w
        ).astype(B16)

    loop(sides, grad_attended)
    steps([put_b1], True, skip=1, stop=2)

    def edges(s):
        at = span(s, rows)
        lane = lax.broadcasted_iota(jnp.int32, (rows, LANES), 1)
        total = jnp.zeros((rows, LANES), F32)
        for p in range(pairs):
            product = r.gatt[at, lanes(p)].astype(F32) * r.att[at, lanes(p)].astype(F32)
            for h in range(2):
                k = 2 * p + h
                total = jnp.where(lane == k, r.lse[s, k], total)
                total = jnp.where(lane == 2 * pairs + k, delta_of(product, h), total)
        total = total.T
        head_at = pl.ds(pl.multiple_of(s * rows, reach), reach)
        tail_at = pl.ds(pl.multiple_of(s * rows + rows - reach, reach), reach)
        r.edge_src[0, span(s, reach), :] = r.gatt[tail_at, :]
        r.edge_src[1, span(s, reach), :] = r.gatt[head_at, :]
        for way in range(2):
            r.stat_src[way, s] = total[: 4 * pairs]

    loop(streams, edges)
    stat.start()
    edge.start()

    def attend_back(s):
        allowed = visible(s)
        at = span(s, rows)
        for p in range(pairs):
            scores = nt(r.qs[s, p], r.k2[s, p]) * scale
            grad = r.gatt[at, lanes(p)]
            grad_probs = nt(grad, r.v2[s, p])
            grad_f = grad.astype(F32)
            product = grad_f * r.att[at, lanes(p)].astype(F32)
            agains, grads = [], []
            for h in range(2):
                cut = slice(h * outer, (h + 1) * outer)
                masked = jnp.where(allowed, scores[:, cut], -1e30)
                again = jnp.exp(masked - r.lse[s, 2 * p + h][:, 0:1])
                delta = delta_of(product, h)
                agains.append(again.astype(B16))
                grads.append((again * (grad_probs[:, cut] - delta) * scale).astype(B16))
            grad_query = nn(jnp.concatenate(grads, axis=1), r.k2[s, p])
            grad_keys = nn(jnp.concatenate(grads, axis=0).T, r.q2[s, p])
            grad_values = nn(jnp.concatenate(agains, axis=0).T, halves(grad_f).astype(B16))
            r.gp[at, lanes(p)] = unrotate(
                grad_query, r.cosine[reach : reach + rows], r.sine[reach : reach + rows]
            ).astype(B16)
            for k, value in ((p, grad_keys), (pairs + p, grad_values)):
                r.own_kv[s, :, lanes(k)] = value[reach : reach + rows]

    loop(streams, attend_back)
    relays(put_b1, skip=3)
    down.last()

    def grad_out(m):
        out = nn(r.tt[span(m, TILE), :], r.att[...]).astype(B16)
        r.ga[span(m, blocks), :, quarter:] = out.reshape(blocks, part, quarter)

    loop(tiles, grad_out)

    def grad_query(m):
        out = nn(r.n1t[span(m, TILE), :], r.gp[:, :quarter]).astype(B16)
        r.ga[span(m, blocks), :, :quarter] = out.reshape(blocks, part, quarter)

    loop(tiles, grad_query)
    exchanges([put_a])

    def norm_again(i):
        s, h = i // per, i % per
        x = r.tok_all[s, span(h, CHUNK), :].astype(F32)
        scaled, inverse, _ = norm_forward(x, r.gain[0:1, :])
        r.scaled[span(i, CHUNK), :] = scaled
        r.inverse[span(i, CHUNK), :] = jnp.broadcast_to(inverse, (CHUNK, LANES))

    loop(streams * per, norm_again, UNROLL)
    down.finish()
    steps([put_b1], True, skip=2)
    edge.arrive()
    stat.arrive()

    def join(s):
        allowed = visible_rims(s)
        empty = jnp.zeros((LANES - 4 * pairs, rows), F32)
        before = jnp.concatenate([r.stat_mid[0, s], empty], axis=0).T[rows - reach :]
        after = jnp.concatenate([r.stat_mid[1, s], empty], axis=0).T[:reach]
        stats = jnp.concatenate([before, after], axis=0)
        for p in range(pairs):
            keys, vals = [
                jnp.concatenate(
                    [ref[s, p, h * outer + reach : h * outer + reach + rows] for h in range(2)],
                    axis=0,
                )
                for ref in (r.k2, r.v2)
            ]
            grad = jnp.concatenate(
                [r.edge_mid[way, span(s, reach), lanes(p)] for way in range(2)], axis=0
            )
            scores = nt(r.hq[s, p], keys) * scale
            grad_probs = nt(grad, vals)
            agains, grads = [], []
            for h in range(2):
                k = 2 * p + h
                cut = slice(h * rows, (h + 1) * rows)
                masked = jnp.where(allowed, scores[:, cut], -1e30)
                again = jnp.exp(masked - stats[:, k : k + 1])
                delta = stats[:, 2 * pairs + k : 2 * pairs + k + 1]
                agains.append(again.astype(B16))
                grads.append((again * (grad_probs[:, cut] - delta) * scale).astype(B16))
            grad_keys = nn(jnp.concatenate(grads, axis=0).T, r.hq2[s, p])
            grad_values = nn(
                jnp.concatenate(agains, axis=0).T, halves(grad.astype(F32)).astype(B16)
            )
            grad_keys = unrotate(
                grad_keys + r.own_kv[s, :, lanes(p)],
                r.cosine[reach : reach + rows],
                r.sine[reach : reach + rows],
            )
            grad_values = grad_values + r.own_kv[s, :, lanes(pairs + p)]
            r.gp[span(s, rows), lanes(pairs + p)] = grad_keys.astype(B16)
            r.gp[span(s, rows), lanes(2 * pairs + p)] = grad_values.astype(B16)

    loop(streams, join)

    def grad_pair(i):
        m, j = i // 2, i % 2
        at = pl.ds(pl.multiple_of((j + 1) * quarter, quarter), quarter)
        out = nn(r.n1t[span(m, TILE), :], r.gp[:, at]).astype(B16)
        r.gc[span(m, blocks), :, span(j, quarter)] = out.reshape(blocks, part, quarter)

    loop(tiles * 2, grad_pair)
    steps([put_a], True, stop=1)

    def one_project(j):
        w = r.a_all[span(j, blocks), :, :three].reshape(TILE, three)
        out = nt(r.gp[...], w)
        at = span(j, TILE)
        r.gain_row[0:1, at] = jnp.sum(out * r.scaled[:, at], axis=0, keepdims=True)
        r.src_b[:, :, at] = out.astype(B16).reshape(streams, rows, TILE)

    loop(tiles, one_project)
    for s in range(seq.n):
        k = s * part // LANES
        r.gain_parts[s] = r.gain_row[:, k * LANES : (k + 1) * LANES]
    exchanges([one])
    exchanges([put_g])
    exchanges([put_c])
    put_b2.last()
    put_b1.last()
    steps([one], True)
    steps([put_a], True, skip=1, stop=2)
    steps([put_g], True, stop=1)
    for j in range(main):
        cut = slice(j * LANES, (j + 1) * LANES)
        for k in range(2):
            at = (2 * j + k) * LANES
            r.din[k, cut, :] = db1[:, at : at + LANES].T
        r.ddown_t[cut, :] = db2[:, cut].T
    rim_sum = db1[:, rim_at:].T
    r.din[0, flat:, :] = rim_sum[:tail]
    r.din[1, flat:, :] = rim_sum[tail : 2 * tail]
    r.ddown_t[flat:, :] = rim_sum[2 * tail : 3 * tail]
    steps([put_c], True, stop=1)
    steps([put_a], True, skip=2)
    steps([put_g], True, skip=1, stop=2)
    one.last()

    def final(h):
        at = span(h, CHUNK)
        here = pl.ds(pl.multiple_of(fsdp.me * rows + h * CHUNK, CHUNK), CHUNK)
        got = norm_backward(
            r.one_sum[at, :], r.scaled[here, :], r.inverse[here, 0:1], r.gain[0:1, :]
        )
        r.dinput[at, :] = r.own_grad[at, :] + got
        middle = r.tok[at, :].astype(F32) + r.attn_all[fsdp.me, at, :].astype(F32)
        r.out[at, :] = (middle + r.down_sum[at, :]).astype(B16)

    loop(per, final)
    steps([put_c], True, skip=1, stop=2)
    steps([put_g], True, skip=2)
    put_a.last()
    put_g.last()
    put_g2.start()
    r.dqkv[0] = da[:, :quarter]
    for k in range(pairs):
        at = quarter + k * LANES
        r.dout[k * LANES : (k + 1) * LANES, :] = da[:, at : at + LANES].T
    steps([put_c], True, skip=2)
    steps([put_g2], False)
    put_g2.finish()
    total = r.gain_got[0]
    for f in range(1, fsdp.n):
        total = total + r.gain_got[f]
    total = pltpu.roll(total, (LANES - shift) % LANES, 1)
    r.dgain_one[...] = total[0:1, :piece]
    r.dgain_two[...] = total[1:2, :piece]
    put_c.last()
    r.dqkv[1] = dc[:, :quarter]
    r.dqkv[2] = dc[:, quarter:]
    for job in (edge, stat, one, put_b1, put_b2, put_a, put_c, put_g):
        job.finish()


def run_layer(tok, grd, gain_in, qkv, out_w, in_two, down_t, freq, lengths):
    n, nf = lax.axis_size("seq"), lax.axis_size("fsdp")
    rows, width = tok.shape
    count, part = down_t.shape
    quarter, piece = out_w.shape[0], gain_in.shape[1]
    gain_block = (16, LANES)
    wide_a, wide_2 = 4 * quarter, count // LANES * LANES
    wide_1 = 2 * wide_2 + LANES
    block_c = (part, 2 * quarter)
    block_a, block_1, block_2 = (part, wide_a), (part, wide_1), (part, wide_2)
    pairs = quarter // LANES
    streams = nf
    group = streams * rows
    outer = rows + 2 * WIN
    vmem = pl.BlockSpec(memory_space=pltpu.VMEM)
    ins = [
        ("tok", tok, vmem),
        ("grd", grd, vmem),
        ("gain_in", gain_in, vmem),
        ("qkv", qkv, vmem),
        ("out_w", out_w, vmem),
        ("in_two", in_two, vmem),
        ("down_t", down_t, vmem),
        ("freq", freq, vmem),
        ("lengths", lengths, pl.BlockSpec(memory_space=pltpu.SMEM)),
    ]
    outs = [
        ("out", (rows, width), B16),
        ("dinput", (rows, width), F32),
        ("dgain_one", (1, piece), F32),
        ("dgain_two", (1, piece), F32),
        ("dqkv", (3, part, quarter), F32),
        ("dout", (quarter, part), F32),
        ("din", (2, count, part), F32),
        ("ddown_t", (count, part), F32),
    ]
    plan = Plan()
    token_block = (rows, width)
    for name, count_, shape, dtype in (
        ("tok", nf, token_block, B16),
        ("grd", nf, token_block, B16),
        ("rim", nf, (2, WIN, width), B16),
        ("a", n, block_a, B16),
        ("b1", n, block_1, B16),
        ("b2", n, block_2, B16),
        ("attn", nf, token_block, B16),
        ("back", nf, token_block, B16),
    ):
        plan.vmem(name + "_all", (count_,) + shape, dtype)
        plan.add(name + "_g", *Gather.scratch(count_))
    for name, count_, shape, dtype in (
        ("attn", nf, token_block, B16),
        ("back", nf, token_block, B16),
        ("down", nf, token_block, B16),
        ("one", nf, token_block, B16),
        ("b1", n, block_1, B16),
        ("b2", n, block_2, B16),
        ("a", n, block_c, B16),
        ("c", n, block_c, B16),
        ("gain", n, (8, LANES), F32),
    ):
        plan.add(name + "_r", *Reduce.scratch(count_, shape, dtype))
    plan.add("b1_relay", *Reduce.relay_scratch(block_1, B16))
    plan.vmem("rim_mid", (2, WIN, width), B16)
    plan.add("halo_s", *Halo.scratch())
    plan.vmem("gains", gain_block, B16)
    plan.vmem("gains_mid", (n,) + gain_block, B16)
    plan.add("gains_g", *Gather.scratch(n))
    plan.vmem("gains_all", (nf, n) + gain_block, B16)
    plan.add("gains2_g", *Gather.scratch(nf))
    plan.vmem("gain_mid", (8, LANES), F32)
    plan.vmem("gain_got", (nf, 8, LANES), F32)
    plan.vmem("cosine", (outer, LANES), F32)
    plan.vmem("sine", (outer, LANES), F32)
    plan.add("gain_g", *Gather.scratch(nf))
    plan.add("edge_s", *Halo.scratch())
    plan.add("stat_s", *Halo.scratch())
    for name, shape, dtype in (
        ("edge_src", (2, streams * WIN, quarter), B16),
        ("edge_mid", (2, streams * WIN, quarter), B16),
        ("stat_src", (2, streams, 4 * pairs, LANES), F32),
        ("stat_mid", (2, streams, 4 * pairs, LANES), F32),
        ("hq", (streams, pairs, 2 * WIN, LANES), B16),
        ("hq2", (streams, pairs, 4 * WIN, LANES), B16),
        ("gain", (gain_block[0], width), F32),
        ("gain_row", (8, width), F32),
        ("gain_parts", (n, 8, LANES), F32),
        ("nx", (streams, outer, width), B16),
        ("n1t", (width, group), B16),
        ("gt", (width, group), B16),
        ("tt", (width, group), B16),
        ("qs", (streams, pairs, rows, LANES), B16),
        ("q2", (streams, pairs, 2 * rows, LANES), B16),
        ("k2", (streams, pairs, 2 * outer, LANES), B16),
        ("v2", (streams, pairs, 2 * outer, LANES), B16),
        ("lse", (streams, 2 * pairs, rows, LANES), F32),
        ("att", (group, quarter), B16),
        ("src_a", (streams,) + token_block, B16),
        ("src_b", (streams,) + token_block, B16),
        ("attn_mid", token_block, B16),
        ("back_mid", token_block, B16),
        ("down_sum", token_block, F32),
        ("one_sum", token_block, F32),
        ("scaled", (group, width), F32),
        ("inverse", (group, LANES), F32),
        ("big", (group, 2 * (wide_2 + LANES)), F32),
        ("mix", (group, wide_2 + LANES), B16),
        ("mix_rim", (group, LANES), B16),
        ("dfull", (width, wide_2 + LANES), B16),
        ("gh", (group, wide_1), B16),
        ("gb1", (n,) + block_1, B16),
        ("gb2", (n,) + block_2, B16),
        ("ga", (n,) + block_c, B16),
        ("gc", (n,) + block_c, B16),
        ("own_grad", token_block, F32),
        ("own_kv", (streams, rows, 2 * quarter), F32),
        ("gatt", (group, quarter), B16),
        ("gp", (group, 3 * quarter), B16),
    ):
        plan.vmem(name, shape, dtype)
    names = [i[0] for i in ins] + [o[0] for o in outs] + plan.names
    return pl.pallas_call(
        functools.partial(layer_kernel, tuple(names)),
        out_shape=[jax.ShapeDtypeStruct(s, d) for _, s, d in outs],
        in_specs=[i[2] for i in ins],
        out_specs=[vmem] * len(outs),
        scratch_shapes=plan.shapes,
        compiler_params=pltpu.CompilerParams(
            collective_id=1, has_side_effects=True, vmem_limit_bytes=63 * 1024 * 1024
        ),
    )(*[i[1] for i in ins])


def settle_kernel(*refs):
    count = len(refs) // 2
    copies = [
        pltpu.make_async_copy(*refs[k : 2 * count : count], refs[2 * count].at[k])
        for k in range(count)
    ]
    for copy in copies:
        copy.start()
    for copy in copies:
        copy.wait()


def settle(arrays):
    anywhere = pl.BlockSpec(memory_space=pl.ANY)
    return pl.pallas_call(
        settle_kernel,
        out_shape=[jax.ShapeDtypeStruct(x.shape, x.dtype) for x in arrays],
        in_specs=[anywhere] * len(arrays),
        out_specs=[pl.BlockSpec(memory_space=pltpu.VMEM)] * len(arrays),
        scratch_shapes=[pltpu.SemaphoreType.DMA((len(arrays),))],
    )(*arrays)


def per_device(
    layer_input,
    doc_lengths,
    attn_gain,
    qkv_weight,
    out_weight,
    mlp_gain,
    in_weight,
    down_weight,
    out_grad,
):
    gain_in = jnp.stack([attn_gain, mlp_gain])
    gain_in = jnp.pad(gain_in, ((0, 6), (0, 0)))
    half = np.arange(LANES)[None, :] % (HEAD // 2)
    freq = 10000.0 ** (-(2.0 / HEAD) * half)
    made = run_layer(
        layer_input[0],
        out_grad[0],
        gain_in,
        qkv_weight.transpose(1, 0, 2),
        out_weight,
        in_weight.transpose(1, 2, 0),
        down_weight.T,
        jnp.asarray(freq, F32),
        doc_lengths,
    )
    output, input_grad, dgain_one, dgain_two, dqkv, dout, din, ddown_t = settle(made)
    return (
        output[None],
        input_grad[None],
        dgain_one[0],
        dqkv.transpose(1, 0, 2),
        dout,
        dgain_two[0],
        din.transpose(2, 0, 1),
        ddown_t.T,
    )


def solution(mesh):
    in_specs = (
        P("fsdp", "seq", None),
        P(),
        P(("seq", "fsdp")),
        P("seq", None, "fsdp"),
        P("fsdp", "seq"),
        P(("seq", "fsdp")),
        P("seq", None, "fsdp"),
        P("seq", "fsdp"),
        P("fsdp", "seq", None),
    )
    out_specs = (
        P("fsdp", "seq", None),
        P("fsdp", "seq", None),
        P(("seq", "fsdp")),
        P("seq", None, "fsdp"),
        P("fsdp", "seq"),
        P(("seq", "fsdp")),
        P("seq", None, "fsdp"),
        P("seq", "fsdp"),
    )
    return jax.shard_map(
        per_device, mesh=mesh, in_specs=in_specs, out_specs=out_specs, check_vma=False
    )
```

```python
import functools

import jax
import jax.numpy as jnp
import numpy as np
from jax import lax
from jax.experimental import pallas as pl
from jax.experimental.pallas import tpu as pltpu
from jax.sharding import PartitionSpec as P

HEAD = 64
WIN = 64


EPSILON = 1e-05


class Place:
    def __init__(self, axis):
        self.axis = axis
        self.n = lax.axis_size(axis)
        self.length = self.n // 2
        me = lax.axis_index(axis)
        self.me = me
        self.at = me // 2
        self.side = me % 2

    def partner(self):
        return {self.axis: self.at * 2 + (1 - self.side)}

    def right(self):
        return {self.axis: self.me + 2}

    def left(self):
        return {self.axis: self.me - 2}

    def has_right(self):
        return self.at < self.length - 1

    def has_left(self):
        return self.at > 0

    def greet(self, barrier):
        mesh = pl.DeviceIdType.MESH
        pl.semaphore_signal(barrier, inc=1, device_id=self.partner(), device_id_type=mesh)

        @pl.when(self.has_left())
        def _():
            pl.semaphore_signal(barrier, inc=1, device_id=self.left(), device_id_type=mesh)

        @pl.when(self.has_right())
        def _():
            pl.semaphore_signal(barrier, inc=1, device_id=self.right(), device_id_type=mesh)

    def diagonal(self):
        there = jnp.where(self.side == 1, self.has_right(), self.has_left())
        return there, {self.axis: self.me + 2 * self.side - 1}

    def peers(self):
        one, none = jnp.int32(1), jnp.int32(0)
        return 1 + jnp.where(self.has_left(), one, none) + jnp.where(self.has_right(), one, none)


def when(condition, action):
    if condition is True:
        action()
    else:
        pl.when(condition)(action)


def remote(src, dst, send, recv, device):
    return pltpu.make_async_remote_copy(
        src_ref=src,
        dst_ref=dst,
        send_sem=send,
        recv_sem=recv,
        device_id=device,
        device_id_type=pl.DeviceIdType.MESH,
    )


class Gather:
    scratch = staticmethod(
        lambda n: [
            pltpu.SemaphoreType.DMA((3, n)),
            pltpu.SemaphoreType.DMA((n,)),
            pltpu.SemaphoreType.DMA,
        ]
    )

    def __init__(self, place, src, dst, sems, relayed=False):
        self.place, self.src, self.dst = place, src, dst
        self.send, self.recv, self.local = sems
        self.relayed = relayed

    def crosses(self, i):
        if not self.relayed:
            return True
        inner = jnp.logical_and(i > 0, i < self.place.length - 1)
        return jnp.logical_or(inner, i == self.place.at)

    def relay(self, d):
        place = self.place
        ends = ((d, 0, 1), (place.length - 1 - d, place.length - 1, 2))
        for at, end, way in ends:
            block = 2 * end + 1 - place.side

            @pl.when(place.at == at)
            def _(block=block, way=way):
                self.copy(0, block, place.partner()).wait_recv()
                (self.ahead if way == 1 else self.behind)(block, False, lambda c: c.start())

    def copy(self, way, block, device, own=False):
        src = self.src if own else self.dst.at[block]
        return remote(src, self.dst.at[block], self.send.at[way, block], self.recv.at[block], device)

    def onward(self, block, own, act):
        place = self.place
        act(self.copy(0, block, place.partner(), own))

    def start(self):
        place = self.place
        if self.src is not None:
            pltpu.make_async_copy(self.src, self.dst.at[place.me], self.local).start()
        self.start_lines()
        self.start_across()

    def start_lines(self):
        place = self.place
        self.ahead(place.me, self.src is not None, lambda c: c.start())
        self.behind(place.me, self.src is not None, lambda c: c.start())

    def start_across(self):
        self.onward(self.place.me, self.src is not None, lambda c: c.start())

    def ahead(self, block, own, act):
        place = self.place

        @pl.when(place.has_right())
        def _():
            act(self.copy(1, block, place.right(), own))

    def behind(self, block, own, act):
        place = self.place

        @pl.when(place.has_left())
        def _():
            act(self.copy(2, block, place.left(), own))

    def step(self, d):
        place = self.place

        @pl.when(place.at - d >= 0)
        def _():
            block = place.me - 2 * d
            self.copy(1, block, place.partner()).wait_recv()
            self.ahead(block, False, lambda c: c.start())
            when(
                self.crosses(place.at - d),
                lambda: self.onward(block, False, lambda c: c.start()),
            )

        @pl.when(place.at + d < place.length)
        def _():
            block = place.me + 2 * d
            self.copy(2, block, place.partner()).wait_recv()
            self.behind(block, False, lambda c: c.start())
            when(
                self.crosses(place.at + d),
                lambda: self.onward(block, False, lambda c: c.start()),
            )

    def finish(self):
        place = self.place
        if self.src is not None:
            pltpu.make_async_copy(self.src, self.dst.at[place.me], self.local).wait()

        def arrived(i, carry):
            inner = True
            if self.relayed:
                inner = jnp.logical_and(i > 0, i < place.length - 1)
            when(
                inner,
                lambda: self.copy(0, 2 * i + 1 - place.side, place.partner()).wait_recv(),
            )
            when(
                self.crosses(i),
                lambda: self.onward(2 * i + place.side, False, lambda c: c.wait_send()),
            )

            @pl.when(i <= place.at)
            def _():
                self.ahead(2 * i + place.side, False, lambda c: c.wait_send())

            @pl.when(i >= place.at)
            def _():
                self.behind(2 * i + place.side, False, lambda c: c.wait_send())

            return carry

        lax.fori_loop(0, place.length, arrived, 0)
        if self.relayed:
            self.ahead(1 - place.side, False, lambda c: c.wait_send())
            self.behind(2 * place.length - 1 - place.side, False, lambda c: c.wait_send())


class Reduce:
    @staticmethod
    def scratch(n, block, dtype):
        length = n // 2
        return [
            pltpu.VMEM((length,) + block, dtype),
            pltpu.VMEM((length + 1,) + block, dtype),
            pltpu.SemaphoreType.DMA((2, length)),
            pltpu.SemaphoreType.DMA((length,)),
            pltpu.SemaphoreType.DMA((length + 1,)),
        ]

    @staticmethod
    def relay_scratch(block, dtype):
        return [
            pltpu.VMEM((2,) + block, dtype),
            pltpu.SemaphoreType.DMA((2,)),
            pltpu.SemaphoreType.DMA((2,)),
        ]

    def __init__(self, place, src, dst, scratch, relays=None):
        self.place, self.src, self.dst = place, src, dst
        self.paired, self.lined, self.send, self.pair_recv, self.line_recv = scratch
        self.relays = relays

    def crosses(self, i):
        if self.relays is None:
            return True
        return jnp.logical_and(i > 0, i < self.place.length - 1)

    def pass_on(self, end, device):
        held, send, recv = self.relays
        block = 2 * (end * (self.place.length - 1)) + 1 - self.place.side
        return self.src.at[block], remote(
            self.src.at[block], held.at[end], send.at[end], recv.at[end], device
        )

    def relay(self, d):
        place = self.place
        finish = place.length - 1
        for end, at in ((0, finish - d), (1, d)):
            device = place.right() if end else place.left()
            final = finish if end else 0

            @pl.when(place.at == at)
            def _(end=end, device=device, final=final):
                block, copy = self.pass_on(end, device)

                @pl.when(d > 0)
                def _():
                    copy.wait_recv()
                    self.add(block, [block, self.relays[0].at[end]])

                @pl.when(place.at != final)
                def _():
                    copy.start()

                @pl.when(place.at == final)
                def _():
                    self.across(final).start()

    def mine(self, i):
        return self.src.at[2 * i + self.place.side]

    def across(self, i):
        place = self.place
        return remote(
            self.src.at[2 * i + 1 - place.side],
            self.paired.at[i],
            self.send.at[0, i],
            self.pair_recv.at[i],
            place.partner(),
        )

    def along(self, i, slot, device):
        return remote(
            self.mine(i), self.lined.at[slot], self.send.at[1, i], self.line_recv.at[slot], device
        )

    def exchange(self, d):
        place = self.place

        @pl.when(place.at + d < place.length)
        def _():
            when(self.crosses(place.at + d), lambda: self.across(place.at + d).start())

        @pl.when(jnp.logical_and(d > 0, place.at - d >= 0))
        def _():
            when(self.crosses(place.at - d), lambda: self.across(place.at - d).start())

    def add(self, out, refs):
        rows = out.shape[0]
        tile = 16 if rows % 16 == 0 else 8

        def each(i, carry):
            at = pl.ds(pl.multiple_of(i * tile, tile), tile)
            total = refs[0][at, :].astype(jnp.float32)
            for ref in refs[1:]:
                total = total + ref[at, :].astype(jnp.float32)
            out[at, :] = total.astype(out.dtype)
            return carry

        lax.fori_loop(0, rows // tile, each, 0)

    def own(self, i):
        self.across(i).wait_recv()
        return [self.mine(i), self.paired.at[i]]

    def combine(self, i, paired, lined):
        def total(pair):
            refs = self.own(i) if pair else [self.mine(i)]

            @pl.when(lined)
            def _():
                self.along(i, i, self.place.partner()).wait_recv()
                self.add(self.mine(i), refs + [self.lined.at[i]])

            if pair:

                @pl.when(jnp.logical_not(lined))
                def _():
                    self.add(self.mine(i), refs)

        when(paired, lambda: total(True))
        if paired is not True:
            pl.when(jnp.logical_not(paired))(lambda: total(False))

    def step(self, d):
        place = self.place

        @pl.when(place.at + d < place.length)
        def _():
            i = place.at + d
            self.combine(i, self.crosses(i), place.has_left())
            self.along(i, i, place.right()).start()

        @pl.when(place.at - d >= 0)
        def _():
            i = place.at - d
            self.combine(i, self.crosses(i), place.has_right())
            slot = jnp.where(d == 1, place.length, i)
            self.along(i, slot, place.left()).start()

    def last(self):
        place = self.place
        i, extra = place.at, place.length
        refs = self.own(i)

        @pl.when(place.has_left())
        def _():
            self.along(i, i, place.partner()).wait_recv()

        @pl.when(place.has_right())
        def _():
            self.along(i, extra, place.partner()).wait_recv()

        both = jnp.logical_and(place.has_left(), place.has_right())

        @pl.when(both)
        def _():
            self.add(self.dst, refs + [self.lined.at[i], self.lined.at[extra]])

        @pl.when(jnp.logical_and(place.has_left(), jnp.logical_not(both)))
        def _():
            self.add(self.dst, refs + [self.lined.at[i]])

        @pl.when(jnp.logical_and(place.has_right(), jnp.logical_not(both)))
        def _():
            self.add(self.dst, refs + [self.lined.at[extra]])

    def finish(self):
        place = self.place

        def each(i, carry):
            crosses = self.crosses(i)
            if crosses is not True:
                crosses = jnp.logical_or(crosses, i == place.at)
            when(crosses, lambda: self.across(i).wait_send())

            @pl.when(i != place.at)
            def _():
                self.along(i, i, place.partner()).wait_send()

            return carry

        lax.fori_loop(0, place.length, each, 0)
        if self.relays is not None:

            @pl.when(place.has_left())
            def _():
                self.pass_on(0, place.left())[1].wait_send()

            @pl.when(place.has_right())
            def _():
                self.pass_on(1, place.right())[1].wait_send()


class Halo:
    scratch = staticmethod(lambda: [pltpu.SemaphoreType.DMA((2,)), pltpu.SemaphoreType.DMA((2,))])

    def __init__(self, place, src, mid, sems):
        self.place, self.src, self.mid = place, src, mid
        self.send, self.recv = sems
        self.after = place.me < place.n - 1
        self.before = place.me > 0

    def copy(self, way):
        rows, width = self.src.shape[0], self.mid.shape[1]
        at = rows - width if way == 0 else 0
        other = {self.place.axis: self.place.me + 1 - 2 * way}
        return remote(
            self.src.at[pl.ds(at, width)],
            self.mid.at[way],
            self.send.at[way],
            self.recv.at[way],
            other,
        )

    def start(self):
        @pl.when(self.after)
        def _():
            self.copy(0).start()

        @pl.when(self.before)
        def _():
            self.copy(1).start()

        @pl.when(jnp.logical_not(self.before))
        def _():
            self.mid[0] = jnp.zeros(self.mid.shape[1:], self.mid.dtype)

        @pl.when(jnp.logical_not(self.after))
        def _():
            self.mid[1] = jnp.zeros(self.mid.shape[1:], self.mid.dtype)

    def arrive(self):
        @pl.when(self.before)
        def _():
            self.copy(0).wait_recv()

        @pl.when(self.after)
        def _():
            self.copy(1).wait_recv()

    def finish(self):
        @pl.when(self.after)
        def _():
            self.copy(0).wait_send()

        @pl.when(self.before)
        def _():
            self.copy(1).wait_send()


def greet_all(places, slanted):
    barrier = pltpu.get_barrier_semaphore()
    extra = jnp.int32(0)
    if slanted:
        there, device = places[0].diagonal()
        extra = jnp.where(there, jnp.int32(1), jnp.int32(0))

        @pl.when(there)
        def _():
            pl.semaphore_signal(
                barrier, inc=1, device_id=device, device_id_type=pl.DeviceIdType.MESH
            )

    for place in places:
        place.greet(barrier)
    pl.semaphore_wait(barrier, extra + sum(place.peers() for place in places))


def steps(jobs, down, skip=0, stop=None):
    length = jobs[0].place.length
    stop = length - 1 if stop is None else min(stop, length - 1)

    def each(k, carry):
        d = length - 1 - k if down else k + 1
        for job in jobs:
            job.step(d)
        return carry

    if skip < stop:
        lax.fori_loop(skip, stop, each, 0)


def relays(job, skip=0, stop=None):
    length = job.place.length
    stop = length if stop is None else stop

    def each(k, carry):
        job.relay(k)
        return carry

    lax.fori_loop(skip, stop, each, 0)


def exchanges(jobs, skip=0, stop=None):
    length = jobs[0].place.length
    stop = length if stop is None else stop

    def each(k, carry):
        for job in jobs:
            job.exchange(length - 1 - k)
        return carry

    lax.fori_loop(skip, stop, each, 0)


B16, F32 = jnp.bfloat16, jnp.float32
LANES = 128
TILE = 256
CHUNK = 32
UNROLL = 4


class Edge(Halo):
    def copy(self, way):
        other = {self.place.axis: self.place.me + 1 - 2 * way}
        return remote(
            self.src.at[way], self.mid.at[way], self.send.at[way], self.recv.at[way], other
        )


class Plan:
    def __init__(self):
        self.names, self.shapes = [], []

    def add(self, name, *items):
        self.names += [name] * len(items)
        self.shapes += items

    def vmem(self, name, shape, dtype):
        self.add(name, pltpu.VMEM(shape, dtype))


class Refs:
    def __init__(self, names, refs):
        self.groups = {}
        for name, ref in zip(names, refs):
            self.groups.setdefault(name, []).append(ref)

    def __getattr__(self, name):
        return self.groups[name][0]

    def all(self, name):
        return self.groups[name]


def nn(left, right):
    return jnp.dot(left, right, preferred_element_type=F32)


def nt(left, right):
    return lax.dot_general(left, right, (((1,), (1,)), ((), ())), preferred_element_type=F32)


def loop(count, body, unroll=1):
    def each(i, carry):
        for k in range(unroll):
            body(i * unroll + k)
        return carry

    lax.fori_loop(0, count // unroll, each, 0)


def span(i, width):
    return pl.ds(pl.multiple_of(i * width, width), width)


def norm_forward(values, gain):
    mean = jnp.mean(values, axis=-1, keepdims=True)
    centred = values - mean
    inverse = lax.rsqrt(jnp.mean(centred * centred, axis=-1, keepdims=True) + EPSILON)
    scaled = centred * inverse
    return (scaled, inverse, (scaled * gain).astype(B16))


def norm_backward(grad, scaled, inverse, gain):
    weighted = grad * gain
    return inverse * (
        weighted
        - jnp.mean(weighted, axis=-1, keepdims=True)
        - scaled * jnp.mean(weighted * scaled, axis=-1, keepdims=True)
    )


def gelu_parts(inner):
    cdf = 0.5 * (1.0 + lax.erf(inner * 0.7071067811865476))
    density = jnp.exp(-0.5 * inner * inner) * 0.3989422804014327
    return (inner * cdf, cdf + inner * density)


def swap(field):
    lane = lax.broadcasted_iota(jnp.int32, field.shape, 1)
    half = HEAD // 2
    return jnp.where(
        lane % HEAD < half, pltpu.roll(field, LANES - half, 1), pltpu.roll(field, half, 1)
    )


def rotate(field, cosine, sine):
    return field * cosine + swap(field) * sine


def unrotate(field, cosine, sine):
    return field * cosine - swap(field) * sine


def halves(field):
    lane = lax.broadcasted_iota(jnp.int32, field.shape, 1)
    low = lane < HEAD
    zero = jnp.zeros_like(field)
    return jnp.concatenate([jnp.where(low, field, zero), jnp.where(low, zero, field)], axis=0)


def layer_kernel(names, *refs):
    r = Refs(names, refs)
    seq, fsdp = Place("seq"), Place("fsdp")
    rows, width = r.tok.shape
    count = r.down_t.shape[0]
    streams = r.tok_all.shape[0]
    group = streams * rows
    quarter = r.att.shape[1]
    pairs = quarter // LANES
    part = r.a_all.shape[1]
    reach, outer = WIN, rows + 2 * WIN
    main = count // LANES
    tail = count - main * LANES
    flat = main * LANES
    rim_at = 2 * flat
    blocks = TILE // part
    tiles = width // TILE
    per = rows // CHUNK
    scale = HEAD**-0.5
    three = 3 * quarter
    half_streams = TILE // rows

    tokens = Gather(fsdp, r.tok, r.tok_all, r.all("tok_g"))
    cots = Gather(fsdp, r.grd, r.grd_all, r.all("grd_g"))
    halo = Halo(seq, r.tok, r.rim_mid, r.all("halo_s"))
    rim = Gather(fsdp, r.rim_mid, r.rim_all, r.all("rim_g"))
    gains = Gather(seq, r.gains, r.gains_mid, r.all("gains_g"))
    gains2 = Gather(fsdp, r.gains_mid, r.gains_all, r.all("gains2_g"))
    get_a = Gather(seq, None, r.a_all, r.all("a_g"), True)
    get_b1 = Gather(seq, None, r.b1_all, r.all("b1_g"))
    get_b2 = Gather(seq, None, r.b2_all, r.all("b2_g"))
    attn = Reduce(fsdp, r.src_a, r.attn_mid, r.all("attn_r"))
    attn2 = Gather(fsdp, r.attn_mid, r.attn_all, r.all("attn_g"))
    back = Reduce(fsdp, r.src_a, r.back_mid, r.all("back_r"))
    back2 = Gather(fsdp, r.back_mid, r.back_all, r.all("back_g"))
    down = Reduce(fsdp, r.src_b, r.down_sum, r.all("down_r"))
    one = Reduce(fsdp, r.src_b, r.one_sum, r.all("one_r"))
    db1 = r.big.at[0:part, 0 : rim_at + LANES]
    db2 = r.big.at[part : 2 * part, 0:flat]
    da = r.big.at[2 * part : 3 * part, 0 : 2 * quarter]
    dc = r.big.at[2 * part : 3 * part, 2 * quarter : 4 * quarter]
    put_b1 = Reduce(seq, r.gb1, db1, r.all("b1_r"), r.all("b1_relay"))
    put_b2 = Reduce(seq, r.gb2, db2, r.all("b2_r"))
    put_a = Reduce(seq, r.ga, da, r.all("a_r"))
    put_c = Reduce(seq, r.gc, dc, r.all("c_r"))
    put_g = Reduce(seq, r.gain_parts, r.gain_mid, r.all("gain_r"))
    put_g2 = Gather(fsdp, r.gain_mid, r.gain_got, r.all("gain_g"))
    edge = Edge(seq, r.edge_src, r.edge_mid, r.all("edge_s"))
    stat = Edge(seq, r.stat_src, r.stat_mid, r.all("stat_s"))

    piece = r.gain_one.shape[1]
    shift = (seq.me * fsdp.n + fsdp.me) * piece % LANES
    filled = [jnp.zeros((8, LANES - piece), F32)] if piece < LANES else []
    both = [r.gain_one[...].astype(F32), r.gain_two[...].astype(F32)]
    both = jnp.concatenate(both + [jnp.zeros((6, piece), F32)], axis=0)
    wide = jnp.concatenate([both] + filled, axis=1)
    wide = jnp.concatenate([pltpu.roll(wide, shift, 1), jnp.zeros((8, LANES), F32)], axis=0)
    r.gains[...] = wide.astype(B16)
    for k in range(3):
        r.a_all[seq.me, :, k * quarter : (k + 1) * quarter] = r.qkv[k]
    for k in range(pairs):
        at = three + k * LANES
        r.a_all[seq.me, :, at : at + LANES] = r.out_w[k * LANES : (k + 1) * LANES, :].T
    greet_all((seq, fsdp), True)
    for job in (gains, get_a, tokens, halo):
        job.start()

    for j in range(main):
        cut = slice(j * LANES, (j + 1) * LANES)
        for k in range(2):
            at = (2 * j + k) * LANES
            r.b1_all[seq.me, :, at : at + LANES] = r.in_two[k, cut, :].T
        r.b2_all[seq.me, :, cut] = r.down_t[cut, :].T
    last = [r.in_two[0, flat:, :], r.in_two[1, flat:, :], r.down_t[flat:, :]]
    last.append(jnp.zeros((LANES - 3 * tail, part), B16))
    r.b1_all[seq.me, :, rim_at:] = jnp.concatenate(last, axis=0).T

    steps([gains, get_a], False, stop=1)
    relays(get_a, stop=1)
    halo.arrive()
    rim.start()
    steps([tokens], False)
    place = seq.me * rows - reach + lax.broadcasted_iota(jnp.int32, (outer, LANES), 0)
    spot = lax.broadcasted_iota(jnp.int32, (outer, LANES), 1) % HEAD
    angle = place.astype(F32) * r.freq[...]
    r.cosine[...] = jnp.cos(angle)
    sine = jnp.sin(angle)
    r.sine[...] = jnp.where(spot < HEAD // 2, -sine, sine)
    steps([gains, get_a], False, skip=1, stop=2)
    relays(get_a, skip=1, stop=2)
    steps([rim], False)
    steps([gains, get_a], False, skip=2)
    relays(get_a, skip=2, stop=3)
    get_b1.start_lines()
    get_b1.start_across()
    gains.finish()
    gains2.start()
    cots.start()
    steps([gains2], False)
    gains2.finish()

    for k in range(width // LANES):
        total = jnp.zeros((r.gains.shape[0], LANES), F32)
        for s in range(k * LANES // part, (k + 1) * LANES // part):
            for f in range(streams):
                total = total + r.gains_all[f, s].astype(F32)
        r.gain[:, k * LANES : (k + 1) * LANES] = total
    tokens.finish()
    rim.finish()
    halo.finish()

    def norm_own(i):
        s, h = i // per, i % per
        x = r.tok_all[s, span(h, CHUNK), :].astype(F32)
        at = pl.ds(pl.multiple_of(reach + h * CHUNK, CHUNK), CHUNK)
        r.nx[s, at, :] = norm_forward(x, r.gain[0:1, :])[2]

    loop(streams * per, norm_own, UNROLL)

    rims = reach // CHUNK

    def norm_rim(i):
        s, w, h = i // (2 * rims), i // rims % 2, i % rims
        x = r.rim_all[s, w, span(h, CHUNK), :].astype(F32)
        at = pl.ds(pl.multiple_of(w * (rows + reach) + h * CHUNK, CHUNK), CHUNK)
        r.nx[s, at, :] = norm_forward(x, r.gain[0:1, :])[2]

    loop(streams * 2 * rims, norm_rim, UNROLL)

    def turn_one(i):
        x = r.nx[:, reach : reach + rows, span(i, LANES)].reshape(group, LANES)
        r.n1t[span(i, LANES), :] = x.T

    def turn_grad(i):
        x = r.grd_all[:, :, span(i, LANES)].reshape(group, LANES)
        r.gt[span(i, LANES), :] = x.T

    relays(get_a, skip=3)
    get_a.finish()

    band = jnp.abs(
        lax.broadcasted_iota(jnp.int32, (rows, outer), 0)
        + reach
        - lax.broadcasted_iota(jnp.int32, (rows, outer), 1)
    )

    def lanes(p):
        return slice(p * LANES, (p + 1) * LANES)

    def project(s):
        x = r.nx[s]
        out = nn(x, r.a_all[:, :, quarter:three].reshape(width, 2 * quarter))
        for p in range(pairs):
            keys = rotate(out[:, lanes(p)], r.cosine[...], r.sine[...])
            r.k2[s, p] = halves(keys).astype(B16)
            r.v2[s, p] = halves(out[:, lanes(pairs + p)]).astype(B16)
        out = nn(x, r.a_all[:, :, :quarter].reshape(width, quarter))
        for p in range(pairs):
            query = rotate(out[:, lanes(p)], r.cosine[...], r.sine[...])
            own = query[reach : reach + rows]
            rims = jnp.concatenate([query[:reach], query[reach + rows :]], axis=0)
            r.qs[s, p] = own.astype(B16)
            r.q2[s, p] = halves(own).astype(B16)
            r.hq[s, p] = rims.astype(B16)
            r.hq2[s, p] = halves(rims).astype(B16)

    loop(streams // 2, project)
    steps([get_b1], False, stop=1)
    loop(streams - streams // 2, lambda i: project(i + streams // 2))

    def documents(s, place):
        docs = r.lengths.shape[1]
        ids = jnp.zeros(place.shape, jnp.int32)
        start = jnp.int32(0)
        for k in range(docs + 1):
            ids = ids + (place >= start).astype(jnp.int32)
            if k < docs:
                start = start + r.lengths[s, k]
        return ids

    first = seq.me * rows

    def visible(s):
        across = first - reach + lax.broadcasted_iota(jnp.int32, (1, outer), 1)
        along = first + lax.broadcasted_iota(jnp.int32, (rows, 1), 0)
        return (band <= reach) & (documents(s, along) == documents(s, across))

    def visible_rims(s):
        along = lax.broadcasted_iota(jnp.int32, (2 * reach, 1), 0)
        along = first + jnp.where(along < reach, along - reach, along - reach + rows)
        across = first + lax.broadcasted_iota(jnp.int32, (1, rows), 1)
        near = jnp.abs(along - across) <= reach
        return near & (documents(s, along) == documents(s, across))

    def delta_of(product, h):
        low = lax.broadcasted_iota(jnp.int32, product.shape, 1) < HEAD
        zero = jnp.zeros_like(product)
        side = jnp.where(low, product, zero) if h == 0 else jnp.where(low, zero, product)
        return jnp.sum(side, axis=-1, keepdims=True)

    def attend(s):
        allowed = visible(s)
        for p in range(pairs):
            scores = nt(r.qs[s, p], r.k2[s, p]) * scale
            probs = []
            for h in range(2):
                masked = jnp.where(allowed, scores[:, h * outer : (h + 1) * outer], -1e30)
                top = jnp.max(masked, axis=-1, keepdims=True)
                expd = jnp.exp(masked - top)
                total = jnp.sum(expd, axis=-1, keepdims=True)
                r.lse[s, 2 * p + h] = jnp.broadcast_to(top + jnp.log(total), (rows, LANES))
                probs.append((expd / total).astype(B16))
            out = nn(jnp.concatenate(probs, axis=1), r.v2[s, p])
            r.att[span(s, rows), lanes(p)] = out.astype(B16)

    loop(streams, attend)
    steps([get_b1], False, skip=1, stop=2)
    get_b2.start_lines()

    def out_project(j):
        w = r.a_all[span(j, blocks), :, three:].reshape(TILE, quarter)
        out = nt(r.att[...], w).astype(B16)
        r.src_a[:, :, span(j, TILE)] = out.reshape(streams, rows, TILE)

    loop(tiles, out_project)
    exchanges([attn])
    steps([attn], True)
    steps([cots], False)
    loop(width // LANES, turn_one)
    cots.finish()
    steps([get_b1], False, skip=2)
    get_b2.start_across()
    attn.last()
    attn2.start()
    loop(width // LANES, turn_grad)
    steps([get_b2], False, stop=1)
    steps([attn2], False)
    steps([get_b2], False, skip=1, stop=2)
    attn2.finish()
    attn.finish()
    steps([get_b2], False, skip=2)

    def norm_two(i):
        s, h = i // per, i % per
        at = span(h, CHUNK)
        x = r.tok_all[s, at, :].astype(F32) + r.attn_all[s, at, :].astype(F32)
        scaled, inverse, normed = norm_forward(x, r.gain[1:2, :])
        r.scaled[span(i, CHUNK), :] = scaled
        r.inverse[span(i, CHUNK), :] = jnp.broadcast_to(inverse, (CHUNK, LANES))
        r.nx[s, pl.ds(pl.multiple_of(rows + h * CHUNK, CHUNK), CHUNK), :] = normed

    loop(streams * per, norm_two, UNROLL)

    def normed_two(m):
        return r.nx[span(m, half_streams), rows : 2 * rows, :].reshape(TILE, width)

    def turn_two(i):
        x = r.nx[:, rows : 2 * rows, span(i, LANES)].reshape(group, LANES)
        r.tt[span(i, LANES), :] = x.T

    loop(width // LANES, turn_two)
    get_b1.finish()

    sides = group // TILE
    rest = flat + LANES

    def hidden(i):
        m, j = i // main, i % main
        w = r.b1_all[:, :, span(j, TILE)].reshape(width, TILE)
        out = nn(normed_two(m), w)
        inner, gate = out[:, :LANES], out[:, LANES:]
        activated, slope = gelu_parts(inner)
        at = span(m, TILE)
        r.big[at, span(j, LANES)] = activated
        r.big[at, pl.ds(pl.multiple_of(rest + j * LANES, LANES), LANES)] = gate * slope
        r.mix[at, span(j, LANES)] = (activated * gate).astype(B16)

    loop(sides * main, hidden)
    lane = lax.broadcasted_iota(jnp.int32, (TILE, LANES), 1)

    def hidden_rim(m):
        w = r.b1_all[:, :, rim_at:].reshape(width, LANES)
        inner = nn(normed_two(m), w)
        gate = pltpu.roll(inner, LANES - tail, 1)
        activated, slope = gelu_parts(inner)
        at = span(m, TILE)
        zero = jnp.zeros((TILE, LANES), F32)
        mixed = jnp.where(lane < tail, activated * gate, zero)
        r.big[at, flat:rest] = jnp.where(lane < tail, activated, zero)
        r.big[at, rest + flat :] = jnp.where(lane < tail, gate * slope, zero)
        r.mix[at, flat:] = mixed.astype(B16)
        r.mix_rim[at, :] = pltpu.roll(mixed, 2 * tail, 1).astype(B16)

    loop(sides, hidden_rim)

    def grad_down(m):
        out = nn(r.gt[span(m, TILE), :], r.mix[:, :flat]).astype(B16)
        r.gb2[span(m, blocks), :, :] = out.reshape(blocks, part, flat)

    loop(tiles, grad_down)
    get_b2.finish()
    exchanges([put_b2])

    def unpack(j):
        at = span(j, TILE)
        r.dfull[at, :flat] = r.b2_all[span(j, blocks), :, :].reshape(TILE, flat)
        x = r.b1_all[span(j, blocks), :, rim_at:].reshape(TILE, LANES).astype(F32)
        x = jnp.where(lane < tail, pltpu.roll(x, LANES - 2 * tail, 1), jnp.zeros_like(x))
        r.dfull[at, flat:] = x.astype(B16)

    loop(tiles, unpack)

    def grad_hidden(m, t, grad):
        at = span(m, TILE)
        inner = grad * r.big[at, pl.ds(pl.multiple_of(rest + t * LANES, LANES), LANES)]
        gate = grad * r.big[at, span(t, LANES)]
        return at, inner, gate

    def grad_mixed(m, first, tiles_of):
        g = r.grd_all[span(m, half_streams)].reshape(TILE, width)
        wide = len(tiles_of) * LANES
        grads = nn(g, r.dfull[:, pl.ds(first, wide)])
        for k, t in enumerate(tiles_of):
            at, inner, gate = grad_hidden(m, t, grads[:, k * LANES : (k + 1) * LANES])
            if t is main:
                r.gh[at, rim_at:] = (inner + pltpu.roll(gate, tail, 1)).astype(B16)
            else:
                r.gh[at, span(2 * t, LANES)] = inner.astype(B16)
                r.gh[at, span(2 * t + 1, LANES)] = gate.astype(B16)

    twos = main // 2

    def grad_two(i):
        m, j = i // twos, i % twos
        grad_mixed(m, pl.multiple_of(j * 2 * LANES, 2 * LANES), [2 * j, 2 * j + 1])

    loop(sides * twos, grad_two)
    loop(sides, lambda m: grad_mixed(m, 2 * twos * LANES, list(range(2 * twos, main)) + [main]))
    steps([put_b2], True, stop=1)

    r.gain_row[...] = jnp.zeros(r.gain_row.shape, F32)

    def back_project(j):
        w = r.b1_all[span(j, blocks)].reshape(TILE, rim_at + LANES)
        out = nt(r.gh[...], w)
        at = span(j, TILE)
        r.gain_row[1:2, at] = jnp.sum(out * r.scaled[:, at], axis=0, keepdims=True)
        r.src_a[:, :, at] = out.astype(B16).reshape(streams, rows, TILE)

    loop(tiles, back_project)
    exchanges([back])

    def grad_in(i):
        m, j = i // main, i % main
        out = nn(r.tt[span(m, 2 * TILE), :], r.gh[:, span(j, TILE)]).astype(B16)
        r.gb1[span(m, 2 * blocks), :, span(j, TILE)] = out.reshape(2 * blocks, part, TILE)

    part_way = tiles // 2 * main // 2
    loop(part_way, grad_in)
    steps([back], True)
    loop(tiles // 2 * main - part_way, lambda i: grad_in(i + part_way))

    def grad_in_rim(m):
        at = span(m, TILE)
        out = nn(r.tt[at, :], r.gh[:, rim_at:]) + nn(r.gt[at, :], r.mix_rim[...])
        r.gb1[span(m, blocks), :, rim_at:] = out.astype(B16).reshape(blocks, part, LANES)

    loop(tiles, grad_in_rim)
    relays(put_b1, stop=1)
    exchanges([put_b1])
    def down_project(j):
        out = nt(r.mix[...], r.dfull[span(j, TILE), :]).astype(B16)
        r.src_b[:, :, span(j, TILE)] = out.reshape(streams, rows, TILE)

    loop(tiles, down_project)
    exchanges([down])
    steps([put_b2], True, skip=1, stop=2)
    back.last()
    back2.start()
    relays(put_b1, skip=1, stop=2)
    steps([put_b2], True, skip=2)
    steps([put_b1], True, stop=1)
    steps([down], True)
    steps([back2], False)
    back2.finish()
    back.finish()

    def middle_grad(i):
        s, h = i // per, i % per
        at = span(h, CHUNK)
        here = span(i, CHUNK)
        got = norm_backward(
            r.back_all[s, at, :].astype(F32),
            r.scaled[here, :],
            r.inverse[here, 0:1],
            r.gain[1:2, :],
        )
        grad = r.grd_all[s, at, :].astype(F32) + got
        r.nx[s, at, :] = grad.astype(B16)

        @pl.when(s == fsdp.me)
        def _():
            r.own_grad[at, :] = grad

    relays(put_b1, skip=2, stop=3)
    loop(streams * per, middle_grad, UNROLL)

    def turn_middle(i):
        x = r.nx[:, :rows, span(i, LANES)].reshape(group, LANES)
        r.tt[span(i, LANES), :] = x.T

    loop(width // LANES, turn_middle)

    def grad_attended(s):
        w = r.a_all[:, :, three:].reshape(width, quarter)
        r.gatt[span(s, TILE), :] = nn(
            r.nx[span(s, half_streams), :rows, :].reshape(TILE, width), w
        ).astype(B16)

    loop(sides, grad_attended)
    steps([put_b1], True, skip=1, stop=2)

    def edges(s):
        at = span(s, rows)
        lane = lax.broadcasted_iota(jnp.int32, (rows, LANES), 1)
        total = jnp.zeros((rows, LANES), F32)
        for p in range(pairs):
            product = r.gatt[at, lanes(p)].astype(F32) * r.att[at, lanes(p)].astype(F32)
            for h in range(2):
                k = 2 * p + h
                total = jnp.where(lane == k, r.lse[s, k], total)
                total = jnp.where(lane == 2 * pairs + k, delta_of(product, h), total)
        total = total.T
        head_at = pl.ds(pl.multiple_of(s * rows, reach), reach)
        tail_at = pl.ds(pl.multiple_of(s * rows + rows - reach, reach), reach)
        r.edge_src[0, span(s, reach), :] = r.gatt[tail_at, :]
        r.edge_src[1, span(s, reach), :] = r.gatt[head_at, :]
        for way in range(2):
            r.stat_src[way, s] = total[: 4 * pairs]

    loop(streams, edges)
    stat.start()
    edge.start()

    def attend_back(s):
        allowed = visible(s)
        at = span(s, rows)
        for p in range(pairs):
            scores = nt(r.qs[s, p], r.k2[s, p]) * scale
            grad = r.gatt[at, lanes(p)]
            grad_probs = nt(grad, r.v2[s, p])
            grad_f = grad.astype(F32)
            product = grad_f * r.att[at, lanes(p)].astype(F32)
            agains, grads = [], []
            for h in range(2):
                cut = slice(h * outer, (h + 1) * outer)
                masked = jnp.where(allowed, scores[:, cut], -1e30)
                again = jnp.exp(masked - r.lse[s, 2 * p + h][:, 0:1])
                delta = delta_of(product, h)
                agains.append(again.astype(B16))
                grads.append((again * (grad_probs[:, cut] - delta) * scale).astype(B16))
            grad_query = nn(jnp.concatenate(grads, axis=1), r.k2[s, p])
            grad_keys = nn(jnp.concatenate(grads, axis=0).T, r.q2[s, p])
            grad_values = nn(jnp.concatenate(agains, axis=0).T, halves(grad_f).astype(B16))
            r.gp[at, lanes(p)] = unrotate(
                grad_query, r.cosine[reach : reach + rows], r.sine[reach : reach + rows]
            ).astype(B16)
            for k, value in ((p, grad_keys), (pairs + p, grad_values)):
                r.own_kv[s, :, lanes(k)] = value[reach : reach + rows]

    loop(streams, attend_back)
    relays(put_b1, skip=3)
    down.last()

    def grad_out(m):
        out = nn(r.tt[span(m, TILE), :], r.att[...]).astype(B16)
        r.ga[span(m, blocks), :, quarter:] = out.reshape(blocks, part, quarter)

    loop(tiles, grad_out)

    def grad_query(m):
        out = nn(r.n1t[span(m, TILE), :], r.gp[:, :quarter]).astype(B16)
        r.ga[span(m, blocks), :, :quarter] = out.reshape(blocks, part, quarter)

    loop(tiles, grad_query)
    exchanges([put_a])

    def norm_again(i):
        s, h = i // per, i % per
        x = r.tok_all[s, span(h, CHUNK), :].astype(F32)
        scaled, inverse, _ = norm_forward(x, r.gain[0:1, :])
        r.scaled[span(i, CHUNK), :] = scaled
        r.inverse[span(i, CHUNK), :] = jnp.broadcast_to(inverse, (CHUNK, LANES))

    loop(streams * per, norm_again, UNROLL)
    down.finish()
    steps([put_b1], True, skip=2)
    edge.arrive()
    stat.arrive()

    def join(s):
        allowed = visible_rims(s)
        empty = jnp.zeros((LANES - 4 * pairs, rows), F32)
        before = jnp.concatenate([r.stat_mid[0, s], empty], axis=0).T[rows - reach :]
        after = jnp.concatenate([r.stat_mid[1, s], empty], axis=0).T[:reach]
        stats = jnp.concatenate([before, after], axis=0)
        for p in range(pairs):
            keys, vals = [
                jnp.concatenate(
                    [ref[s, p, h * outer + reach : h * outer + reach + rows] for h in range(2)],
                    axis=0,
                )
                for ref in (r.k2, r.v2)
            ]
            grad = jnp.concatenate(
                [r.edge_mid[way, span(s, reach), lanes(p)] for way in range(2)], axis=0
            )
            scores = nt(r.hq[s, p], keys) * scale
            grad_probs = nt(grad, vals)
            agains, grads = [], []
            for h in range(2):
                k = 2 * p + h
                cut = slice(h * rows, (h + 1) * rows)
                masked = jnp.where(allowed, scores[:, cut], -1e30)
                again = jnp.exp(masked - stats[:, k : k + 1])
                delta = stats[:, 2 * pairs + k : 2 * pairs + k + 1]
                agains.append(again.astype(B16))
                grads.append((again * (grad_probs[:, cut] - delta) * scale).astype(B16))
            grad_keys = nn(jnp.concatenate(grads, axis=0).T, r.hq2[s, p])
            grad_values = nn(
                jnp.concatenate(agains, axis=0).T, halves(grad.astype(F32)).astype(B16)
            )
            grad_keys = unrotate(
                grad_keys + r.own_kv[s, :, lanes(p)],
                r.cosine[reach : reach + rows],
                r.sine[reach : reach + rows],
            )
            grad_values = grad_values + r.own_kv[s, :, lanes(pairs + p)]
            r.gp[span(s, rows), lanes(pairs + p)] = grad_keys.astype(B16)
            r.gp[span(s, rows), lanes(2 * pairs + p)] = grad_values.astype(B16)

    loop(streams, join)

    def grad_pair(i):
        m, j = i // 2, i % 2
        at = pl.ds(pl.multiple_of((j + 1) * quarter, quarter), quarter)
        out = nn(r.n1t[span(m, TILE), :], r.gp[:, at]).astype(B16)
        r.gc[span(m, blocks), :, span(j, quarter)] = out.reshape(blocks, part, quarter)

    loop(tiles * 2, grad_pair)
    steps([put_a], True, stop=1)

    def one_project(j):
        w = r.a_all[span(j, blocks), :, :three].reshape(TILE, three)
        out = nt(r.gp[...], w)
        at = span(j, TILE)
        r.gain_row[0:1, at] = jnp.sum(out * r.scaled[:, at], axis=0, keepdims=True)
        r.src_b[:, :, at] = out.astype(B16).reshape(streams, rows, TILE)

    loop(tiles, one_project)
    for s in range(seq.n):
        k = s * part // LANES
        r.gain_parts[s] = r.gain_row[:, k * LANES : (k + 1) * LANES]
    exchanges([one])
    exchanges([put_g])
    exchanges([put_c])
    put_b2.last()
    put_b1.last()
    steps([one], True)
    steps([put_a], True, skip=1, stop=2)
    steps([put_g], True, stop=1)
    for j in range(main):
        cut = slice(j * LANES, (j + 1) * LANES)
        for k in range(2):
            at = (2 * j + k) * LANES
            r.din[k, cut, :] = db1[:, at : at + LANES].T
        r.ddown_t[cut, :] = db2[:, cut].T
    rim_sum = db1[:, rim_at:].T
    r.din[0, flat:, :] = rim_sum[:tail]
    r.din[1, flat:, :] = rim_sum[tail : 2 * tail]
    r.ddown_t[flat:, :] = rim_sum[2 * tail : 3 * tail]
    steps([put_c], True, stop=1)
    steps([put_a], True, skip=2)
    steps([put_g], True, skip=1, stop=2)
    one.last()

    def final(h):
        at = span(h, CHUNK)
        here = pl.ds(pl.multiple_of(fsdp.me * rows + h * CHUNK, CHUNK), CHUNK)
        got = norm_backward(
            r.one_sum[at, :], r.scaled[here, :], r.inverse[here, 0:1], r.gain[0:1, :]
        )
        r.dinput[at, :] = r.own_grad[at, :] + got
        middle = r.tok[at, :].astype(F32) + r.attn_all[fsdp.me, at, :].astype(F32)
        r.out[at, :] = (middle + r.down_sum[at, :]).astype(B16)

    loop(per, final)
    steps([put_c], True, skip=1, stop=2)
    steps([put_g], True, skip=2)
    put_a.last()
    put_g.last()
    put_g2.start()
    r.dqkv[0] = da[:, :quarter]
    for k in range(pairs):
        at = quarter + k * LANES
        r.dout[k * LANES : (k + 1) * LANES, :] = da[:, at : at + LANES].T
    steps([put_c], True, skip=2)
    steps([put_g2], False)
    put_g2.finish()
    total = r.gain_got[0]
    for f in range(1, fsdp.n):
        total = total + r.gain_got[f]
    total = pltpu.roll(total, (LANES - shift) % LANES, 1)
    r.dgain_one[...] = total[0:1, :piece]
    r.dgain_two[...] = total[1:2, :piece]
    put_c.last()
    r.dqkv[1] = dc[:, :quarter]
    r.dqkv[2] = dc[:, quarter:]
    for job in (edge, stat, one, put_b1, put_b2, put_a, put_c, put_g):
        job.finish()


def run_layer(tok, grd, gain_one, gain_two, qkv, out_w, in_two, down_t, freq, lengths):
    n, nf = lax.axis_size("seq"), lax.axis_size("fsdp")
    rows, width = tok.shape
    count, part = down_t.shape
    quarter, piece = out_w.shape[0], gain_one.shape[1]
    gain_block = (16, LANES)
    wide_a, wide_2 = 4 * quarter, count // LANES * LANES
    wide_1 = 2 * wide_2 + LANES
    block_c = (part, 2 * quarter)
    block_a, block_1, block_2 = (part, wide_a), (part, wide_1), (part, wide_2)
    pairs = quarter // LANES
    streams = nf
    group = streams * rows
    outer = rows + 2 * WIN
    vmem = pl.BlockSpec(memory_space=pltpu.VMEM)
    ins = [
        ("tok", tok, vmem),
        ("grd", grd, vmem),
        ("gain_one", gain_one, vmem),
        ("gain_two", gain_two, vmem),
        ("qkv", qkv, vmem),
        ("out_w", out_w, vmem),
        ("in_two", in_two, vmem),
        ("down_t", down_t, vmem),
        ("freq", freq, vmem),
        ("lengths", lengths, pl.BlockSpec(memory_space=pltpu.SMEM)),
    ]
    outs = [
        ("out", (rows, width), B16),
        ("dinput", (rows, width), F32),
        ("dgain_one", (1, piece), F32),
        ("dgain_two", (1, piece), F32),
        ("dqkv", (3, part, quarter), F32),
        ("dout", (quarter, part), F32),
        ("din", (2, count, part), F32),
        ("ddown_t", (count, part), F32),
    ]
    plan = Plan()
    token_block = (rows, width)
    for name, count_, shape, dtype in (
        ("tok", nf, token_block, B16),
        ("grd", nf, token_block, B16),
        ("rim", nf, (2, WIN, width), B16),
        ("a", n, block_a, B16),
        ("b1", n, block_1, B16),
        ("b2", n, block_2, B16),
        ("attn", nf, token_block, B16),
        ("back", nf, token_block, B16),
    ):
        plan.vmem(name + "_all", (count_,) + shape, dtype)
        plan.add(name + "_g", *Gather.scratch(count_))
    for name, count_, shape, dtype in (
        ("attn", nf, token_block, B16),
        ("back", nf, token_block, B16),
        ("down", nf, token_block, B16),
        ("one", nf, token_block, B16),
        ("b1", n, block_1, B16),
        ("b2", n, block_2, B16),
        ("a", n, block_c, B16),
        ("c", n, block_c, B16),
        ("gain", n, (8, LANES), F32),
    ):
        plan.add(name + "_r", *Reduce.scratch(count_, shape, dtype))
    plan.add("b1_relay", *Reduce.relay_scratch(block_1, B16))
    plan.vmem("rim_mid", (2, WIN, width), B16)
    plan.add("halo_s", *Halo.scratch())
    plan.vmem("gains", gain_block, B16)
    plan.vmem("gains_mid", (n,) + gain_block, B16)
    plan.add("gains_g", *Gather.scratch(n))
    plan.vmem("gains_all", (nf, n) + gain_block, B16)
    plan.add("gains2_g", *Gather.scratch(nf))
    plan.vmem("gain_mid", (8, LANES), F32)
    plan.vmem("gain_got", (nf, 8, LANES), F32)
    plan.vmem("cosine", (outer, LANES), F32)
    plan.vmem("sine", (outer, LANES), F32)
    plan.add("gain_g", *Gather.scratch(nf))
    plan.add("edge_s", *Halo.scratch())
    plan.add("stat_s", *Halo.scratch())
    for name, shape, dtype in (
        ("edge_src", (2, streams * WIN, quarter), B16),
        ("edge_mid", (2, streams * WIN, quarter), B16),
        ("stat_src", (2, streams, 4 * pairs, LANES), F32),
        ("stat_mid", (2, streams, 4 * pairs, LANES), F32),
        ("hq", (streams, pairs, 2 * WIN, LANES), B16),
        ("hq2", (streams, pairs, 4 * WIN, LANES), B16),
        ("gain", (gain_block[0], width), F32),
        ("gain_row", (8, width), F32),
        ("gain_parts", (n, 8, LANES), F32),
        ("nx", (streams, outer, width), B16),
        ("n1t", (width, group), B16),
        ("gt", (width, group), B16),
        ("tt", (width, group), B16),
        ("qs", (streams, pairs, rows, LANES), B16),
        ("q2", (streams, pairs, 2 * rows, LANES), B16),
        ("k2", (streams, pairs, 2 * outer, LANES), B16),
        ("v2", (streams, pairs, 2 * outer, LANES), B16),
        ("lse", (streams, 2 * pairs, rows, LANES), F32),
        ("att", (group, quarter), B16),
        ("src_a", (streams,) + token_block, B16),
        ("src_b", (streams,) + token_block, B16),
        ("attn_mid", token_block, B16),
        ("back_mid", token_block, B16),
        ("down_sum", token_block, F32),
        ("one_sum", token_block, F32),
        ("scaled", (group, width), F32),
        ("inverse", (group, LANES), F32),
        ("big", (group, 2 * (wide_2 + LANES)), F32),
        ("mix", (group, wide_2 + LANES), B16),
        ("mix_rim", (group, LANES), B16),
        ("dfull", (width, wide_2 + LANES), B16),
        ("gh", (group, wide_1), B16),
        ("gb1", (n,) + block_1, B16),
        ("gb2", (n,) + block_2, B16),
        ("ga", (n,) + block_c, B16),
        ("gc", (n,) + block_c, B16),
        ("own_grad", token_block, F32),
        ("own_kv", (streams, rows, 2 * quarter), F32),
        ("gatt", (group, quarter), B16),
        ("gp", (group, 3 * quarter), B16),
    ):
        plan.vmem(name, shape, dtype)
    names = [i[0] for i in ins] + [o[0] for o in outs] + plan.names
    return pl.pallas_call(
        functools.partial(layer_kernel, tuple(names)),
        out_shape=[jax.ShapeDtypeStruct(s, d) for _, s, d in outs],
        in_specs=[i[2] for i in ins],
        out_specs=[vmem] * len(outs),
        scratch_shapes=plan.shapes,
        compiler_params=pltpu.CompilerParams(
            collective_id=1, has_side_effects=True, vmem_limit_bytes=63 * 1024 * 1024
        ),
    )(*[i[1] for i in ins])


def settle_kernel(*refs):
    count = len(refs) // 2
    copies = [
        pltpu.make_async_copy(*refs[k : 2 * count : count], refs[2 * count].at[k])
        for k in range(count)
    ]
    for copy in copies:
        copy.start()
    for copy in copies:
        copy.wait()


def settle(arrays):
    anywhere = pl.BlockSpec(memory_space=pl.ANY)
    return pl.pallas_call(
        settle_kernel,
        out_shape=[jax.ShapeDtypeStruct(x.shape, x.dtype) for x in arrays],
        in_specs=[anywhere] * len(arrays),
        out_specs=[pl.BlockSpec(memory_space=pltpu.VMEM)] * len(arrays),
        scratch_shapes=[pltpu.SemaphoreType.DMA((len(arrays),))],
    )(*arrays)


def per_device(
    layer_input,
    doc_lengths,
    attn_gain,
    qkv_weight,
    out_weight,
    mlp_gain,
    in_weight,
    down_weight,
    out_grad,
):
    half = np.arange(LANES)[None, :] % (HEAD // 2)
    freq = 10000.0 ** (-(2.0 / HEAD) * half)
    made = run_layer(
        layer_input[0],
        out_grad[0],
        attn_gain[None],
        mlp_gain[None],
        qkv_weight.transpose(1, 0, 2),
        out_weight,
        in_weight.transpose(1, 2, 0),
        down_weight.T,
        jnp.asarray(freq, F32),
        doc_lengths,
    )
    output, input_grad, dgain_one, dgain_two, dqkv, dout, din, ddown_t = settle(made)
    return (
        output[None],
        input_grad[None],
        dgain_one[0],
        dqkv.transpose(1, 0, 2),
        dout,
        dgain_two[0],
        din.transpose(2, 0, 1),
        ddown_t.T,
    )


def solution(mesh):
    in_specs = (
        P("fsdp", "seq", None),
        P(),
        P(("seq", "fsdp")),
        P("seq", None, "fsdp"),
        P("fsdp", "seq"),
        P(("seq", "fsdp")),
        P("seq", None, "fsdp"),
        P("seq", "fsdp"),
        P("fsdp", "seq", None),
    )
    out_specs = (
        P("fsdp", "seq", None),
        P("fsdp", "seq", None),
        P(("seq", "fsdp")),
        P("seq", None, "fsdp"),
        P("fsdp", "seq"),
        P(("seq", "fsdp")),
        P("seq", None, "fsdp"),
        P("seq", "fsdp"),
    )
    return jax.shard_map(
        per_device, mesh=mesh, in_specs=in_specs, out_specs=out_specs, check_vma=False
    )
```
